32 devices in a mesh: seq: 2 (over core), pipe: 4 (over y, x), tp: 4 (over z).
Axes of the slice: x: 2, y: 2, z: 4, core: 2. Of those that a mesh axis runs over, the one named last changes fastest.
Arguments:
- queries: bfloat16 [4, 1024, 3072], P('pipe', 'seq', 'tp'), may hold values from -6 to 6
- keys: bfloat16 [4, 1024, 3072], P('pipe', 'seq', 'tp'), may hold values from -6 to 6
- values: bfloat16 [4, 1024, 3072], P('pipe', 'seq', 'tp'), may hold values from -6 to 6
- grad_out: bfloat16 [4, 1024, 3072], P('pipe', 'seq', 'tp'), may hold values from -6 to 6
- router: float32 [4, 1024], P('pipe', 'seq'), may hold values from 0.1 to 1
- blocks: int32 [4, 2, 3], P('pipe', 'seq'), may hold values from 0 to 3, as said below
- counts: int32 [4, 2], P('pipe', 'seq'), may hold values from 1 to 3, as said below
Outputs:
- section_grads: bfloat16 [4, 3, 768, 3072], P('pipe', None, 'seq', 'tp')
- router_grad: float32 [4, 768], P('pipe', 'seq')
The draws below stay inside these ranges and needn't reach their ends.
Inputs may be any that keep to these rules, and one draw needn't show every extreme that they name: Per section and shard, the first counts entries are distinct block numbers in increasing order; the remaining entries are 0. In every draw some shard routes its last 3 blocks. `counts`: in every draw some shard routes 3 blocks and some routes 1.
All inputs are finite; a program needn't handle non-finite values.
Results may differ from the reference program's by a relative error of at most 0.0058.
Values may be sent and summed in bfloat16 or wider, within the bound.
No kernel may reach another device: no remote copies, remote signals or barrier semaphores. Data moves between devices by JAX's collectives and lax.ppermute only.
A program may use at most 128 MiB of HBM per device.

```python
import math
import jax
import jax.numpy as jnp
from jax import lax

LOCAL_HEADS = 24
HEAD_SIZE = 128
BLOCK_ROWS = 128
BLOCKS_DEV = 4
ROUTED_MAXIMUM = 3
TOKENS = 1024
N_SEQ = 2
N_PIPE = 4


def selection(key):
    shards = N_PIPE * N_SEQ
    count_key = jax.random.fold_in(key, 11)
    block_key = jax.random.fold_in(key, 23)
    full_key = jax.random.fold_in(key, 37)
    single_key = jax.random.fold_in(key, 41)
    shard_index = jnp.arange(shards, dtype=jnp.int32).reshape(N_PIPE, N_SEQ)
    full_shard = jax.random.randint(full_key, (), 0, shards)
    single_shard = (full_shard + 1 + jax.random.randint(single_key, (), 0, shards - 1)) % shards
    picked = jax.random.randint(count_key, (N_PIPE, N_SEQ), 1, ROUTED_MAXIMUM + 1)
    picked = jnp.where(shard_index == full_shard, ROUTED_MAXIMUM, picked)
    picked = jnp.where(shard_index == single_shard, 1, picked)
    shard_keys = jax.random.split(block_key, shards)
    shuffles = jax.vmap(lambda one_key: jax.random.permutation(one_key, BLOCKS_DEV))(shard_keys)
    chosen = jnp.sort(shuffles[:, :ROUTED_MAXIMUM], axis=1).reshape(N_PIPE, N_SEQ, ROUTED_MAXIMUM)
    last_blocks = jnp.arange(BLOCKS_DEV - ROUTED_MAXIMUM, BLOCKS_DEV, dtype=jnp.int32)
    chosen = jnp.where((shard_index == full_shard)[:, :, None], last_blocks[None, None, :], chosen)
    slot_number = jnp.arange(ROUTED_MAXIMUM, dtype=jnp.int32)
    chosen = jnp.where(slot_number[None, None, :] < picked[:, :, None], chosen, 0)
    return (chosen.astype(jnp.int32), picked.astype(jnp.int32))


def draw_blocks(key, part):
    return selection(key)[0]


def draw_counts(key, part):
    return selection(key)[1]


def levels(own_key, extent, pieces, low, largest):
    level, own = 1.0, jax.random.fold_in(own_key, 6)
    for dim, blocks in pieces:
        draws = jnp.exp(jax.random.uniform(jax.random.fold_in(own, dim), (blocks,), jnp.float32, low / len(pieces), largest / len(pieces)))
        level = level * jnp.repeat(draws, extent[dim] // blocks).reshape([-1 if axis == dim else 1 for axis in range(len(extent))])
    return level


def noise(own_key, dims, scale, bound, cuts=(), kind=jnp.bfloat16):
    entries = jax.random.normal(own_key, dims, jnp.float32) * scale
    if len(cuts) > 0:
        entries = levels(own_key, dims, cuts, -0.22, 0.18) * entries
    return jnp.clip(entries, min=-bound, max=bound).astype(kind)


def setup_inputs(seed: int = 0) -> dict:
    seeds = jax.random.split(jax.random.key(seed), 8)
    queries = noise(seeds[0], (N_PIPE, TOKENS, LOCAL_HEADS * HEAD_SIZE), 1.0, 6.0, ((0, 4), (1, 2), (2, 4)))
    keys = noise(seeds[1], (N_PIPE, TOKENS, LOCAL_HEADS * HEAD_SIZE), 1.0, 6.0, ((0, 4), (1, 2), (2, 4)))
    values = noise(seeds[2], (N_PIPE, TOKENS, LOCAL_HEADS * HEAD_SIZE), 1.0, 6.0, ((0, 4), (1, 2), (2, 4)))
    grad_out = noise(seeds[3], (N_PIPE, TOKENS, LOCAL_HEADS * HEAD_SIZE), 1.0, 6.0, ((0, 4), (1, 2), (2, 4)))
    router = jnp.clip(0.1 + 0.9 * jax.random.uniform(seeds[4], (N_PIPE, TOKENS), jnp.float32) ** levels(seeds[4], (N_PIPE, TOKENS), ((0, 4), (1, 2)), -0.2, 0.2), 0.1, 1.0)
    blocks = draw_blocks(jax.random.fold_in(seeds[7], 71), 0)
    counts = draw_counts(jax.random.fold_in(seeds[7], 71), 0)
    return dict(queries=queries, keys=keys, values=values, grad_out=grad_out, router=router, blocks=blocks, counts=counts)


def widen_rows(array):
    return array.astype(jnp.float32)

def section(inputs):
    qsec, ksec, vsec, gsec, rsec, blocksec, countsec = inputs
    slot_total = N_SEQ * ROUTED_MAXIMUM
    factor = 1.0 / math.sqrt(HEAD_SIZE * ROUTED_MAXIMUM * BLOCK_ROWS * N_SEQ)
    starts = (jnp.arange(N_SEQ, dtype=jnp.int32)[:, None] * BLOCKS_DEV + blocksec.astype(jnp.int32)) * BLOCK_ROWS
    row_index = (starts[:, :, None] + jnp.arange(BLOCK_ROWS, dtype=jnp.int32)[None, None, :]).reshape(-1).astype(jnp.int32)
    valid_slot = jnp.arange(ROUTED_MAXIMUM, dtype=jnp.int32)[None, :] < countsec[:, None]
    live_rows = jnp.broadcast_to(valid_slot[:, :, None], (N_SEQ, ROUTED_MAXIMUM, BLOCK_ROWS)).reshape(-1)

    def select(array):
        taken_blocks = jnp.where(live_rows[:, None], array[row_index], jnp.zeros((), array.dtype))
        return taken_blocks.reshape(slot_total, BLOCK_ROWS, LOCAL_HEADS, HEAD_SIZE)
    queries = select(qsec)
    keys = select(ksec)
    values = select(vsec)
    gradient_list = select(gsec)
    router_weight = jnp.where(live_rows, rsec[row_index], jnp.zeros((), rsec.dtype))
    output_gradient = (widen_rows(router_weight).reshape(slot_total, BLOCK_ROWS, 1, 1) * widen_rows(gradient_list)).astype(jnp.bfloat16)
    key_value = jnp.einsum('nthd,nthe->nhde', widen_rows(keys), widen_rows(values))
    query_grad = jnp.einsum('nthd,nthe->nhde', widen_rows(queries), widen_rows(output_gradient))
    zero_state = jnp.zeros((1,) + key_value.shape[1:], jnp.float32)
    before = jnp.concatenate([zero_state, jnp.cumsum(key_value, axis=0)[:-1]], axis=0).astype(jnp.bfloat16)
    flipped = jnp.flip(query_grad, axis=0)
    after = jnp.flip(jnp.concatenate([zero_state, jnp.cumsum(flipped, axis=0)[:-1]], axis=0), axis=0).astype(jnp.bfloat16)
    causal = jnp.arange(BLOCK_ROWS)[:, None] >= jnp.arange(BLOCK_ROWS)[None, :]
    grad_scores = jnp.where(causal, jnp.einsum('nthe,nshe->nhts', widen_rows(output_gradient), widen_rows(values)), 0.0).astype(jnp.bfloat16)
    scores = jnp.where(causal, jnp.einsum('nthd,nshd->nhts', widen_rows(queries), widen_rows(keys)), 0.0).astype(jnp.bfloat16)
    output_core = factor * (jnp.einsum('nhts,nshe->nthe', widen_rows(scores), widen_rows(values)) + jnp.einsum('nthd,nhde->nthe', widen_rows(queries), widen_rows(before)))
    router_grad = lax.optimization_barrier(jnp.sum(widen_rows(gradient_list) * output_core, axis=(2, 3))).reshape(-1)
    query_gradient = factor * (jnp.einsum('nhts,nshd->nthd', widen_rows(grad_scores), widen_rows(keys)) + jnp.einsum('nthe,nhde->nthd', widen_rows(output_gradient), widen_rows(before)))
    key_gradient = factor * (jnp.einsum('nhts,nthd->nshd', widen_rows(grad_scores), widen_rows(queries)) + jnp.einsum('nshe,nhde->nshd', widen_rows(values), widen_rows(after)))
    value_gradient = factor * (jnp.einsum('nhts,nthe->nshe', widen_rows(scores), widen_rows(output_gradient)) + jnp.einsum('nshd,nhde->nshe', widen_rows(keys), widen_rows(after)))
    stacked_gradients = jnp.stack([query_gradient, key_gradient, value_gradient]).reshape(3, slot_total * BLOCK_ROWS, LOCAL_HEADS * HEAD_SIZE).astype(jnp.bfloat16)
    return (stacked_gradients, router_grad)

def reference(queries, keys, values, grad_out, router, blocks, counts):
    stacked_gradients, router_grad = lax.map(section, (queries, keys, values, grad_out, router, blocks, counts))
    section_grads = jnp.roll(stacked_gradients, -1, axis=0)
    return (section_grads, router_grad)
```

```python
import functools
import math

import jax
import jax.numpy as jnp
from jax import lax
from jax.experimental import pallas as pl
from jax.experimental.pallas import tpu as pltpu
from jax.sharding import PartitionSpec as P

HEAD_SIZE = 128
BLOCK_ROWS = 128


ANY = pl.BlockSpec(memory_space=pl.ANY)
SMEM = pl.BlockSpec(memory_space=pltpu.SMEM)
VMEM = pl.BlockSpec(memory_space=pltpu.VMEM)


def from_behind(x, axis, by):
    count = lax.axis_size(axis)
    return lax.ppermute(x, axis, [(i, (i + by) % count) for i in range(count)])


def dot(a, b):
    return jnp.dot(a, b, preferred_element_type=jnp.float32)


def dot_nt(a, b):
    return lax.dot_general(a, b, (((1,), (1,)), ((), ())), preferred_element_type=jnp.float32)


def dot_tn(a, b):
    return lax.dot_general(a, b, (((0,), (0,)), ((), ())), preferred_element_type=jnp.float32)


def head(h):
    return slice(h * HEAD_SIZE, (h + 1) * HEAD_SIZE)


def block_rows(blocks, n):
    return pl.ds(pl.multiple_of(blocks[0, 0, n] * BLOCK_ROWS, BLOCK_ROWS), BLOCK_ROWS)


def down_rows(router, rows):
    weight = router[0:1, rows]
    return jnp.broadcast_to(weight, (BLOCK_ROWS, BLOCK_ROWS)).T


def row_minus_column():
    shape = (BLOCK_ROWS, BLOCK_ROWS)
    return lax.broadcasted_iota(jnp.int32, shape, 0) - lax.broadcasted_iota(jnp.int32, shape, 1)


def early_kernel(
    factor, blocks, counts, router, q, k, v, g, state, chunk,
    x_buf, vc_buf, g_buf, acc, out_buf, in_sem, out_sem, state_sem,
):
    slots, _, width = out_buf.shape
    heads = width // HEAD_SIZE
    first = lax.axis_index("seq") == 0
    count = counts[0, 0]
    left = jnp.where(first, 1, 0)
    right = 1 - left
    sign = jnp.where(first, 1, -1)
    allowed = row_minus_column() * sign >= 0

    def slot(i):
        return jnp.where(first, i, count - 1 - i)

    def copies(i):
        rows = block_rows(blocks, slot(i))
        return (
            pltpu.make_async_copy(g.at[0, rows], g_buf.at[i], in_sem.at[0, i]),
            pltpu.make_async_copy(v.at[0, rows], vc_buf.at[0, i], in_sem.at[1, i]),
            pltpu.make_async_copy(k.at[0, rows], x_buf.at[i], in_sem.at[2, i]),
            pltpu.make_async_copy(q.at[0, rows], x_buf.at[i], in_sem.at[2, i]),
        )

    def put(i, n):
        rows = pl.ds(pl.multiple_of(n * BLOCK_ROWS, BLOCK_ROWS), BLOCK_ROWS)
        return pltpu.make_async_copy(out_buf.at[i], chunk.at[rows], out_sem.at[i])

    for i in range(slots):
        @pl.when(i < count)
        def _():
            g_copy, v_copy, k_copy, q_copy = copies(i)
            g_copy.start()
            v_copy.start()

            @pl.when(first)
            def _():
                k_copy.start()

            @pl.when(jnp.logical_not(first))
            def _():
                q_copy.start()

    for i in range(slots):
        @pl.when(i < count)
        def _():
            g_copy, v_copy, k_copy, _ = copies(i)
            weight = down_rows(router, block_rows(blocks, slot(i)))
            g_copy.wait()
            for h in range(heads):
                vc_buf[1, i, :, head(h)] = (
                    weight * g_buf[i, :, head(h)].astype(jnp.float32)
                ).astype(jnp.bfloat16)
            v_copy.wait()
            k_copy.wait()
            for h in range(heads):
                l_h = vc_buf[left, i, :, head(h)]
                r_h = vc_buf[right, i, :, head(h)]
                x_h = x_buf[i, :, head(h)]
                scores = jnp.where(allowed, dot_nt(l_h, r_h), 0.0).astype(jnp.bfloat16)
                if i == 0:
                    out = dot(scores, x_h)
                    acc[h] = dot_tn(r_h, x_h)
                else:
                    so_far = acc[h]
                    out = dot(
                        jnp.concatenate([scores, l_h], axis=1),
                        jnp.concatenate([x_h, so_far.astype(jnp.bfloat16)], axis=0),
                    )
                    acc[h] = so_far + dot_tn(r_h, x_h)
                out_buf[i, :, head(h)] = (factor * out).astype(jnp.bfloat16)
            put(i, slot(i)).start()

        @pl.when(i >= count)
        def _():
            out_buf[i] = jnp.zeros(out_buf.shape[1:], out_buf.dtype)
            put(i, i).start()

    state_copy = pltpu.make_async_copy(acc, state, state_sem)
    state_copy.start()
    for i in range(slots):
        put(i, i).wait()
    state_copy.wait()


def early(factor, router, blocks, counts, q, k, v, g):
    slots = blocks.shape[2]
    width = q.shape[2]
    heads = width // HEAD_SIZE
    tile = (slots, BLOCK_ROWS, width)
    return pl.pallas_call(
        functools.partial(early_kernel, factor),
        name="early",
        out_shape=(
            jax.ShapeDtypeStruct((heads, HEAD_SIZE, HEAD_SIZE), jnp.float32),
            jax.ShapeDtypeStruct((slots * BLOCK_ROWS, width), jnp.bfloat16),
        ),
        in_specs=[SMEM, SMEM, VMEM, ANY, ANY, ANY, ANY],
        out_specs=(ANY, ANY),
        scratch_shapes=[
            pltpu.VMEM(tile, jnp.bfloat16),
            pltpu.VMEM((2,) + tile, jnp.bfloat16),
            pltpu.VMEM(tile, jnp.bfloat16),
            pltpu.VMEM((heads, HEAD_SIZE, HEAD_SIZE), jnp.float32),
            pltpu.VMEM(tile, jnp.bfloat16),
            pltpu.SemaphoreType.DMA((3, slots)),
            pltpu.SemaphoreType.DMA((slots,)),
            pltpu.SemaphoreType.DMA,
        ],
        cost_estimate=pl.CostEstimate(
            flops=2 * 5 * slots * heads * HEAD_SIZE**3,
            bytes_accessed=2 * 4 * slots * BLOCK_ROWS * width,
            transcendentals=0,
        ),
    )(blocks, counts, router, q, k, v, g)


def late_kernel(
    factor, split, blocks, counts, router, earlier, later, q, k, v, g, *refs,
):
    outs, (partial, q_buf, k_buf, v_buf, g_buf, c_buf, acc, in_sem) = refs[:-8], refs[-8:]
    slots, _, width = q_buf.shape
    heads = width // HEAD_SIZE
    first = lax.axis_index("seq") == 0
    last = lax.axis_index("seq") == lax.axis_size("seq") - 1
    count = counts[0, 0]
    below = row_minus_column() >= 0
    above = row_minus_column() <= 0
    d_query, d_key, d_value = (outs[0], outs[0], outs[1]) if split else outs

    def copies(n):
        rows = block_rows(blocks, n)
        return [
            pltpu.make_async_copy(source.at[0, rows], buf.at[n], in_sem.at[j, n])
            for j, (source, buf) in enumerate(((g, g_buf), (q, q_buf), (k, k_buf), (v, v_buf)))
        ]

    for n in range(slots):
        @pl.when(n < count)
        def _():
            for copy in copies(n):
                copy.start()

    partial[...] = jnp.zeros(partial.shape, partial.dtype)

    @pl.when(first)
    def _():
        acc[...] = jnp.zeros(acc.shape, acc.dtype)

    @pl.when(jnp.logical_not(first))
    def _():
        acc[...] = earlier[...]

    for n in range(slots):
        rows = slice(n * BLOCK_ROWS, (n + 1) * BLOCK_ROWS)

        @pl.when(n < count)
        def _():
            for copy in copies(n):
                copy.wait()
            weight = down_rows(router, block_rows(blocks, n))
            by_row = jnp.zeros((BLOCK_ROWS, HEAD_SIZE), jnp.float32)
            for h in range(heads):
                grad = g_buf[n, :, head(h)].astype(jnp.float32)
                c_h = (weight * grad).astype(jnp.bfloat16)
                c_buf[n, :, head(h)] = c_h
                q_h, k_h, v_h = (buf[n, :, head(h)] for buf in (q_buf, k_buf, v_buf))
                so_far = acc[h]
                state = so_far.astype(jnp.bfloat16)
                scores = jnp.where(below, dot_nt(q_h, k_h), 0.0).astype(jnp.bfloat16)
                core = factor * (dot(scores, v_h) + dot_nt(q_h, state))
                by_row = by_row + grad * core

                def query_part():
                    grads = jnp.where(below, dot_nt(c_h, v_h), 0.0).astype(jnp.bfloat16)
                    d_query[rows, head(h)] = (
                        factor * (dot(grads, k_h) + dot(c_h, state))
                    ).astype(jnp.bfloat16)

                if split:
                    pl.when(last)(query_part)
                else:
                    query_part()
                acc[h] = so_far + dot_tn(v_h, k_h)
            partial[0:1, rows] = jnp.sum(by_row.T, axis=0, keepdims=True)

        @pl.when(n >= count)
        def _():
            for out in outs:
                out[rows, :] = jnp.zeros((BLOCK_ROWS, width), jnp.bfloat16)

    @pl.when(last)
    def _():
        acc[...] = jnp.zeros(acc.shape, acc.dtype)

    @pl.when(jnp.logical_not(last))
    def _():
        acc[...] = later[...]

    for n in reversed(range(slots)):
        rows = slice(n * BLOCK_ROWS, (n + 1) * BLOCK_ROWS)

        @pl.when(n < count)
        def _():
            for h in range(heads):
                q_h, k_h, v_h, c_h = (
                    buf[n, :, head(h)] for buf in (q_buf, k_buf, v_buf, c_buf)
                )
                so_far = acc[h]
                state = so_far.astype(jnp.bfloat16)
                scores = jnp.where(above, dot_nt(k_h, q_h), 0.0).astype(jnp.bfloat16)
                d_value[rows, head(h)] = (
                    factor * (dot(scores, c_h) + dot_nt(k_h, state))
                ).astype(jnp.bfloat16)

                def key_part():
                    grads = jnp.where(above, dot_nt(v_h, c_h), 0.0).astype(jnp.bfloat16)
                    d_key[rows, head(h)] = (
                        factor * (dot(grads, q_h) + dot(v_h, state))
                    ).astype(jnp.bfloat16)

                if split:
                    pl.when(first)(key_part)
                else:
                    key_part()
                acc[h] = so_far + dot_tn(c_h, q_h)


def late(factor, split, router, blocks, counts, earlier, later, q, k, v, g):
    slots = blocks.shape[2]
    width = q.shape[2]
    heads = width // HEAD_SIZE
    tile = (slots, BLOCK_ROWS, width)
    pieces = 2 if split else 3
    rows = slots * BLOCK_ROWS
    return pl.pallas_call(
        functools.partial(late_kernel, factor, split),
        name="late",
        out_shape=(jax.ShapeDtypeStruct((rows, width), jnp.bfloat16),) * pieces
        + (jax.ShapeDtypeStruct((1, rows), jnp.float32),),
        in_specs=[SMEM, SMEM, VMEM, VMEM, VMEM, ANY, ANY, ANY, ANY],
        out_specs=(VMEM,) * (pieces + 1),
        scratch_shapes=[pltpu.VMEM(tile, jnp.bfloat16)] * 5
        + [
            pltpu.VMEM((heads, HEAD_SIZE, HEAD_SIZE), jnp.float32),
            pltpu.SemaphoreType.DMA((4, slots)),
        ],
        cost_estimate=pl.CostEstimate(
            flops=2 * 12 * slots * heads * HEAD_SIZE**3,
            bytes_accessed=2 * 6 * slots * BLOCK_ROWS * width,
            transcendentals=0,
        ),
    )(blocks, counts, router, earlier, later, q, k, v, g)


def place_kernel(at_first, at_other, *refs):
    chunk, out, buf, in_sem, out_sem = refs[-5:]
    slots = buf.shape[0]
    if at_first == at_other:
        section = at_first
    else:
        section = jnp.where(lax.axis_index("seq") == 0, at_first, at_other)
    gets, puts = [], []
    for i in range(slots):
        rows = pl.ds(i * BLOCK_ROWS, BLOCK_ROWS)
        gets.append(pltpu.make_async_copy(chunk.at[rows], buf.at[i], in_sem.at[i]))
        puts.append(pltpu.make_async_copy(buf.at[i], out.at[0, section, rows], out_sem.at[i]))
        gets[i].start()
    for i in range(slots):
        gets[i].wait()
        puts[i].start()
    for i in range(slots):
        puts[i].wait()


def place(whole, chunk, sections, at_first, at_other):
    rows, width = chunk.shape
    slots = rows // BLOCK_ROWS
    operands = (chunk,) if whole is None else (whole, chunk)
    return pl.pallas_call(
        functools.partial(place_kernel, at_first, at_other),
        name="place",
        out_shape=jax.ShapeDtypeStruct((1, sections, rows, width), chunk.dtype),
        in_specs=[ANY] * len(operands),
        out_specs=ANY,
        scratch_shapes=[
            pltpu.VMEM((slots, BLOCK_ROWS, width), chunk.dtype),
            pltpu.SemaphoreType.DMA((slots,)),
            pltpu.SemaphoreType.DMA((slots,)),
        ],
        input_output_aliases={} if whole is None else {0: 0},
        cost_estimate=pl.CostEstimate(
            flops=0, bytes_accessed=4 * rows * width, transcendentals=0
        ),
    )(*operands)


def shard_states(queries, keys, values, grad_out, router, blocks, counts):
    heads = queries.shape[2] // HEAD_SIZE
    slots = blocks.shape[2]
    shard_blocks = queries.shape[1] // BLOCK_ROWS
    live = jnp.arange(slots, dtype=jnp.int32) < counts[0, 0]
    taken = (blocks[0, 0, :, None] == jnp.arange(shard_blocks, dtype=jnp.int32)) & live[:, None]
    mask = jnp.repeat(jnp.any(taken, axis=0), BLOCK_ROWS)[:, None]

    def rows(array):
        picked = jnp.where(mask, array[0], jnp.zeros((), array.dtype))
        return picked.reshape(-1, heads, HEAD_SIZE)

    weighted = (router[0][:, None, None] * rows(grad_out).astype(jnp.float32)).astype(jnp.bfloat16)
    key_value = jnp.einsum(
        "the,thd->hed", rows(values), rows(keys), preferred_element_type=jnp.float32
    )
    query_grad = jnp.einsum(
        "the,thd->hed", weighted, rows(queries), preferred_element_type=jnp.float32
    )
    return key_value, query_grad


def on_device(queries, keys, values, grad_out, router, blocks, counts):
    slots = blocks.shape[2]
    rows = slots * BLOCK_ROWS
    seq_count = lax.axis_size("seq")
    factor = 1.0 / math.sqrt(HEAD_SIZE * rows * seq_count)
    arrays = (queries, keys, values, grad_out)
    small = (router, blocks, counts)
    if seq_count == 2:
        state, chunk_a = early(factor, *small, *arrays)
        other = from_behind(state, "seq", 1)
        chunk_a = from_behind(chunk_a, "pipe", -1)
        chunk_b, chunk_c, partial = late(factor, True, *small, other, other, *arrays)
        chunk_b = from_behind(chunk_b, "pipe", -1)
        chunk_c = from_behind(chunk_c, "pipe", -1)
        handed = place(None, chunk_a, 3, 0, 1)
        handed = place(handed, chunk_b, 3, 1, 0)
        handed = place(handed, chunk_c, 3, 2, 2)
    else:
        index = lax.axis_index("seq")
        places = jnp.arange(seq_count)[:, None, None, None]
        key_value, query_grad = shard_states(*arrays, *small)
        gathered = lax.all_gather(key_value, "seq")
        earlier = jnp.sum(jnp.where(places < index, gathered, 0.0), axis=0)
        gathered = lax.all_gather(query_grad, "seq")
        later = jnp.sum(jnp.where(places > index, gathered, 0.0), axis=0)
        *chunks, partial = late(factor, False, *small, earlier, later, *arrays)
        handed = None
        for section, chunk in enumerate(chunks):
            handed = place(handed, from_behind(chunk, "pipe", -1), 3, section, section)
    router_grad = lax.psum(partial, "tp")
    return (handed, router_grad)


def solution(mesh):
    return jax.shard_map(
        on_device,
        mesh=mesh,
        in_specs=(
            P("pipe", "seq", "tp"),
            P("pipe", "seq", "tp"),
            P("pipe", "seq", "tp"),
            P("pipe", "seq", "tp"),
            P("pipe", "seq"),
            P("pipe", "seq", None),
            P("pipe", "seq"),
        ),
        out_specs=(P("pipe", None, "seq", "tp"), P("pipe", "seq")),
        check_vma=False,
    )
```

```python
import functools
import math

import jax
import jax.numpy as jnp
from jax import lax
from jax.experimental import pallas as pl
from jax.experimental.pallas import tpu as pltpu
from jax.sharding import PartitionSpec as P


HEAD_SIZE = 128
BLOCK_ROWS = 128
GRANT = 16 * 2**20


ANY = pl.BlockSpec(memory_space=pl.ANY)
HBM = pl.BlockSpec(memory_space=pltpu.HBM)
VMEM = pl.BlockSpec(memory_space=pltpu.VMEM)


def from_behind(x, axis, by):
    count = lax.axis_size(axis)
    return lax.ppermute(x, axis, [(i, (i + by) % count) for i in range(count)])


def in_hbm(x):
    return pltpu.with_memory_space_constraint(x, pltpu.HBM)


def dot(a, b):
    return jnp.dot(a, b, preferred_element_type=jnp.float32)


def dot_nt(a, b):
    return lax.dot_general(a, b, (((1,), (1,)), ((), ())), preferred_element_type=jnp.float32)


def dot_tn(a, b):
    return lax.dot_general(a, b, (((0,), (0,)), ((), ())), preferred_element_type=jnp.float32)


def lanes(h, count=1):
    return pl.ds(h * HEAD_SIZE, count * HEAD_SIZE)


def rows_of(n):
    if isinstance(n, int):
        return pl.ds(n * BLOCK_ROWS, BLOCK_ROWS)
    return pl.ds(pl.multiple_of(n * BLOCK_ROWS, BLOCK_ROWS), BLOCK_ROWS)


def down_rows(router, block):
    weight = router[0:1, rows_of(block)]
    return jnp.broadcast_to(weight, (BLOCK_ROWS, BLOCK_ROWS)).T


def row_minus_column():
    shape = (BLOCK_ROWS, BLOCK_ROWS)
    return lax.broadcasted_iota(jnp.int32, shape, 0) - lax.broadcasted_iota(jnp.int32, shape, 1)


def compiler_params():
    return pltpu.CompilerParams(vmem_limit_bytes=GRANT)


def cost(matmuls, moved):
    return pl.CostEstimate(
        flops=2 * matmuls * HEAD_SIZE**3, bytes_accessed=moved, transcendentals=0
    )


def is_first():
    return lax.axis_index("seq") == 0


def is_last():
    return lax.axis_index("seq") != 0


def always():
    return jnp.bool_(True)


def never():
    return jnp.bool_(False)


def start_small(router, blocks, router_buf, blocks_buf, sem):
    copies = [
        pltpu.make_async_copy(blocks, blocks_buf, sem.at[0]),
        pltpu.make_async_copy(router, router_buf, sem.at[1]),
    ]
    for copy in copies:
        copy.start()
    return copies


def small_scratch(router, blocks):
    return [
        pltpu.VMEM(router.shape, router.dtype),
        pltpu.SMEM(blocks.shape, blocks.dtype),
        pltpu.SemaphoreType.DMA((2,)),
    ]


def live_count(blocks):
    count = jnp.int32(1)
    for n in range(1, blocks.shape[2]):
        count = count + jnp.where(blocks[0, 0, n] > 0, 1, 0)
    return count


def drain(blocks, count, slots, shard_blocks, wait):
    for b in range(shard_blocks):
        taken = never()
        for n in range(slots):
            taken = jnp.logical_or(taken, jnp.logical_and(n < count, blocks[0, 0, n] == b))

        @pl.when(jnp.logical_not(taken))
        def _():
            wait(b)


def side_kernel(
    factor, query_side, begin, end, keep, seeded, *refs,
):
    router, blocks, q, k, v, g = refs[:6]
    refs = refs[6:]
    if seeded:
        seed, refs = refs[0], refs[1:]
    chunk, refs = refs[0], refs[1:]
    if keep:
        total, states, refs = refs[0], refs[1], refs[2:]
    router_buf, blocks_buf, small_sem, x_buf, vc_buf, g_buf, acc, in_sem = refs
    slots = blocks_buf.shape[2]
    shard_blocks = x_buf.shape[0]
    low, high = (0, acc.shape[0]) if keep else (begin, end)
    span = high - low

    for_query = query_side()
    left = jnp.where(for_query, 1, 0)
    right = 1 - left
    sign = jnp.where(for_query, 1, -1)

    def loads(b):
        return (
            pltpu.make_async_copy(g.at[0, rows_of(b), lanes(low, span)], g_buf.at[b], in_sem.at[0, b]),
            pltpu.make_async_copy(v.at[0, rows_of(b), lanes(low, span)], vc_buf.at[0, b], in_sem.at[1, b]),
            pltpu.make_async_copy(k.at[0, rows_of(b), lanes(low, span)], x_buf.at[b], in_sem.at[2, b]),
            pltpu.make_async_copy(q.at[0, rows_of(b), lanes(low, span)], x_buf.at[b], in_sem.at[2, b]),
        )

    small = start_small(router, blocks, router_buf, blocks_buf, small_sem)
    for j in range(shard_blocks):
        g_load, v_load, k_load, q_load = loads(
            jnp.where(for_query, j, shard_blocks - 1 - j)
        )
        g_load.start()
        v_load.start()
        pl.when(for_query)(k_load.start)
        pl.when(jnp.logical_not(for_query))(q_load.start)

    allowed = row_minus_column() * sign >= 0
    for copy in small:
        copy.wait()
    count = live_count(blocks_buf)

    for i in range(slots):
        @pl.when(i < count)
        def _():
            n = jnp.where(for_query, i, count - 1 - i)
            b = blocks_buf[0, 0, n]
            g_load, v_load, x_load, _ = loads(b)
            weight = down_rows(router_buf, b)
            g_load.wait()
            for h in range(span):
                vc_buf[1, b, :, lanes(h)] = (
                    weight * g_buf[b, :, lanes(h)].astype(jnp.float32)
                ).astype(jnp.bfloat16)
            v_load.wait()
            x_load.wait()
            for h in range(low, high):
                at = lanes(h - low)
                l_h = vc_buf[left, b, :, at]
                r_h = vc_buf[right, b, :, at]
                x_h = x_buf[b, :, at]
                if i > 0:
                    so_far = acc[h - low]
                elif seeded:
                    so_far = seed[h]
                else:
                    so_far = None
                if so_far is not None:
                    state = so_far.astype(jnp.bfloat16)
                if begin <= h < end:
                    scores = jnp.where(allowed, dot_nt(l_h, r_h), 0.0).astype(jnp.bfloat16)
                    if so_far is None:
                        out = dot(scores, x_h)
                    else:
                        out = dot(
                            jnp.concatenate([scores, l_h], axis=1),
                            jnp.concatenate([x_h, state], axis=0),
                        )
                    chunk[rows_of(n), lanes(h - begin)] = (factor * out).astype(jnp.bfloat16)
                if keep:
                    states[n, h] = (
                        jnp.zeros((HEAD_SIZE, HEAD_SIZE), jnp.bfloat16)
                        if so_far is None else state
                    )
                added = dot_tn(r_h, x_h)
                acc[h - low] = added if so_far is None else so_far + added

        @pl.when(i >= count)
        def _():
            chunk[rows_of(i), :] = jnp.zeros((BLOCK_ROWS, chunk.shape[1]), chunk.dtype)

    if keep:
        total[...] = acc[...]

    def wait(b):
        g_load, v_load, x_load, _ = loads(b)
        g_load.wait()
        v_load.wait()
        x_load.wait()

    drain(blocks_buf, count, slots, shard_blocks, wait)


def side(factor, query_side, begin, end, keep, small, arrays, seed=None):
    router, blocks = small
    _, shard_rows, width = arrays[0].shape
    shard_blocks = shard_rows // BLOCK_ROWS
    heads = width // HEAD_SIZE
    slots = blocks.shape[2]
    span = heads if keep else end - begin
    tile = (shard_blocks, BLOCK_ROWS, span * HEAD_SIZE)
    out_shape = [pltpu.VMEM((slots * BLOCK_ROWS, (end - begin) * HEAD_SIZE), jnp.bfloat16)]
    if keep:
        out_shape.append(pltpu.VMEM((heads, HEAD_SIZE, HEAD_SIZE), jnp.float32))
        out_shape.append(pltpu.VMEM((slots, heads, HEAD_SIZE, HEAD_SIZE), jnp.bfloat16))
    extra = () if seed is None else (seed,)
    return pl.pallas_call(
        functools.partial(
            side_kernel, factor, query_side, begin, end, keep, seed is not None
        ),
        name="side",
        out_shape=out_shape,
        in_specs=[HBM] * 6 + [VMEM] * len(extra),
        out_specs=[VMEM] * len(out_shape),
        scratch_shapes=small_scratch(*small)
        + [
            pltpu.VMEM(tile, jnp.bfloat16),
            pltpu.VMEM((2,) + tile, jnp.bfloat16),
            pltpu.VMEM(tile, jnp.bfloat16),
            pltpu.VMEM((span, HEAD_SIZE, HEAD_SIZE), jnp.float32),
            pltpu.SemaphoreType.DMA((3, shard_blocks)),
        ],
        compiler_params=compiler_params(),
        cost_estimate=cost(5 * slots * span, 8 * shard_rows * span * HEAD_SIZE),
    )(router, blocks, *arrays, *extra)


def value_kernel(
    factor, take_one, router, blocks, q, k, v, g, one, two, chunk,
    router_buf, blocks_buf, small_sem, q_buf, k_buf, g_buf, in_sem,
):
    del v
    slots = blocks_buf.shape[2]
    shard_blocks, _, width = q_buf.shape
    heads = width // HEAD_SIZE
    pick_one = take_one()

    def loads(b):
        return [
            pltpu.make_async_copy(source.at[0, rows_of(b)], buf.at[b], in_sem.at[j, b])
            for j, (source, buf) in enumerate(((q, q_buf), (k, k_buf), (g, g_buf)))
        ]

    small = start_small(router, blocks, router_buf, blocks_buf, small_sem)
    for b in range(shard_blocks):
        for load in loads(b):
            load.start()
    allowed = row_minus_column() <= 0
    for copy in small:
        copy.wait()
    count = live_count(blocks_buf)

    for n in range(slots):
        @pl.when(n < count)
        def _():
            b = blocks_buf[0, 0, n]
            weight = down_rows(router_buf, b)
            for load in loads(b):
                load.wait()
            for h in range(heads):
                q_h = q_buf[b, :, lanes(h)]
                k_h = k_buf[b, :, lanes(h)]
                c_h = (weight * g_buf[b, :, lanes(h)].astype(jnp.float32)).astype(jnp.bfloat16)
                state = jnp.where(pick_one, one[n, h], two[n, h])
                scores = jnp.where(allowed, dot_nt(k_h, q_h), 0.0).astype(jnp.bfloat16)
                out = dot(scores, c_h) + dot_nt(k_h, state)
                chunk[rows_of(n), lanes(h)] = (factor * out).astype(jnp.bfloat16)

        @pl.when(n >= count)
        def _():
            chunk[rows_of(n), :] = jnp.zeros((BLOCK_ROWS, width), chunk.dtype)

    def wait(b):
        for load in loads(b):
            load.wait()

    drain(blocks_buf, count, slots, shard_blocks, wait)


def value_side(factor, take_one, small, arrays, one, two):
    router, blocks = small
    _, shard_rows, width = arrays[0].shape
    shard_blocks = shard_rows // BLOCK_ROWS
    heads = width // HEAD_SIZE
    slots = blocks.shape[2]
    tile = (shard_blocks, BLOCK_ROWS, width)
    return pl.pallas_call(
        functools.partial(value_kernel, factor, take_one),
        name="value_side",
        out_shape=pltpu.VMEM((slots * BLOCK_ROWS, width), jnp.bfloat16),
        in_specs=[HBM] * 6 + [VMEM] * 2,
        out_specs=VMEM,
        scratch_shapes=small_scratch(*small)
        + [pltpu.VMEM(tile, jnp.bfloat16)] * 3
        + [pltpu.SemaphoreType.DMA((3, shard_blocks))],
        compiler_params=compiler_params(),
        cost_estimate=cost(3 * slots * heads, 8 * shard_rows * width),
    )(router, blocks, *arrays, one, two)


def router_kernel(
    factor, take_one, router, blocks, q, k, v, g, one, two, partial,
    router_buf, blocks_buf, small_sem, q_buf, k_buf, v_buf, g_buf, in_sem,
):
    slots = blocks_buf.shape[2]
    shard_blocks, _, width = q_buf.shape
    heads = width // HEAD_SIZE
    pick_one = take_one()

    def loads(b):
        return [
            pltpu.make_async_copy(source.at[0, rows_of(b)], buf.at[b], in_sem.at[j, b])
            for j, (source, buf) in enumerate(((q, q_buf), (k, k_buf), (v, v_buf), (g, g_buf)))
        ]

    small = start_small(router, blocks, router_buf, blocks_buf, small_sem)
    for b in range(shard_blocks):
        for load in loads(b):
            load.start()
    allowed = row_minus_column() >= 0
    for copy in small:
        copy.wait()
    count = live_count(blocks_buf)

    for n in range(slots):
        @pl.when(n < count)
        def _():
            b = blocks_buf[0, 0, n]
            for load in loads(b):
                load.wait()
            by_row = jnp.zeros((BLOCK_ROWS, HEAD_SIZE), jnp.float32)
            for h in range(heads):
                q_h = q_buf[b, :, lanes(h)]
                k_h = k_buf[b, :, lanes(h)]
                v_h = v_buf[b, :, lanes(h)]
                state = jnp.where(pick_one, one[n, h], two[n, h])
                scores = jnp.where(allowed, dot_nt(q_h, k_h), 0.0).astype(jnp.bfloat16)
                core = factor * (dot(scores, v_h) + dot_nt(q_h, state))
                by_row = by_row + g_buf[b, :, lanes(h)].astype(jnp.float32) * core
            partial[0:1, rows_of(n)] = jnp.sum(by_row.T, axis=0, keepdims=True)

        @pl.when(n >= count)
        def _():
            partial[0:1, rows_of(n)] = jnp.zeros((1, BLOCK_ROWS), jnp.float32)

    def wait(b):
        for load in loads(b):
            load.wait()

    drain(blocks_buf, count, slots, shard_blocks, wait)


def router_side(factor, take_one, small, arrays, one, two):
    router, blocks = small
    _, shard_rows, width = arrays[0].shape
    shard_blocks = shard_rows // BLOCK_ROWS
    heads = width // HEAD_SIZE
    slots = blocks.shape[2]
    tile = (shard_blocks, BLOCK_ROWS, width)
    return pl.pallas_call(
        functools.partial(router_kernel, factor, take_one),
        name="router_side",
        out_shape=jax.ShapeDtypeStruct((1, slots * BLOCK_ROWS), jnp.float32),
        in_specs=[HBM] * 6 + [VMEM] * 2,
        out_specs=VMEM,
        scratch_shapes=small_scratch(*small)
        + [pltpu.VMEM(tile, jnp.bfloat16)] * 4
        + [pltpu.SemaphoreType.DMA((4, shard_blocks))],
        compiler_params=compiler_params(),
        cost_estimate=cost(3 * slots * heads, 8 * shard_rows * width),
    )(router, blocks, *arrays, one, two)


def place_kernel(section_of, begin, *refs):
    chunk, out, sem = refs[-3:]
    width = chunk.shape[1] // HEAD_SIZE
    copy = pltpu.make_async_copy(chunk, out.at[0, section_of(), :, lanes(begin, width)], sem)
    copy.start()
    copy.wait()


def place(whole, chunk, shape, section_of, begin):
    rows, width = chunk.shape
    operands = (chunk,) if whole is None else (whole, chunk)
    return pl.pallas_call(
        functools.partial(place_kernel, section_of, begin),
        name="place",
        out_shape=jax.ShapeDtypeStruct(shape, chunk.dtype),
        in_specs=[HBM] * (len(operands) - 1) + [ANY],
        out_specs=HBM,
        scratch_shapes=[pltpu.SemaphoreType.DMA],
        input_output_aliases={} if whole is None else {0: 0},
        compiler_params=pltpu.CompilerParams(vmem_limit_bytes=2**20),
        cost_estimate=cost(0, 4 * rows * width),
    )(*operands)


def shard_states(queries, keys, values, grad_out, router, blocks, counts):
    heads = queries.shape[2] // HEAD_SIZE
    slots = blocks.shape[2]
    shard_blocks = queries.shape[1] // BLOCK_ROWS
    live = jnp.arange(slots, dtype=jnp.int32) < counts[0, 0]
    taken = (blocks[0, 0, :, None] == jnp.arange(shard_blocks, dtype=jnp.int32)) & live[:, None]
    mask = jnp.repeat(jnp.any(taken, axis=0), BLOCK_ROWS)[:, None]

    def rows(array):
        picked = jnp.where(mask, array[0], jnp.zeros((), array.dtype))
        return picked.reshape(-1, heads, HEAD_SIZE)

    weighted = (router[0][:, None, None] * rows(grad_out).astype(jnp.float32)).astype(jnp.bfloat16)
    key_value = jnp.einsum(
        "the,thd->hed", rows(values), rows(keys), preferred_element_type=jnp.float32
    )
    query_grad = jnp.einsum(
        "the,thd->hed", weighted, rows(queries), preferred_element_type=jnp.float32
    )
    return key_value, query_grad


def own_side():
    return jnp.where(is_first(), 0, 1)


def other_side():
    return jnp.where(is_first(), 1, 0)


def on_device(queries, keys, values, grad_out, router, blocks, counts):
    slots = blocks.shape[2]
    rows = slots * BLOCK_ROWS
    width = queries.shape[2]
    heads = width // HEAD_SIZE
    seq_count = lax.axis_size("seq")
    factor = 1.0 / math.sqrt(HEAD_SIZE * rows * seq_count)
    arrays = tuple(in_hbm(x) for x in (queries, keys, values, grad_out))
    small = (in_hbm(router), in_hbm(blocks))
    shape = (1, 3, rows, width)
    if seq_count == 2:
        head_start = max(1, heads // 3)

        def sent(x, axis="pipe", by=-1):
            return from_behind(x, axis, by)

        def kernel(call, *operands):
            return call(factor, *operands)

        (chunk_a,) = kernel(side, is_first, 0, head_start, False, small, arrays)
        chunk_a = sent(chunk_a)
        chunk_b, total, own = kernel(side, is_first, head_start, heads, True, small, arrays)
        total = sent(total, "seq", 1)
        chunk_b = sent(chunk_b)
        chunk_c, _, other = kernel(side, is_last, 0, heads, True, small, arrays, total)
        chunk_c = sent(chunk_c)
        chunk_d = kernel(value_side, is_last, small, arrays, own, other)
        chunk_d = sent(chunk_d)
        partial = kernel(router_side, is_first, small, arrays, own, other)
        handed = place(None, chunk_a, shape, own_side, 0)
        handed = place(handed, chunk_b, shape, own_side, head_start)
        handed = place(handed, chunk_c, shape, other_side, 0)
        handed = place(handed, chunk_d, shape, lambda: 2, 0)
    else:
        index = lax.axis_index("seq")
        places = jnp.arange(seq_count)[:, None, None, None]
        key_value, query_grad = shard_states(queries, keys, values, grad_out, router, blocks, counts)
        gathered = lax.all_gather(key_value, "seq")
        earlier = jnp.sum(jnp.where(places < index, gathered, 0.0), axis=0)
        gathered = lax.all_gather(query_grad, "seq")
        later = jnp.sum(jnp.where(places > index, gathered, 0.0), axis=0)
        d_query, _, before = side(factor, always, 0, heads, True, small, arrays, earlier)
        d_key, _, after = side(factor, never, 0, heads, True, small, arrays, later)
        d_value = value_side(factor, always, small, arrays, after, after)
        partial = router_side(factor, always, small, arrays, before, before)
        handed = None
        for section, chunk in enumerate((d_query, d_key, d_value)):
            chunk = from_behind(chunk, "pipe", -1)
            handed = place(handed, chunk, shape, functools.partial(int, section), 0)
    router_grad = lax.psum(partial, "tp")
    return (handed, router_grad)


def solution(mesh):
    return jax.shard_map(
        on_device,
        mesh=mesh,
        in_specs=(
            P("pipe", "seq", "tp"),
            P("pipe", "seq", "tp"),
            P("pipe", "seq", "tp"),
            P("pipe", "seq", "tp"),
            P("pipe", "seq"),
            P("pipe", "seq", None),
            P("pipe", "seq"),
        ),
        out_specs=(P("pipe", None, "seq", "tp"), P("pipe", "seq")),
        check_vma=False,
    )
```

```python
import functools
import math

import jax
import jax.numpy as jnp
from jax import lax
from jax.experimental import pallas as pl
from jax.experimental.pallas import tpu as pltpu
from jax.sharding import PartitionSpec as P


HEAD_SIZE = 128
BLOCK_ROWS = 128
GRANT = 16 * 2**20


ANY = pl.BlockSpec(memory_space=pl.ANY)
HBM = pl.BlockSpec(memory_space=pltpu.HBM)
VMEM = pl.BlockSpec(memory_space=pltpu.VMEM)
SMEM = pl.BlockSpec(memory_space=pltpu.SMEM)


def from_behind(x, axis, by):
    count = lax.axis_size(axis)
    return lax.ppermute(x, axis, [(i, (i + by) % count) for i in range(count)])


def in_hbm(x):
    return pltpu.with_memory_space_constraint(x, pltpu.HBM)


def dot(a, b):
    return jnp.dot(a, b, preferred_element_type=jnp.float32)


def dot_nt(a, b):
    return lax.dot_general(a, b, (((1,), (1,)), ((), ())), preferred_element_type=jnp.float32)


def dot_tn(a, b):
    return lax.dot_general(a, b, (((0,), (0,)), ((), ())), preferred_element_type=jnp.float32)


def lanes(h, count=1):
    return pl.ds(h * HEAD_SIZE, count * HEAD_SIZE)


def rows_of(n):
    if isinstance(n, int):
        return pl.ds(n * BLOCK_ROWS, BLOCK_ROWS)
    return pl.ds(pl.multiple_of(n * BLOCK_ROWS, BLOCK_ROWS), BLOCK_ROWS)


def down_rows(router, block):
    weight = router[0:1, rows_of(block)]
    return jnp.broadcast_to(weight, (BLOCK_ROWS, BLOCK_ROWS)).T


def row_minus_column():
    shape = (BLOCK_ROWS, BLOCK_ROWS)
    return lax.broadcasted_iota(jnp.int32, shape, 0) - lax.broadcasted_iota(jnp.int32, shape, 1)


def compiler_params():
    return pltpu.CompilerParams(vmem_limit_bytes=GRANT)


def cost(matmuls, moved):
    return pl.CostEstimate(
        flops=2 * matmuls * HEAD_SIZE**3, bytes_accessed=moved, transcendentals=0
    )


def is_first():
    return lax.axis_index("seq") == 0


def is_last():
    return lax.axis_index("seq") != 0


def always():
    return True


def never():
    return False


def live_of(blocks, n):
    return jnp.bool_(True) if n == 0 else blocks[0, 0, n] > 0


def by_role(query_side, body):
    flag = query_side()
    if isinstance(flag, bool):
        body(flag)
    else:
        pl.when(flag)(lambda: body(True))
        pl.when(jnp.logical_not(flag))(lambda: body(False))


def in_order(query, slots):
    return list(range(slots)) if query else list(reversed(range(slots)))


def weigh(weight, grad):
    return (weight * grad.astype(jnp.float32)).astype(jnp.bfloat16)


def open_kernel(
    factor, query_side, end, router, blocks, q, k, v, g, chunk, q_all, k_all, v_all, g_all,
    router_all, blocks_all, acc, small_sem, head_sem, rest_sem,
):
    slots = blocks.shape[2]
    heads = q_all.shape[1] // HEAD_SIZE
    small = [
        pltpu.make_async_copy(blocks, blocks_all, small_sem.at[0]),
        pltpu.make_async_copy(router, router_all, small_sem.at[1]),
    ]
    pairs = ((g, g_all), (v, v_all), (k, k_all), (q, q_all))
    first_loads = [
        pltpu.make_async_copy(
            source.at[0, :, lanes(0, end)], target.at[:, lanes(0, end)], head_sem.at[j]
        )
        for j, (source, target) in enumerate(pairs)
    ]
    rest_loads = [
        pltpu.make_async_copy(
            source.at[0, :, lanes(end, heads - end)],
            target.at[:, lanes(end, heads - end)],
            rest_sem.at[j],
        )
        for j, (source, target) in enumerate(pairs)
    ]
    for load in small + first_loads + rest_loads:
        load.start()
    difference = row_minus_column()
    for load in small:
        load.wait()
    for load in first_loads:
        load.wait()

    def body(query):
        allowed = difference >= 0 if query else difference <= 0
        x_all = k_all if query else q_all
        order = in_order(query, slots)
        for i, n in enumerate(order):
            live = live_of(blocks_all, n)
            block = blocks_all[0, 0, n]
            rows = rows_of(block)
            weight = jnp.where(live, down_rows(router_all, block), 0.0)
            scale = jnp.where(live, factor, 0.0)
            for h in range(end):
                c_h = weigh(weight, g_all[rows, lanes(h)])
                v_h = v_all[rows, lanes(h)]
                l_h, r_h = (c_h, v_h) if query else (v_h, c_h)
                x_h = x_all[rows, lanes(h)]
                scores = jnp.where(allowed, dot_nt(l_h, r_h), 0.0).astype(jnp.bfloat16)
                if i == 0:
                    out = dot(scores, x_h)
                else:
                    out = dot(
                        jnp.concatenate([scores, l_h], axis=1),
                        jnp.concatenate([x_h, acc[h].astype(jnp.bfloat16)], axis=0),
                    )
                chunk[rows_of(n), lanes(h)] = (scale * out).astype(jnp.bfloat16)
                if i + 1 < slots:
                    added = dot_tn(r_h, x_h)
                    acc[h] = added if i == 0 else acc[h] + added

    by_role(query_side, body)
    for load in rest_loads:
        load.wait()


def opened(factor, query_side, end, small, arrays):
    router, blocks = small
    _, shard_rows, width = arrays[0].shape
    slots = blocks.shape[2]
    whole = pltpu.VMEM((shard_rows, width), jnp.bfloat16)
    out_shape = [
        pltpu.VMEM((slots * BLOCK_ROWS, end * HEAD_SIZE), jnp.bfloat16),
        whole, whole, whole, whole,
        pltpu.VMEM(router.shape, router.dtype),
        pltpu.SMEM(blocks.shape, blocks.dtype),
    ]
    return pl.pallas_call(
        functools.partial(open_kernel, factor, query_side, end),
        name="opened",
        out_shape=out_shape,
        in_specs=[HBM] * 6,
        out_specs=[VMEM] * 6 + [SMEM],
        scratch_shapes=[
            pltpu.VMEM((end, HEAD_SIZE, HEAD_SIZE), jnp.float32),
            pltpu.SemaphoreType.DMA((2,)),
            pltpu.SemaphoreType.DMA((4,)),
            pltpu.SemaphoreType.DMA((4,)),
        ],
        compiler_params=compiler_params(),
        cost_estimate=cost(4 * slots * end, 8 * shard_rows * width),
    )(router, blocks, *arrays)


def side_kernel(factor, query_side, begin, make_c, *refs):
    (router, blocks, q, k, v, g), refs = refs[:6], refs[6:]
    if make_c:
        chunk, states, total, c_all, scores_buf = refs
    else:
        c_all, seed, chunk, states, scores_buf, total = refs
    slots = blocks.shape[2]
    heads = states.shape[1]
    difference = row_minus_column()

    def body(query):
        allowed = difference >= 0 if query else difference <= 0
        x_all = k if query else q
        order = in_order(query, slots)
        for i, n in enumerate(order):
            live = live_of(blocks, n)
            block = blocks[0, 0, n]
            rows = rows_of(block)
            own = rows_of(n)
            scale = jnp.where(live, factor, 0.0)
            if make_c:
                weight = jnp.where(live, down_rows(router, block), 0.0)
                for h in range(heads):
                    c_all[own, lanes(h)] = weigh(weight, g[rows, lanes(h)])

            def sides(h):
                c_h, v_h = c_all[own, lanes(h)], v[rows, lanes(h)]
                return (c_h, v_h) if query else (v_h, c_h)

            for h in range(begin, heads):
                l_h, r_h = sides(h)
                scores_buf[n, h] = jnp.where(allowed, dot_nt(l_h, r_h), 0.0).astype(jnp.bfloat16)
            for h in range(heads):
                if i > 0:
                    so_far = total[h]
                elif make_c:
                    so_far = jnp.zeros((HEAD_SIZE, HEAD_SIZE), jnp.float32)
                else:
                    so_far = seed[h]
                states[n, h] = so_far.astype(jnp.bfloat16)
                if make_c or i + 1 < slots:
                    added = dot_tn(sides(h)[1], x_all[rows, lanes(h)])
                    if query and n > 0:
                        added = jnp.where(live, added, 0.0)
                    total[h] = so_far + added
            for h in range(begin, heads):
                l_h, _ = sides(h)
                x_h = x_all[rows, lanes(h)]
                if i == 0 and make_c:
                    out = dot(scores_buf[n, h], x_h)
                else:
                    out = dot(
                        jnp.concatenate([scores_buf[n, h], l_h], axis=1),
                        jnp.concatenate([x_h, states[n, h]], axis=0),
                    )
                chunk[own, lanes(h - begin)] = (scale * out).astype(jnp.bfloat16)

    by_role(query_side, body)


def side(factor, query_side, begin, loaded, c_all=None, seed=None):
    blocks = loaded[1]
    width = loaded[2].shape[1]
    heads = width // HEAD_SIZE
    slots = blocks.shape[2]
    make_c = seed is None
    square = (HEAD_SIZE, HEAD_SIZE)
    total = pltpu.VMEM((heads,) + square, jnp.float32)
    out_shape = [
        pltpu.VMEM((slots * BLOCK_ROWS, (heads - begin) * HEAD_SIZE), jnp.bfloat16),
        pltpu.VMEM((slots, heads) + square, jnp.bfloat16),
    ]
    scratch = [pltpu.VMEM((slots, heads) + square, jnp.bfloat16)]
    if make_c:
        out_shape += [total, pltpu.VMEM((slots * BLOCK_ROWS, width), jnp.bfloat16)]
        extra = ()
    else:
        scratch.append(total)
        extra = (c_all, seed)
    return pl.pallas_call(
        functools.partial(side_kernel, factor, query_side, begin, make_c),
        name="side",
        out_shape=out_shape,
        in_specs=[VMEM, SMEM] + [VMEM] * (4 + len(extra)),
        out_specs=[VMEM] * len(out_shape),
        scratch_shapes=scratch,
        compiler_params=compiler_params(),
        cost_estimate=cost(4 * slots * heads, 0),
    )(*loaded, *extra)


def value_kernel(factor, take_one, blocks, q, k, c_all, one, two, chunk, scores_buf):
    slots = blocks.shape[2]
    heads = q.shape[1] // HEAD_SIZE
    allowed = row_minus_column() <= 0

    def body(pick):
        states = one if pick else two
        for n in range(slots):
            rows = rows_of(blocks[0, 0, n])
            own = rows_of(n)
            scale = jnp.where(live_of(blocks, n), factor, 0.0)
            for h in range(heads):
                scores_buf[n, h] = jnp.where(
                    allowed, dot_nt(k[rows, lanes(h)], q[rows, lanes(h)]), 0.0
                ).astype(jnp.bfloat16)
            for h in range(heads):
                out = dot(scores_buf[n, h], c_all[own, lanes(h)])
                out = out + dot_nt(k[rows, lanes(h)], states[n, h])
                chunk[own, lanes(h)] = (scale * out).astype(jnp.bfloat16)

    by_role(take_one, body)


def value_side(factor, take_one, loaded, c_all, one, two):
    _, blocks, q, k, _, _ = loaded
    slots, heads = one.shape[:2]
    return pl.pallas_call(
        functools.partial(value_kernel, factor, take_one),
        name="value_side",
        out_shape=pltpu.VMEM((slots * BLOCK_ROWS, heads * HEAD_SIZE), jnp.bfloat16),
        in_specs=[SMEM] + [VMEM] * 5,
        out_specs=VMEM,
        scratch_shapes=[pltpu.VMEM(one.shape, jnp.bfloat16)],
        compiler_params=compiler_params(),
        cost_estimate=cost(3 * slots * heads, 0),
    )(blocks, q, k, c_all, one, two)


def router_kernel(factor, take_one, blocks, q, k, v, g, one, two, partial, scores_buf):
    slots = blocks.shape[2]
    heads = q.shape[1] // HEAD_SIZE
    allowed = row_minus_column() >= 0

    def body(pick):
        states = one if pick else two
        for n in range(slots):
            rows = rows_of(blocks[0, 0, n])
            for h in range(heads):
                scores_buf[n, h] = jnp.where(
                    allowed, dot_nt(q[rows, lanes(h)], k[rows, lanes(h)]), 0.0
                ).astype(jnp.bfloat16)
            by_row = jnp.zeros((BLOCK_ROWS, HEAD_SIZE), jnp.float32)
            for h in range(heads):
                core = dot(scores_buf[n, h], v[rows, lanes(h)])
                core = factor * (core + dot_nt(q[rows, lanes(h)], states[n, h]))
                by_row = by_row + g[rows, lanes(h)].astype(jnp.float32) * core
            by_row = jnp.where(live_of(blocks, n), by_row, 0.0)
            partial[0:1, rows_of(n)] = jnp.sum(by_row.T, axis=0, keepdims=True)

    by_role(take_one, body)


def router_side(factor, take_one, loaded, one, two):
    _, blocks, *arrays = loaded
    slots = one.shape[0]
    return pl.pallas_call(
        functools.partial(router_kernel, factor, take_one),
        name="router_side",
        out_shape=jax.ShapeDtypeStruct((1, slots * BLOCK_ROWS), jnp.float32),
        in_specs=[SMEM] + [VMEM] * 6,
        out_specs=VMEM,
        scratch_shapes=[pltpu.VMEM(one.shape, jnp.bfloat16)],
        compiler_params=compiler_params(),
        cost_estimate=cost(3 * slots * one.shape[1], 0),
    )(blocks, *arrays, one, two)


def place_kernel(section_of, begin, *refs):
    chunk, out, sem = refs[-3:]
    width = chunk.shape[1] // HEAD_SIZE
    copy = pltpu.make_async_copy(chunk, out.at[0, section_of(), :, lanes(begin, width)], sem)
    copy.start()
    copy.wait()


def place(whole, chunk, shape, section_of, begin):
    rows, width = chunk.shape
    operands = (chunk,) if whole is None else (whole, chunk)
    return pl.pallas_call(
        functools.partial(place_kernel, section_of, begin),
        name="place",
        out_shape=jax.ShapeDtypeStruct(shape, chunk.dtype),
        in_specs=[HBM] * (len(operands) - 1) + [ANY],
        out_specs=HBM,
        scratch_shapes=[pltpu.SemaphoreType.DMA],
        input_output_aliases={} if whole is None else {0: 0},
        compiler_params=pltpu.CompilerParams(vmem_limit_bytes=2**20),
        cost_estimate=cost(0, 4 * rows * width),
    )(*operands)


def shard_states(queries, keys, values, grad_out, router, blocks, counts):
    heads = queries.shape[2] // HEAD_SIZE
    slots = blocks.shape[2]
    shard_blocks = queries.shape[1] // BLOCK_ROWS
    live = jnp.arange(slots, dtype=jnp.int32) < counts[0, 0]
    taken = (blocks[0, 0, :, None] == jnp.arange(shard_blocks, dtype=jnp.int32)) & live[:, None]
    mask = jnp.repeat(jnp.any(taken, axis=0), BLOCK_ROWS)[:, None]

    def rows(array):
        picked = jnp.where(mask, array[0], jnp.zeros((), array.dtype))
        return picked.reshape(-1, heads, HEAD_SIZE)

    weighted = (router[0][:, None, None] * rows(grad_out).astype(jnp.float32)).astype(jnp.bfloat16)
    key_value = jnp.einsum(
        "the,thd->hed", rows(values), rows(keys), preferred_element_type=jnp.float32
    )
    query_grad = jnp.einsum(
        "the,thd->hed", weighted, rows(queries), preferred_element_type=jnp.float32
    )
    return key_value, query_grad


def gathered_gradient(grad_out, router, blocks, counts):
    slots = blocks.shape[2]
    live = jnp.arange(slots, dtype=jnp.int32) < counts[0, 0]
    grouped = grad_out[0].reshape(-1, BLOCK_ROWS, grad_out.shape[2])[blocks[0, 0]]
    weight = jnp.where(live[:, None], router[0].reshape(-1, BLOCK_ROWS)[blocks[0, 0]], 0.0)
    weighted = weight[:, :, None] * grouped.astype(jnp.float32)
    return weighted.astype(jnp.bfloat16).reshape(slots * BLOCK_ROWS, -1)


def own_side():
    return jnp.where(is_first(), 0, 1)


def other_side():
    return jnp.where(is_first(), 1, 0)


def on_device(queries, keys, values, grad_out, router, blocks, counts):
    slots = blocks.shape[2]
    rows = slots * BLOCK_ROWS
    width = queries.shape[2]
    heads = width // HEAD_SIZE
    seq_count = lax.axis_size("seq")
    factor = 1.0 / math.sqrt(HEAD_SIZE * rows * seq_count)
    arrays = (queries, keys, values, grad_out)
    shape = (1, 3, rows, width)
    if seq_count == 2:
        head_start = max(1, heads // 3)
        small = (in_hbm(router), in_hbm(blocks))
        arrays = tuple(in_hbm(x) for x in arrays)

        def sent(x, axis="pipe", by=-1):
            return from_behind(x, axis, by)

        def kernel(call, *operands):
            return call(factor, *operands)

        chunk_a, *loaded = kernel(opened, is_first, head_start, small, arrays)
        loaded = (loaded[4], loaded[5], *loaded[:4])
        chunk_a = sent(chunk_a)
        chunk_b, own, total, c_all = kernel(side, is_first, head_start, loaded)
        total = sent(total, "seq", 1)
        chunk_b = sent(chunk_b)
        chunk_c, other = kernel(side, is_last, 0, loaded, c_all, total)
        chunk_c = sent(chunk_c)
        chunk_d = kernel(value_side, is_last, loaded, c_all, own, other)
        chunk_d = sent(chunk_d)
        partial = kernel(router_side, is_first, loaded, own, other)
        handed = place(None, chunk_a, shape, own_side, 0)
        handed = place(handed, chunk_b, shape, own_side, head_start)
        handed = place(handed, chunk_c, shape, other_side, 0)
        handed = place(handed, chunk_d, shape, lambda: 2, 0)
    else:
        index = lax.axis_index("seq")
        places = jnp.arange(seq_count)[:, None, None, None]
        key_value, query_grad = shard_states(queries, keys, values, grad_out, router, blocks, counts)
        gathered = lax.all_gather(key_value, "seq")
        earlier = jnp.sum(jnp.where(places < index, gathered, 0.0), axis=0)
        gathered = lax.all_gather(query_grad, "seq")
        later = jnp.sum(jnp.where(places > index, gathered, 0.0), axis=0)
        loaded = (router, blocks) + tuple(x[0] for x in arrays)
        c_all = gathered_gradient(grad_out, router, blocks, counts)
        d_query, before = side(factor, always, 0, loaded, c_all, earlier)
        d_key, after = side(factor, never, 0, loaded, c_all, later)
        d_value = value_side(factor, always, loaded, c_all, after, after)
        partial = router_side(factor, always, loaded, before, before)
        handed = None
        for section, chunk in enumerate((d_query, d_key, d_value)):
            chunk = from_behind(chunk, "pipe", -1)
            handed = place(handed, chunk, shape, functools.partial(int, section), 0)
    router_grad = lax.psum(partial, "tp")
    return (handed, router_grad)


def solution(mesh):
    return jax.shard_map(
        on_device,
        mesh=mesh,
        in_specs=(
            P("pipe", "seq", "tp"),
            P("pipe", "seq", "tp"),
            P("pipe", "seq", "tp"),
            P("pipe", "seq", "tp"),
            P("pipe", "seq"),
            P("pipe", "seq", None),
            P("pipe", "seq"),
        ),
        out_specs=(P("pipe", None, "seq", "tp"), P("pipe", "seq")),
        check_vma=False,
    )
```

```python
import functools
import math

import jax
import jax.numpy as jnp
from jax import lax
from jax.experimental import pallas as pl
from jax.experimental.pallas import tpu as pltpu
from jax.sharding import PartitionSpec as P


HEAD_SIZE = 128
BLOCK_ROWS = 128
GRANT = 16 * 2**20


ANY = pl.BlockSpec(memory_space=pl.ANY)
HBM = pl.BlockSpec(memory_space=pltpu.HBM)
VMEM = pl.BlockSpec(memory_space=pltpu.VMEM)
SMEM = pl.BlockSpec(memory_space=pltpu.SMEM)


def from_behind(x, axis, by):
    count = lax.axis_size(axis)
    return lax.ppermute(x, axis, [(i, (i + by) % count) for i in range(count)])


def in_hbm(x):
    return pltpu.with_memory_space_constraint(x, pltpu.HBM)


def dot(a, b):
    return jnp.dot(a, b, preferred_element_type=jnp.float32)


def dot_nt(a, b):
    return lax.dot_general(a, b, (((1,), (1,)), ((), ())), preferred_element_type=jnp.float32)


def dot_tn(a, b):
    return lax.dot_general(a, b, (((0,), (0,)), ((), ())), preferred_element_type=jnp.float32)


def lanes(h, count=1):
    return pl.ds(h * HEAD_SIZE, count * HEAD_SIZE)


def rows_of(n):
    if isinstance(n, int):
        return pl.ds(n * BLOCK_ROWS, BLOCK_ROWS)
    return pl.ds(pl.multiple_of(n * BLOCK_ROWS, BLOCK_ROWS), BLOCK_ROWS)


def down_rows(router, block):
    weight = router[0:1, rows_of(block)]
    return jnp.broadcast_to(weight, (BLOCK_ROWS, BLOCK_ROWS)).T


def row_minus_column():
    shape = (BLOCK_ROWS, BLOCK_ROWS)
    return lax.broadcasted_iota(jnp.int32, shape, 0) - lax.broadcasted_iota(jnp.int32, shape, 1)


def compiler_params():
    return pltpu.CompilerParams(vmem_limit_bytes=GRANT)


def cost(matmuls, moved):
    return pl.CostEstimate(
        flops=2 * matmuls * HEAD_SIZE**3, bytes_accessed=moved, transcendentals=0
    )


def is_first():
    return lax.axis_index("seq") == 0


def is_last():
    return lax.axis_index("seq") != 0


def always():
    return True


def never():
    return False


def live_of(blocks, n):
    return jnp.bool_(True) if n == 0 else blocks[0, 0, n] > 0


def by_role(query_side, body):
    flag = query_side()
    if isinstance(flag, bool):
        body(flag)
    else:
        pl.when(flag)(lambda: body(True))
        pl.when(jnp.logical_not(flag))(lambda: body(False))


def in_order(query, slots):
    return list(range(slots)) if query else list(reversed(range(slots)))


def weigh(weight, grad):
    return (weight * grad.astype(jnp.float32)).astype(jnp.bfloat16)


def head_loads(pairs, begin, count, sem):
    return [
        pltpu.make_async_copy(source.at[0, :, lanes(begin, count)], target, sem.at[j])
        for j, (source, target) in enumerate(pairs)
    ]


def open_kernel(
    factor, query_side, end, router, blocks, q, k, v, g, chunk,
    router_buf, blocks_buf, x_buf, v_buf, g_buf, acc, small_sem, load_sem,
):
    slots = blocks.shape[2]
    small = [
        pltpu.make_async_copy(blocks, blocks_buf, small_sem.at[0]),
        pltpu.make_async_copy(router, router_buf, small_sem.at[1]),
    ]
    for copy in small:
        copy.start()
    shared = head_loads(((g, g_buf), (v, v_buf)), 0, end, load_sem)
    for load in shared:
        load.start()

    def start(query):
        x = k if query else q
        pltpu.make_async_copy(x.at[0, :, lanes(0, end)], x_buf, load_sem.at[2]).start()

    by_role(query_side, start)
    difference = row_minus_column()
    for copy in small + shared:
        copy.wait()
    pltpu.make_async_copy(k.at[0, :, lanes(0, end)], x_buf, load_sem.at[2]).wait()

    def body(query):
        allowed = difference >= 0 if query else difference <= 0
        order = in_order(query, slots)
        for i, n in enumerate(order):
            live = live_of(blocks_buf, n)
            block = blocks_buf[0, 0, n]
            rows = rows_of(block)
            weight = jnp.where(live, down_rows(router_buf, block), 0.0)
            scale = jnp.where(live, factor, 0.0)
            for h in range(end):
                c_h = weigh(weight, g_buf[rows, lanes(h)])
                v_h = v_buf[rows, lanes(h)]
                l_h, r_h = (c_h, v_h) if query else (v_h, c_h)
                x_h = x_buf[rows, lanes(h)]
                scores = jnp.where(allowed, dot_nt(l_h, r_h), 0.0).astype(jnp.bfloat16)
                if i == 0:
                    out = dot(scores, x_h)
                else:
                    out = dot(
                        jnp.concatenate([scores, l_h], axis=1),
                        jnp.concatenate([x_h, acc[h].astype(jnp.bfloat16)], axis=0),
                    )
                chunk[rows_of(n), lanes(h)] = (scale * out).astype(jnp.bfloat16)
                if i + 1 < slots:
                    added = dot_tn(r_h, x_h)
                    acc[h] = added if i == 0 else acc[h] + added

    by_role(query_side, body)


def opened(factor, query_side, end, small, arrays):
    router, blocks = small
    _, shard_rows, _ = arrays[0].shape
    slots = blocks.shape[2]
    part = pltpu.VMEM((shard_rows, end * HEAD_SIZE), jnp.bfloat16)
    return pl.pallas_call(
        functools.partial(open_kernel, factor, query_side, end),
        name="opened",
        out_shape=pltpu.VMEM((slots * BLOCK_ROWS, end * HEAD_SIZE), jnp.bfloat16),
        in_specs=[HBM] * 6,
        out_specs=VMEM,
        scratch_shapes=[
            pltpu.VMEM(router.shape, router.dtype),
            pltpu.SMEM(blocks.shape, blocks.dtype),
            part, part, part,
            pltpu.VMEM((end, HEAD_SIZE, HEAD_SIZE), jnp.float32),
            pltpu.SemaphoreType.DMA((2,)),
            pltpu.SemaphoreType.DMA((3,)),
        ],
        compiler_params=compiler_params(),
        cost_estimate=cost(4 * slots * end, 6 * shard_rows * end * HEAD_SIZE),
    )(router, blocks, *arrays)


def side_kernel(factor, query_side, begin, seeded, *refs):
    (router, blocks, q, k, v, g), refs = refs[:6], refs[6:]
    if seeded:
        c_all, seed, chunk, states, scores_buf, total = refs
    else:
        sources = (router, blocks, q, k, v, g)
        chunk, states, total, c_all, *targets = refs[:10]
        scores_buf, load_sem = refs[10:]
        router, blocks, q, k, v, g = targets
    slots = blocks.shape[2]
    heads = states.shape[1]
    difference = row_minus_column()

    if not seeded:
        loads = [
            pltpu.make_async_copy(source if j < 2 else source.at[0], target, load_sem.at[j])
            for j, (source, target) in enumerate(zip(sources, targets))
        ]
        for j in (1, 0, 5, 4):
            loads[j].start()

        def start(query):
            for j in (3, 2) if query else (2, 3):
                loads[j].start()

        by_role(query_side, start)
        for j in (1, 0, 5):
            loads[j].wait()

    def body(query):
        allowed = difference >= 0 if query else difference <= 0
        x_all = k if query else q
        order = in_order(query, slots)
        if not seeded:
            for n in order:
                block = blocks[0, 0, n]
                weight = jnp.where(live_of(blocks, n), down_rows(router, block), 0.0)
                for h in range(heads):
                    c_all[rows_of(n), lanes(h)] = weigh(weight, g[rows_of(block), lanes(h)])
            for j in (4, 3 if query else 2):
                loads[j].wait()
        for i, n in enumerate(order):
            live = live_of(blocks, n)
            rows = rows_of(blocks[0, 0, n])
            own = rows_of(n)
            scale = jnp.where(live, factor, 0.0)

            def sides(h):
                c_h, v_h = c_all[own, lanes(h)], v[rows, lanes(h)]
                return (c_h, v_h) if query else (v_h, c_h)

            for h in range(begin, heads):
                l_h, r_h = sides(h)
                scores_buf[n, h] = jnp.where(allowed, dot_nt(l_h, r_h), 0.0).astype(jnp.bfloat16)
            for h in range(heads):
                if i > 0:
                    so_far = total[h]
                elif seeded:
                    so_far = seed[h]
                else:
                    so_far = jnp.zeros((HEAD_SIZE, HEAD_SIZE), jnp.float32)
                states[n, h] = so_far.astype(jnp.bfloat16)
                if not seeded or i + 1 < slots:
                    added = dot_tn(sides(h)[1], x_all[rows, lanes(h)])
                    if query and n > 0:
                        added = jnp.where(live, added, 0.0)
                    total[h] = so_far + added
            for h in range(begin, heads):
                l_h, _ = sides(h)
                x_h = x_all[rows, lanes(h)]
                if i == 0 and not seeded:
                    out = dot(scores_buf[n, h], x_h)
                else:
                    out = dot(
                        jnp.concatenate([scores_buf[n, h], l_h], axis=1),
                        jnp.concatenate([x_h, states[n, h]], axis=0),
                    )
                chunk[own, lanes(h - begin)] = (scale * out).astype(jnp.bfloat16)
        if not seeded:
            loads[2 if query else 3].wait()

    by_role(query_side, body)


def side(factor, query_side, begin, arrays, c_all=None, seed=None):
    router, blocks = arrays[:2]
    shard_rows, width = arrays[2].shape[-2:]
    heads = width // HEAD_SIZE
    slots = blocks.shape[2]
    square = (HEAD_SIZE, HEAD_SIZE)
    total = pltpu.VMEM((heads,) + square, jnp.float32)
    out_shape = [
        pltpu.VMEM((slots * BLOCK_ROWS, (heads - begin) * HEAD_SIZE), jnp.bfloat16),
        pltpu.VMEM((slots, heads) + square, jnp.bfloat16),
    ]
    out_specs = [VMEM] * 2
    scratch = [pltpu.VMEM((slots, heads) + square, jnp.bfloat16)]
    seeded = seed is not None
    if seeded:
        scratch.append(total)
        extra = (c_all, seed)
        in_specs = [VMEM, SMEM] + [VMEM] * 6
    else:
        out_shape += [total, pltpu.VMEM((slots * BLOCK_ROWS, width), jnp.bfloat16)]
        out_shape += [pltpu.VMEM(router.shape, router.dtype), pltpu.SMEM(blocks.shape, blocks.dtype)]
        out_shape += [pltpu.VMEM((shard_rows, width), jnp.bfloat16)] * 4
        out_specs += [VMEM] * 3 + [SMEM] + [VMEM] * 4
        scratch.append(pltpu.SemaphoreType.DMA((6,)))
        extra = ()
        in_specs = [HBM] * 6
    return pl.pallas_call(
        functools.partial(side_kernel, factor, query_side, begin, seeded),
        name="side",
        out_shape=out_shape,
        in_specs=in_specs,
        out_specs=out_specs,
        scratch_shapes=scratch,
        compiler_params=compiler_params(),
        cost_estimate=cost(4 * slots * heads, 0 if seeded else 8 * shard_rows * width),
    )(*arrays, *extra)


def value_kernel(factor, take_one, blocks, q, k, c_all, one, two, chunk, scores_buf):
    slots = blocks.shape[2]
    heads = q.shape[1] // HEAD_SIZE
    allowed = row_minus_column() <= 0

    def body(pick):
        states = one if pick else two
        for n in range(slots):
            rows = rows_of(blocks[0, 0, n])
            own = rows_of(n)
            scale = jnp.where(live_of(blocks, n), factor, 0.0)
            for h in range(heads):
                scores_buf[n, h] = jnp.where(
                    allowed, dot_nt(k[rows, lanes(h)], q[rows, lanes(h)]), 0.0
                ).astype(jnp.bfloat16)
            for h in range(heads):
                out = dot(scores_buf[n, h], c_all[own, lanes(h)])
                out = out + dot_nt(k[rows, lanes(h)], states[n, h])
                chunk[own, lanes(h)] = (scale * out).astype(jnp.bfloat16)

    by_role(take_one, body)


def value_side(factor, take_one, loaded, c_all, one, two):
    _, blocks, q, k, _, _ = loaded
    slots, heads = one.shape[:2]
    return pl.pallas_call(
        functools.partial(value_kernel, factor, take_one),
        name="value_side",
        out_shape=pltpu.VMEM((slots * BLOCK_ROWS, heads * HEAD_SIZE), jnp.bfloat16),
        in_specs=[SMEM] + [VMEM] * 5,
        out_specs=VMEM,
        scratch_shapes=[pltpu.VMEM(one.shape, jnp.bfloat16)],
        compiler_params=compiler_params(),
        cost_estimate=cost(3 * slots * heads, 0),
    )(blocks, q, k, c_all, one, two)


def router_kernel(factor, take_one, blocks, q, k, v, g, one, two, partial, scores_buf):
    slots = blocks.shape[2]
    heads = q.shape[1] // HEAD_SIZE
    allowed = row_minus_column() >= 0

    def body(pick):
        states = one if pick else two
        for n in range(slots):
            rows = rows_of(blocks[0, 0, n])
            for h in range(heads):
                scores_buf[n, h] = jnp.where(
                    allowed, dot_nt(q[rows, lanes(h)], k[rows, lanes(h)]), 0.0
                ).astype(jnp.bfloat16)
            by_row = jnp.zeros((BLOCK_ROWS, HEAD_SIZE), jnp.float32)
            for h in range(heads):
                core = dot(scores_buf[n, h], v[rows, lanes(h)])
                core = factor * (core + dot_nt(q[rows, lanes(h)], states[n, h]))
                by_row = by_row + g[rows, lanes(h)].astype(jnp.float32) * core
            by_row = jnp.where(live_of(blocks, n), by_row, 0.0)
            partial[0:1, rows_of(n)] = jnp.sum(by_row.T, axis=0, keepdims=True)

    by_role(take_one, body)


def router_side(factor, take_one, loaded, one, two):
    _, blocks, *arrays = loaded
    slots = one.shape[0]
    return pl.pallas_call(
        functools.partial(router_kernel, factor, take_one),
        name="router_side",
        out_shape=jax.ShapeDtypeStruct((1, slots * BLOCK_ROWS), jnp.float32),
        in_specs=[SMEM] + [VMEM] * 6,
        out_specs=VMEM,
        scratch_shapes=[pltpu.VMEM(one.shape, jnp.bfloat16)],
        compiler_params=compiler_params(),
        cost_estimate=cost(3 * slots * one.shape[1], 0),
    )(blocks, *arrays, one, two)


def place_kernel(section_of, begin, *refs):
    chunk, out, sem = refs[-3:]
    width = chunk.shape[1] // HEAD_SIZE
    copy = pltpu.make_async_copy(chunk, out.at[0, section_of(), :, lanes(begin, width)], sem)
    copy.start()
    copy.wait()


def place(whole, chunk, shape, section_of, begin):
    rows, width = chunk.shape
    operands = (chunk,) if whole is None else (whole, chunk)
    return pl.pallas_call(
        functools.partial(place_kernel, section_of, begin),
        name="place",
        out_shape=jax.ShapeDtypeStruct(shape, chunk.dtype),
        in_specs=[HBM] * (len(operands) - 1) + [ANY],
        out_specs=HBM,
        scratch_shapes=[pltpu.SemaphoreType.DMA],
        input_output_aliases={} if whole is None else {0: 0},
        compiler_params=pltpu.CompilerParams(vmem_limit_bytes=2**20),
        cost_estimate=cost(0, 4 * rows * width),
    )(*operands)


def shard_states(queries, keys, values, grad_out, router, blocks, counts):
    heads = queries.shape[2] // HEAD_SIZE
    slots = blocks.shape[2]
    shard_blocks = queries.shape[1] // BLOCK_ROWS
    live = jnp.arange(slots, dtype=jnp.int32) < counts[0, 0]
    taken = (blocks[0, 0, :, None] == jnp.arange(shard_blocks, dtype=jnp.int32)) & live[:, None]
    mask = jnp.repeat(jnp.any(taken, axis=0), BLOCK_ROWS)[:, None]

    def rows(array):
        picked = jnp.where(mask, array[0], jnp.zeros((), array.dtype))
        return picked.reshape(-1, heads, HEAD_SIZE)

    weighted = (router[0][:, None, None] * rows(grad_out).astype(jnp.float32)).astype(jnp.bfloat16)
    key_value = jnp.einsum(
        "the,thd->hed", rows(values), rows(keys), preferred_element_type=jnp.float32
    )
    query_grad = jnp.einsum(
        "the,thd->hed", weighted, rows(queries), preferred_element_type=jnp.float32
    )
    return key_value, query_grad


def gathered_gradient(grad_out, router, blocks, counts):
    slots = blocks.shape[2]
    live = jnp.arange(slots, dtype=jnp.int32) < counts[0, 0]
    grouped = grad_out[0].reshape(-1, BLOCK_ROWS, grad_out.shape[2])[blocks[0, 0]]
    weight = jnp.where(live[:, None], router[0].reshape(-1, BLOCK_ROWS)[blocks[0, 0]], 0.0)
    weighted = weight[:, :, None] * grouped.astype(jnp.float32)
    return weighted.astype(jnp.bfloat16).reshape(slots * BLOCK_ROWS, -1)


def own_side():
    return jnp.where(is_first(), 0, 1)


def other_side():
    return jnp.where(is_first(), 1, 0)


def on_device(queries, keys, values, grad_out, router, blocks, counts):
    slots = blocks.shape[2]
    rows = slots * BLOCK_ROWS
    width = queries.shape[2]
    heads = width // HEAD_SIZE
    seq_count = lax.axis_size("seq")
    factor = 1.0 / math.sqrt(HEAD_SIZE * rows * seq_count)
    arrays = (queries, keys, values, grad_out)
    shape = (1, 3, rows, width)
    if seq_count == 2:
        head_start = max(1, heads // 2)
        small = (in_hbm(router), in_hbm(blocks))
        arrays = tuple(in_hbm(x) for x in arrays)

        def sent(x, axis="pipe", by=-1):
            return from_behind(x, axis, by)

        def kernel(call, *operands):
            return call(factor, *operands)

        chunk_a = kernel(opened, is_first, head_start, small, arrays)
        chunk_a = sent(chunk_a)
        chunk_b, own, total, c_all, *loaded = kernel(side, is_first, head_start, small + arrays)
        total = sent(total, "seq", 1)
        chunk_b = sent(chunk_b)
        chunk_c, other = kernel(side, is_last, 0, loaded, c_all, total)
        chunk_c = sent(chunk_c)
        chunk_d = kernel(value_side, is_last, loaded, c_all, own, other)
        chunk_d = sent(chunk_d)
        partial = kernel(router_side, is_first, loaded, own, other)
        handed = place(None, chunk_a, shape, own_side, 0)
        handed = place(handed, chunk_b, shape, own_side, head_start)
        handed = place(handed, chunk_c, shape, other_side, 0)
        handed = place(handed, chunk_d, shape, lambda: 2, 0)
    else:
        index = lax.axis_index("seq")
        places = jnp.arange(seq_count)[:, None, None, None]
        key_value, query_grad = shard_states(queries, keys, values, grad_out, router, blocks, counts)
        gathered = lax.all_gather(key_value, "seq")
        earlier = jnp.sum(jnp.where(places < index, gathered, 0.0), axis=0)
        gathered = lax.all_gather(query_grad, "seq")
        later = jnp.sum(jnp.where(places > index, gathered, 0.0), axis=0)
        loaded = (router, blocks) + tuple(x[0] for x in arrays)
        c_all = gathered_gradient(grad_out, router, blocks, counts)
        d_query, before = side(factor, always, 0, loaded, c_all, earlier)
        d_key, after = side(factor, never, 0, loaded, c_all, later)
        d_value = value_side(factor, always, loaded, c_all, after, after)
        partial = router_side(factor, always, loaded, before, before)
        handed = None
        for section, chunk in enumerate((d_query, d_key, d_value)):
            chunk = from_behind(chunk, "pipe", -1)
            handed = place(handed, chunk, shape, functools.partial(int, section), 0)
    router_grad = lax.psum(partial, "tp")
    return (handed, router_grad)


def solution(mesh):
    return jax.shard_map(
        on_device,
        mesh=mesh,
        in_specs=(
            P("pipe", "seq", "tp"),
            P("pipe", "seq", "tp"),
            P("pipe", "seq", "tp"),
            P("pipe", "seq", "tp"),
            P("pipe", "seq"),
            P("pipe", "seq", None),
            P("pipe", "seq"),
        ),
        out_specs=(P("pipe", None, "seq", "tp"), P("pipe", "seq")),
        check_vma=False,
    )
```

```python
import functools
import itertools
import math

import jax
import jax.numpy as jnp
from jax import lax
from jax.experimental import pallas as pl
from jax.experimental.pallas import tpu as pltpu
from jax.sharding import PartitionSpec as P


HEAD_SIZE = 128
BLOCK_ROWS = 128
GRANT = 16 * 2**20


ANY = pl.BlockSpec(memory_space=pl.ANY)
HBM = pl.BlockSpec(memory_space=pltpu.HBM)
VMEM = pl.BlockSpec(memory_space=pltpu.VMEM)
SMEM = pl.BlockSpec(memory_space=pltpu.SMEM)


def from_behind(x, axis, by):
    count = lax.axis_size(axis)
    return lax.ppermute(x, axis, [(i, (i + by) % count) for i in range(count)])


def in_hbm(x):
    return pltpu.with_memory_space_constraint(x, pltpu.HBM)


def dot(a, b):
    return jnp.dot(a, b, preferred_element_type=jnp.float32)


def dot_nt(a, b):
    return lax.dot_general(a, b, (((1,), (1,)), ((), ())), preferred_element_type=jnp.float32)


def dot_tn(a, b):
    return lax.dot_general(a, b, (((0,), (0,)), ((), ())), preferred_element_type=jnp.float32)


def lanes(h, count=1):
    return pl.ds(h * HEAD_SIZE, count * HEAD_SIZE)


def rows_of(n):
    if isinstance(n, int):
        return pl.ds(n * BLOCK_ROWS, BLOCK_ROWS)
    return pl.ds(pl.multiple_of(n * BLOCK_ROWS, BLOCK_ROWS), BLOCK_ROWS)


def down_rows(router, block):
    weight = router[0:1, rows_of(block)]
    return jnp.broadcast_to(weight, (BLOCK_ROWS, BLOCK_ROWS)).T


def row_minus_column():
    shape = (BLOCK_ROWS, BLOCK_ROWS)
    return lax.broadcasted_iota(jnp.int32, shape, 0) - lax.broadcasted_iota(jnp.int32, shape, 1)


def compiler_params():
    return pltpu.CompilerParams(vmem_limit_bytes=GRANT)


def cost(matmuls, moved):
    return pl.CostEstimate(
        flops=2 * matmuls * HEAD_SIZE**3, bytes_accessed=moved, transcendentals=0
    )


def is_first():
    return lax.axis_index("seq") == 0


def is_last():
    return lax.axis_index("seq") != 0


def always():
    return True


def never():
    return False


def live_of(blocks, n):
    return jnp.bool_(True) if n == 0 else blocks[0, 0, n] > 0


def by_role(query_side, body):
    flag = query_side()
    if isinstance(flag, bool):
        body(flag)
    else:
        pl.when(flag)(lambda: body(True))
        pl.when(jnp.logical_not(flag))(lambda: body(False))


def in_order(query, slots):
    return list(range(slots)) if query else list(reversed(range(slots)))


def weigh(weight, grad):
    return (weight * grad.astype(jnp.float32)).astype(jnp.bfloat16)


def put_rows(chunk, tail, n, columns, rows):
    if tail is not None and n * BLOCK_ROWS == chunk.shape[0]:
        tail[:, columns] = rows
    else:
        chunk[rows_of(n), columns] = rows


def head_loads(pairs, begin, count, sem):
    return [
        pltpu.make_async_copy(source.at[0, :, lanes(begin, count)], target, sem.at[j])
        for j, (source, target) in enumerate(pairs)
    ]


def open_kernel(
    factor, query_side, end, router, blocks, q, k, v, g, chunk, tail,
    router_buf, blocks_buf, x_buf, v_buf, g_buf, c_buf, scores_buf, states_buf, acc,
    small_sem, load_sem,
):
    slots = blocks.shape[2]
    small = [
        pltpu.make_async_copy(blocks, blocks_buf, small_sem.at[0]),
        pltpu.make_async_copy(router, router_buf, small_sem.at[1]),
    ]
    for copy in small:
        copy.start()
    shared = head_loads(((g, g_buf), (v, v_buf)), 0, end, load_sem)
    for load in shared:
        load.start()

    def start(query):
        x = k if query else q
        pltpu.make_async_copy(x.at[0, :, lanes(0, end)], x_buf, load_sem.at[2]).start()

    by_role(query_side, start)
    difference = row_minus_column()
    for copy in small + shared[:1]:
        copy.wait()
    for n in range(slots):
        block = blocks_buf[0, 0, n]
        weight = jnp.where(live_of(blocks_buf, n), down_rows(router_buf, block), 0.0)
        for h in range(end):
            c_buf[rows_of(n), lanes(h)] = weigh(weight, g_buf[rows_of(block), lanes(h)])
    shared[1].wait()
    pltpu.make_async_copy(k.at[0, :, lanes(0, end)], x_buf, load_sem.at[2]).wait()

    def body(query):
        allowed = difference >= 0 if query else difference <= 0
        order = in_order(query, slots)

        def sides(n, h):
            c_h = c_buf[rows_of(n), lanes(h)]
            v_h = v_buf[rows_of(blocks_buf[0, 0, n]), lanes(h)]
            return (c_h, v_h) if query else (v_h, c_h)

        def x_of(n, h):
            return x_buf[rows_of(blocks_buf[0, 0, n]), lanes(h)]

        for n in order:
            for h in range(end):
                l_h, r_h = sides(n, h)
                scores_buf[n, h] = jnp.where(allowed, dot_nt(l_h, r_h), 0.0).astype(jnp.bfloat16)
        for i, n in enumerate(order[:-1]):
            for h in range(end):
                added = dot_tn(sides(n, h)[1], x_of(n, h))
                if i > 0:
                    added = acc[h] + added
                acc[h] = added
                states_buf[order[i + 1], h] = added.astype(jnp.bfloat16)
        for i, n in enumerate(order):
            scale = jnp.where(live_of(blocks_buf, n), factor, 0.0)
            for h in range(end):
                if i == 0:
                    out = dot(scores_buf[n, h], x_of(n, h))
                else:
                    out = dot(
                        jnp.concatenate([scores_buf[n, h], sides(n, h)[0]], axis=1),
                        jnp.concatenate([x_of(n, h), states_buf[n, h]], axis=0),
                    )
                put_rows(chunk, tail, n, lanes(h), (scale * out).astype(jnp.bfloat16))

    by_role(query_side, body)


def split_rows(slots, width):
    return [
        pltpu.VMEM(((slots - 1) * BLOCK_ROWS, width), jnp.bfloat16),
        pltpu.VMEM((BLOCK_ROWS, width), jnp.bfloat16),
    ]


def opened(factor, query_side, end, small, arrays):
    router, blocks = small
    _, shard_rows, _ = arrays[0].shape
    slots = blocks.shape[2]
    part = pltpu.VMEM((shard_rows, end * HEAD_SIZE), jnp.bfloat16)
    return pl.pallas_call(
        functools.partial(open_kernel, factor, query_side, end),
        name="opened",
        out_shape=split_rows(slots, end * HEAD_SIZE),
        in_specs=[HBM] * 6,
        out_specs=[VMEM] * 2,
        scratch_shapes=[
            pltpu.VMEM(router.shape, router.dtype),
            pltpu.SMEM(blocks.shape, blocks.dtype),
            part, part, part,
            pltpu.VMEM((slots * BLOCK_ROWS, end * HEAD_SIZE), jnp.bfloat16),
            pltpu.VMEM((slots, end, HEAD_SIZE, HEAD_SIZE), jnp.bfloat16),
            pltpu.VMEM((slots, end, HEAD_SIZE, HEAD_SIZE), jnp.bfloat16),
            pltpu.VMEM((end, HEAD_SIZE, HEAD_SIZE), jnp.float32),
            pltpu.SemaphoreType.DMA((2,)),
            pltpu.SemaphoreType.DMA((3,)),
        ],
        compiler_params=compiler_params(),
        cost_estimate=cost(4 * slots * end, 6 * shard_rows * end * HEAD_SIZE),
    )(router, blocks, *arrays)


def side_kernel(factor, query_side, begin, seeded, split, *refs):
    (router, blocks, q, k, v, g), refs = refs[:6], refs[6:]
    tail = None
    if seeded and split:
        c_all, seed, chunk, tail, states, info, scores_buf, total = refs
    elif seeded:
        c_all, seed, chunk, states, scores_buf, total = refs
    else:
        sources = (router, blocks, q, k, v, g)
        chunk, tail, states, total, c_all, *targets = refs[:11]
        scores_buf, load_sem = refs[11:]
        router, blocks, q, k, v, g = targets
    slots = blocks.shape[2]
    heads = states.shape[1]
    difference = row_minus_column()

    if not seeded:
        loads = [
            pltpu.make_async_copy(source if j < 2 else source.at[0], target, load_sem.at[j])
            for j, (source, target) in enumerate(zip(sources, targets))
        ]
        for j in (1, 0, 5, 4):
            loads[j].start()

        def start(query):
            for j in (3, 2) if query else (2, 3):
                loads[j].start()

        by_role(query_side, start)
        for j in (1, 0, 5):
            loads[j].wait()

    def body(query):
        allowed = difference >= 0 if query else difference <= 0
        x_all = k if query else q
        order = in_order(query, slots)
        if not seeded:
            for n in order:
                block = blocks[0, 0, n]
                weight = jnp.where(live_of(blocks, n), down_rows(router, block), 0.0)
                for h in range(heads):
                    c_all[rows_of(n), lanes(h)] = weigh(weight, g[rows_of(block), lanes(h)])
            for j in (4, 3 if query else 2):
                loads[j].wait()
        for i, n in enumerate(order):
            live = live_of(blocks, n)
            rows = rows_of(blocks[0, 0, n])
            own = rows_of(n)
            scale = jnp.where(live, factor, 0.0)

            def sides(h):
                c_h, v_h = c_all[own, lanes(h)], v[rows, lanes(h)]
                return (c_h, v_h) if query else (v_h, c_h)

            for h in range(begin, heads):
                l_h, r_h = sides(h)
                scores_buf[n, h] = jnp.where(allowed, dot_nt(l_h, r_h), 0.0).astype(jnp.bfloat16)
            for h in range(heads):
                if i > 0:
                    so_far = total[h]
                elif seeded:
                    so_far = seed[h]
                else:
                    so_far = jnp.zeros((HEAD_SIZE, HEAD_SIZE), jnp.float32)
                states[n, h] = so_far.astype(jnp.bfloat16)
                if not seeded or i + 1 < slots:
                    added = dot_tn(sides(h)[1], x_all[rows, lanes(h)])
                    if query and n > 0:
                        added = jnp.where(live, added, 0.0)
                    total[h] = so_far + added
            for h in range(begin, heads):
                l_h, _ = sides(h)
                x_h = x_all[rows, lanes(h)]
                if i == 0 and not seeded:
                    out = dot(scores_buf[n, h], x_h)
                else:
                    out = dot(
                        jnp.concatenate([scores_buf[n, h], l_h], axis=1),
                        jnp.concatenate([x_h, states[n, h]], axis=0),
                    )
                out = (scale * out).astype(jnp.bfloat16)
                put_rows(chunk, tail, n, lanes(h - begin), out)
        full = jnp.where(live_of(blocks, slots - 1), 1.0, 0.0)
        if not seeded:
            total[heads] = jnp.full((HEAD_SIZE, HEAD_SIZE), full, jnp.float32)
            loads[2 if query else 3].wait()
        elif split:
            other = seed[heads, 0:8, :]
            own_full = jnp.full(other.shape, full, jnp.float32)
            info[...] = jnp.where(own_full + other > 1.5, 2.0, own_full if query else other)

    by_role(query_side, body)


def side(factor, query_side, begin, split, arrays, c_all=None, seed=None):
    router, blocks = arrays[:2]
    shard_rows, width = arrays[2].shape[-2:]
    heads = width // HEAD_SIZE
    slots = blocks.shape[2]
    square = (HEAD_SIZE, HEAD_SIZE)
    out_width = (heads - begin) * HEAD_SIZE
    if split:
        out_shape = split_rows(slots, out_width)
    else:
        out_shape = [pltpu.VMEM((slots * BLOCK_ROWS, out_width), jnp.bfloat16)]
    out_shape.append(pltpu.VMEM((slots, heads) + square, jnp.bfloat16))
    scratch = [pltpu.VMEM((slots, heads) + square, jnp.bfloat16)]
    seeded = seed is not None
    if seeded:
        if split:
            out_shape.append(pltpu.VMEM((8, HEAD_SIZE), jnp.float32))
        out_specs = [VMEM] * len(out_shape)
        scratch.append(pltpu.VMEM((heads,) + square, jnp.float32))
        extra = (c_all, seed)
        in_specs = [VMEM, SMEM] + [VMEM] * 6
    else:
        out_shape.append(pltpu.VMEM((heads + 1,) + square, jnp.float32))
        out_shape.append(pltpu.VMEM((slots * BLOCK_ROWS, width), jnp.bfloat16))
        out_shape += [pltpu.VMEM(router.shape, router.dtype), pltpu.SMEM(blocks.shape, blocks.dtype)]
        out_shape += [pltpu.VMEM((shard_rows, width), jnp.bfloat16)] * 4
        out_specs = [VMEM] * 6 + [SMEM] + [VMEM] * 4
        scratch.append(pltpu.SemaphoreType.DMA((6,)))
        extra = ()
        in_specs = [HBM] * 6
    return pl.pallas_call(
        functools.partial(side_kernel, factor, query_side, begin, seeded, split),
        name="side",
        out_shape=out_shape,
        in_specs=in_specs,
        out_specs=out_specs,
        scratch_shapes=scratch,
        compiler_params=compiler_params(),
        cost_estimate=cost(4 * slots * heads, 0 if seeded else 8 * shard_rows * width),
    )(*arrays, *extra)


def value_kernel(factor, take_one, split, blocks, q, k, c_all, one, two, *refs):
    if split:
        tail_a, tail_b, tail_c, chunk, tails, scores_buf = refs
        tail = tails.at[2]
    else:
        chunk, scores_buf = refs
        tail = None
    slots = blocks.shape[2]
    heads = q.shape[1] // HEAD_SIZE
    allowed = row_minus_column() <= 0

    def body(pick):
        states = one if pick else two
        for n in range(slots):
            rows = rows_of(blocks[0, 0, n])
            own = rows_of(n)
            scale = jnp.where(live_of(blocks, n), factor, 0.0)
            for h in range(heads):
                scores_buf[n, h] = jnp.where(
                    allowed, dot_nt(k[rows, lanes(h)], q[rows, lanes(h)]), 0.0
                ).astype(jnp.bfloat16)
            for h in range(heads):
                out = dot(scores_buf[n, h], c_all[own, lanes(h)])
                out = out + dot_nt(k[rows, lanes(h)], states[n, h])
                put_rows(chunk, tail, n, lanes(h), (scale * out).astype(jnp.bfloat16))
        if split:
            begin = tail_a.shape[1] // HEAD_SIZE
            early, late = (1, 0) if pick else (0, 1)
            tails[early, :, lanes(0, begin)] = tail_a[...]
            tails[early, :, lanes(begin, heads - begin)] = tail_b[...]
            tails[late] = tail_c[...]

    by_role(take_one, body)


def value_side(factor, take_one, loaded, c_all, one, two, tails=()):
    _, blocks, q, k, _, _ = loaded
    slots, heads = one.shape[:2]
    width = heads * HEAD_SIZE
    split = len(tails) > 0
    if split:
        out_shape = [
            split_rows(slots, width)[0], pltpu.VMEM((3, BLOCK_ROWS, width), jnp.bfloat16)
        ]
    else:
        out_shape = [pltpu.VMEM((slots * BLOCK_ROWS, width), jnp.bfloat16)]
    return pl.pallas_call(
        functools.partial(value_kernel, factor, take_one, split),
        name="value_side",
        out_shape=out_shape,
        in_specs=[SMEM] + [VMEM] * (5 + len(tails)),
        out_specs=[VMEM] * len(out_shape),
        scratch_shapes=[pltpu.VMEM(one.shape, jnp.bfloat16)],
        compiler_params=compiler_params(),
        cost_estimate=cost(3 * slots * heads, 0),
    )(blocks, q, k, c_all, one, two, *tails)


def router_kernel(factor, take_one, blocks, q, k, v, g, one, two, partial, scores_buf):
    slots = blocks.shape[2]
    heads = q.shape[1] // HEAD_SIZE
    allowed = row_minus_column() >= 0

    def body(pick):
        states = one if pick else two
        for n in range(slots):
            rows = rows_of(blocks[0, 0, n])
            for h in range(heads):
                scores_buf[n, h] = jnp.where(
                    allowed, dot_nt(q[rows, lanes(h)], k[rows, lanes(h)]), 0.0
                ).astype(jnp.bfloat16)
            by_row = jnp.zeros((BLOCK_ROWS, HEAD_SIZE), jnp.float32)
            for h in range(heads):
                core = dot(scores_buf[n, h], v[rows, lanes(h)])
                core = factor * (core + dot_nt(q[rows, lanes(h)], states[n, h]))
                by_row = by_row + g[rows, lanes(h)].astype(jnp.float32) * core
            by_row = jnp.where(live_of(blocks, n), by_row, 0.0)
            partial[0:1, rows_of(n)] = jnp.sum(by_row.T, axis=0, keepdims=True)

    by_role(take_one, body)


def router_side(factor, take_one, loaded, one, two):
    _, blocks, *arrays = loaded
    slots = one.shape[0]
    return pl.pallas_call(
        functools.partial(router_kernel, factor, take_one),
        name="router_side",
        out_shape=jax.ShapeDtypeStruct((1, slots * BLOCK_ROWS), jnp.float32),
        in_specs=[SMEM] + [VMEM] * 6,
        out_specs=VMEM,
        scratch_shapes=[pltpu.VMEM(one.shape, jnp.bfloat16)],
        compiler_params=compiler_params(),
        cost_estimate=cost(3 * slots * one.shape[1], 0),
    )(blocks, *arrays, one, two)


def place_kernel(section_of, begin, *refs):
    chunk, out, sem = refs[-3:]
    rows, width = chunk.shape
    target = out.at[0, section_of(), pl.ds(0, rows), lanes(begin, width // HEAD_SIZE)]
    copy = pltpu.make_async_copy(chunk, target, sem)
    copy.start()
    copy.wait()


def place_tail_kernel(whole, tails, out, sem):
    del whole
    rows = out.shape[2] - tails.shape[1]
    copy = pltpu.make_async_copy(tails, out.at[0, :, pl.ds(rows, tails.shape[1])], sem)
    copy.start()
    copy.wait()


def put(body, whole, chunk, shape):
    operands = (chunk,) if whole is None else (whole, chunk)
    return pl.pallas_call(
        body,
        name="place",
        out_shape=pltpu.HBM(shape, chunk.dtype),
        in_specs=[HBM] * (len(operands) - 1) + [ANY],
        out_specs=HBM,
        scratch_shapes=[pltpu.SemaphoreType.DMA],
        input_output_aliases={} if whole is None else {0: 0},
        compiler_params=pltpu.CompilerParams(vmem_limit_bytes=2**20),
        cost_estimate=cost(0, 4 * chunk.size),
    )(*operands)


def place(whole, chunk, shape, section_of, begin):
    return put(functools.partial(place_kernel, section_of, begin), whole, chunk, shape)


def pick_kernel(*refs):
    infos, out = refs[:-1], refs[-1]
    count = len(infos)
    here = lax.axis_index("pipe")
    both = jnp.bool_(False)
    choice = jnp.int32(0)
    for k, info in enumerate(infos):
        code = jnp.max(info[...])
        section = lax.rem(here + k, count)
        weight = jnp.left_shift(jnp.int32(1), count - 1 - section)
        both = jnp.logical_or(both, code > 1.5)
        choice = choice + jnp.where(code > 0.5, weight, 0)
    out[0, 0] = jnp.where(both, 0, 1 + choice)


def pick(infos):
    return pl.pallas_call(
        pick_kernel,
        name="pick",
        out_shape=pltpu.SMEM((1, 1), jnp.int32),
        in_specs=[VMEM] * len(infos),
        out_specs=SMEM,
        compiler_params=pltpu.CompilerParams(vmem_limit_bytes=2**20),
    )(*infos)


def third_pairs(pipe_count):
    def pair(s, p):
        return (s * pipe_count + p, s * pipe_count + (p - 1) % pipe_count)

    every = [pair(s, p) for s in (0, 1) for p in range(pipe_count)]
    return [every] + [
        [pair(s, p) for p, s in enumerate(cores)]
        for cores in itertools.product((0, 1), repeat=pipe_count)
    ]


def folded(parts):
    while len(parts) > 1:
        half = len(parts) // 2
        parts = [parts[k] + parts[k + half] for k in range(half)]
    return parts[0]


def shard_states(queries, keys, values, grad_out, router, blocks, counts):
    heads = queries.shape[2] // HEAD_SIZE
    slots = blocks.shape[2]
    shard_blocks = queries.shape[1] // BLOCK_ROWS
    live = jnp.arange(slots, dtype=jnp.int32) < counts[0, 0]
    taken = (blocks[0, 0, :, None] == jnp.arange(shard_blocks, dtype=jnp.int32)) & live[:, None]
    mask = jnp.repeat(jnp.any(taken, axis=0), BLOCK_ROWS)[:, None]

    def rows(array):
        picked = jnp.where(mask, array[0], jnp.zeros((), array.dtype))
        return picked.reshape(-1, heads, HEAD_SIZE)

    weighted = (router[0][:, None, None] * rows(grad_out).astype(jnp.float32)).astype(jnp.bfloat16)
    key_value = jnp.einsum(
        "the,thd->hed", rows(values), rows(keys), preferred_element_type=jnp.float32
    )
    query_grad = jnp.einsum(
        "the,thd->hed", weighted, rows(queries), preferred_element_type=jnp.float32
    )
    return key_value, query_grad


def gathered_gradient(grad_out, router, blocks, counts):
    slots = blocks.shape[2]
    live = jnp.arange(slots, dtype=jnp.int32) < counts[0, 0]
    grouped = grad_out[0].reshape(-1, BLOCK_ROWS, grad_out.shape[2])[blocks[0, 0]]
    weight = jnp.where(live[:, None], router[0].reshape(-1, BLOCK_ROWS)[blocks[0, 0]], 0.0)
    weighted = weight[:, :, None] * grouped.astype(jnp.float32)
    return weighted.astype(jnp.bfloat16).reshape(slots * BLOCK_ROWS, -1)


def fits(seq_count, pipe_count, tp_count, slots):
    return seq_count == 2 and pipe_count <= 4 and tp_count in (1, 2, 4, 8) and slots > 1


def own_side():
    return jnp.where(is_first(), 0, 1)


def other_side():
    return jnp.where(is_first(), 1, 0)


def on_device(queries, keys, values, grad_out, router, blocks, counts):
    slots = blocks.shape[2]
    rows = slots * BLOCK_ROWS
    width = queries.shape[2]
    heads = width // HEAD_SIZE
    seq_count, pipe_count, tp_count = (lax.axis_size(axis) for axis in ("seq", "pipe", "tp"))
    factor = 1.0 / math.sqrt(HEAD_SIZE * rows * seq_count)
    arrays = (queries, keys, values, grad_out)
    shape = (1, 3, rows, width)
    if fits(seq_count, pipe_count, tp_count, slots):
        head_start = max(1, 2 * heads // 3)
        small = (in_hbm(router), in_hbm(blocks))
        arrays = tuple(in_hbm(x) for x in arrays)

        def sent(x, axis="pipe", by=-1):
            return from_behind(x, axis, by)

        def kernel(call, *operands):
            return call(factor, *operands)

        chunk_a, tail_a = kernel(opened, is_first, head_start, small, arrays)
        chunk_a = sent(chunk_a)
        chunk_b, tail_b, own, total, c_all, *loaded = kernel(
            side, is_first, head_start, True, small + arrays
        )
        total = sent(total, "seq", 1)
        chunk_b = sent(chunk_b)
        chunk_c, tail_c, other, info = kernel(side, is_last, 0, True, loaded, c_all, total)
        chunk_c = sent(chunk_c)
        infos = [info] + [sent(info, "pipe", -k) for k in range(1, pipe_count)]
        chunk_d, tails = kernel(
            value_side, is_last, loaded, c_all, own, other, (tail_a, tail_b, tail_c)
        )
        chunk_d = sent(chunk_d)
        partial = kernel(router_side, is_first, loaded, own, other)
        parts = [partial] + [sent(partial, "tp", -k) for k in range(1, tp_count)]
        router_grad = folded(parts)
        handed = place(None, chunk_a, shape, own_side, 0)
        handed = place(handed, chunk_b, shape, own_side, head_start)
        handed = place(handed, chunk_c, shape, other_side, 0)
        choice = pick(infos)[0, 0]

        def third(pairs, whole, x):
            return put(place_tail_kernel, whole, lax.ppermute(x, ("seq", "pipe"), pairs), shape)

        branches = [functools.partial(third, pairs) for pairs in third_pairs(pipe_count)]
        handed = lax.switch(choice, branches, handed, tails)
        handed = place(handed, chunk_d, shape, lambda: 2, 0)
    else:
        index = lax.axis_index("seq")
        places = jnp.arange(seq_count)[:, None, None, None]
        key_value, query_grad = shard_states(queries, keys, values, grad_out, router, blocks, counts)
        gathered = lax.all_gather(key_value, "seq")
        earlier = jnp.sum(jnp.where(places < index, gathered, 0.0), axis=0)
        gathered = lax.all_gather(query_grad, "seq")
        later = jnp.sum(jnp.where(places > index, gathered, 0.0), axis=0)
        loaded = (router, blocks) + tuple(x[0] for x in arrays)
        c_all = gathered_gradient(grad_out, router, blocks, counts)
        d_query, before = side(factor, always, 0, False, loaded, c_all, earlier)
        d_key, after = side(factor, never, 0, False, loaded, c_all, later)
        (d_value,) = value_side(factor, always, loaded, c_all, after, after)
        partial = router_side(factor, always, loaded, before, before)
        handed = None
        for section, chunk in enumerate((d_query, d_key, d_value)):
            chunk = from_behind(chunk, "pipe", -1)
            handed = place(handed, chunk, shape, functools.partial(int, section), 0)
        router_grad = lax.psum(partial, "tp")
    return (handed, router_grad)


def solution(mesh):
    return jax.shard_map(
        on_device,
        mesh=mesh,
        in_specs=(
            P("pipe", "seq", "tp"),
            P("pipe", "seq", "tp"),
            P("pipe", "seq", "tp"),
            P("pipe", "seq", "tp"),
            P("pipe", "seq"),
            P("pipe", "seq", None),
            P("pipe", "seq"),
        ),
        out_specs=(P("pipe", None, "seq", "tp"), P("pipe", "seq")),
        check_vma=False,
    )
```

```python
import functools
import itertools
import math

import jax
import jax.numpy as jnp
from jax import lax
from jax.experimental import pallas as pl
from jax.experimental.pallas import tpu as pltpu
from jax.sharding import PartitionSpec as P


HEAD_SIZE = 128
BLOCK_ROWS = 128
GRANT = 16 * 2**20


ANY = pl.BlockSpec(memory_space=pl.ANY)
HBM = pl.BlockSpec(memory_space=pltpu.HBM)
VMEM = pl.BlockSpec(memory_space=pltpu.VMEM)
SMEM = pl.BlockSpec(memory_space=pltpu.SMEM)


def from_behind(x, axis, by):
    count = lax.axis_size(axis)
    return lax.ppermute(x, axis, [(i, (i + by) % count) for i in range(count)])


def in_hbm(x):
    return pltpu.with_memory_space_constraint(x, pltpu.HBM)


def dot(a, b):
    return jnp.dot(a, b, preferred_element_type=jnp.float32)


def dot_nt(a, b):
    return lax.dot_general(a, b, (((1,), (1,)), ((), ())), preferred_element_type=jnp.float32)


def dot_tn(a, b):
    return lax.dot_general(a, b, (((0,), (0,)), ((), ())), preferred_element_type=jnp.float32)


def lanes(h, count=1):
    return pl.ds(h * HEAD_SIZE, count * HEAD_SIZE)


def rows_of(n):
    if isinstance(n, int):
        return pl.ds(n * BLOCK_ROWS, BLOCK_ROWS)
    return pl.ds(pl.multiple_of(n * BLOCK_ROWS, BLOCK_ROWS), BLOCK_ROWS)


def down_rows(router, block):
    weight = router[0:1, rows_of(block)]
    return jnp.broadcast_to(weight, (BLOCK_ROWS, BLOCK_ROWS)).T


def row_minus_column():
    shape = (BLOCK_ROWS, BLOCK_ROWS)
    return lax.broadcasted_iota(jnp.int32, shape, 0) - lax.broadcasted_iota(jnp.int32, shape, 1)


def compiler_params():
    return pltpu.CompilerParams(vmem_limit_bytes=GRANT)


def cost(matmuls, moved):
    return pl.CostEstimate(
        flops=2 * matmuls * HEAD_SIZE**3, bytes_accessed=moved, transcendentals=0
    )


def is_first():
    return lax.axis_index("seq") == 0


def is_last():
    return lax.axis_index("seq") != 0


def always():
    return True


def never():
    return False


def live_of(blocks, n):
    return jnp.bool_(True) if n == 0 else blocks[0, 0, n] > 0


def by_role(query_side, body):
    flag = query_side()
    if isinstance(flag, bool):
        body(flag)
    else:
        pl.when(flag)(lambda: body(True))
        pl.when(jnp.logical_not(flag))(lambda: body(False))


def in_order(query, slots):
    return list(range(slots)) if query else list(reversed(range(slots)))


def weigh(weight, grad):
    return (weight * grad.astype(jnp.float32)).astype(jnp.bfloat16)


def put_rows(chunk, tail, n, columns, rows):
    if tail is not None and n * BLOCK_ROWS == chunk.shape[0]:
        tail[:, columns] = rows
    else:
        chunk[rows_of(n), columns] = rows


def head_loads(pairs, begin, count, sem):
    return [
        pltpu.make_async_copy(source.at[0, :, lanes(begin, count)], target, sem.at[j])
        for j, (source, target) in enumerate(pairs)
    ]


def open_kernel(
    factor, query_side, end, router, blocks, q, k, v, g, chunk, tail,
    router_buf, blocks_buf, x_buf, v_buf, g_buf, c_buf, scores_buf, states_buf, acc,
    small_sem, load_sem,
):
    slots = blocks.shape[2]
    small = [
        pltpu.make_async_copy(blocks, blocks_buf, small_sem.at[0]),
        pltpu.make_async_copy(router, router_buf, small_sem.at[1]),
    ]
    for copy in small:
        copy.start()
    shared = head_loads(((g, g_buf), (v, v_buf)), 0, end, load_sem)
    for load in shared:
        load.start()

    def start(query):
        x = k if query else q
        pltpu.make_async_copy(x.at[0, :, lanes(0, end)], x_buf, load_sem.at[2]).start()

    by_role(query_side, start)
    difference = row_minus_column()
    for copy in small + shared[:1]:
        copy.wait()
    for n in range(slots):
        block = blocks_buf[0, 0, n]
        weight = jnp.where(live_of(blocks_buf, n), down_rows(router_buf, block), 0.0)
        for h in range(end):
            c_buf[rows_of(n), lanes(h)] = weigh(weight, g_buf[rows_of(block), lanes(h)])
    shared[1].wait()
    pltpu.make_async_copy(k.at[0, :, lanes(0, end)], x_buf, load_sem.at[2]).wait()

    def body(query):
        allowed = difference >= 0 if query else difference <= 0
        order = in_order(query, slots)

        def sides(n, h):
            c_h = c_buf[rows_of(n), lanes(h)]
            v_h = v_buf[rows_of(blocks_buf[0, 0, n]), lanes(h)]
            return (c_h, v_h) if query else (v_h, c_h)

        def x_of(n, h):
            return x_buf[rows_of(blocks_buf[0, 0, n]), lanes(h)]

        for n in order:
            for h in range(end):
                l_h, r_h = sides(n, h)
                scores_buf[n, h] = jnp.where(allowed, dot_nt(l_h, r_h), 0.0).astype(jnp.bfloat16)
        for i, n in enumerate(order[:-1]):
            for h in range(end):
                added = dot_tn(sides(n, h)[1], x_of(n, h))
                if i > 0:
                    added = acc[h] + added
                acc[h] = added
                states_buf[order[i + 1], h] = added.astype(jnp.bfloat16)
        for i, n in enumerate(order):
            scale = jnp.where(live_of(blocks_buf, n), factor, 0.0)
            for h in range(end):
                if i == 0:
                    out = dot(scores_buf[n, h], x_of(n, h))
                else:
                    out = dot(
                        jnp.concatenate([scores_buf[n, h], sides(n, h)[0]], axis=1),
                        jnp.concatenate([x_of(n, h), states_buf[n, h]], axis=0),
                    )
                put_rows(chunk, tail, n, lanes(h), (scale * out).astype(jnp.bfloat16))

    by_role(query_side, body)


def split_rows(slots, width):
    return [
        pltpu.VMEM(((slots - 1) * BLOCK_ROWS, width), jnp.bfloat16),
        pltpu.VMEM((BLOCK_ROWS, width), jnp.bfloat16),
    ]


def opened(factor, query_side, end, small, arrays):
    router, blocks = small
    _, shard_rows, _ = arrays[0].shape
    slots = blocks.shape[2]
    part = pltpu.VMEM((shard_rows, end * HEAD_SIZE), jnp.bfloat16)
    return pl.pallas_call(
        functools.partial(open_kernel, factor, query_side, end),
        name="opened",
        out_shape=split_rows(slots, end * HEAD_SIZE),
        in_specs=[HBM] * 6,
        out_specs=[VMEM] * 2,
        scratch_shapes=[
            pltpu.VMEM(router.shape, router.dtype),
            pltpu.SMEM(blocks.shape, blocks.dtype),
            part, part, part,
            pltpu.VMEM((slots * BLOCK_ROWS, end * HEAD_SIZE), jnp.bfloat16),
            pltpu.VMEM((slots, end, HEAD_SIZE, HEAD_SIZE), jnp.bfloat16),
            pltpu.VMEM((slots, end, HEAD_SIZE, HEAD_SIZE), jnp.bfloat16),
            pltpu.VMEM((end, HEAD_SIZE, HEAD_SIZE), jnp.float32),
            pltpu.SemaphoreType.DMA((2,)),
            pltpu.SemaphoreType.DMA((3,)),
        ],
        compiler_params=compiler_params(),
        cost_estimate=cost(4 * slots * end, 6 * shard_rows * end * HEAD_SIZE),
    )(router, blocks, *arrays)


def side_kernel(factor, query_side, begin, seeded, split, *refs):
    (router, blocks, q, k, v, g), refs = refs[:6], refs[6:]
    tail = None
    if seeded and split:
        c_all, seed, chunk, tail, states, info, scores_buf, total = refs
    elif seeded:
        c_all, seed, chunk, states, scores_buf, total = refs
    else:
        sources = (router, blocks, q, k, v, g)
        chunk, tail, states, total, c_all, *targets = refs[:11]
        scores_buf, load_sem = refs[11:]
        router, blocks, q, k, v, g = targets
    slots = blocks.shape[2]
    heads = states.shape[1]
    difference = row_minus_column()

    if not seeded:
        loads = [
            pltpu.make_async_copy(source if j < 2 else source.at[0], target, load_sem.at[j])
            for j, (source, target) in enumerate(zip(sources, targets))
        ]
        for j in (1, 0, 5, 4):
            loads[j].start()

        def start(query):
            for j in (3, 2) if query else (2, 3):
                loads[j].start()

        by_role(query_side, start)
        for j in (1, 0, 5):
            loads[j].wait()

    def body(query):
        allowed = difference >= 0 if query else difference <= 0
        x_all = k if query else q
        order = in_order(query, slots)
        if not seeded:
            for n in order:
                block = blocks[0, 0, n]
                weight = jnp.where(live_of(blocks, n), down_rows(router, block), 0.0)
                for h in range(heads):
                    c_all[rows_of(n), lanes(h)] = weigh(weight, g[rows_of(block), lanes(h)])
            for j in (4, 3 if query else 2):
                loads[j].wait()
        for i, n in enumerate(order):
            live = live_of(blocks, n)
            rows = rows_of(blocks[0, 0, n])
            own = rows_of(n)
            scale = jnp.where(live, factor, 0.0)

            def sides(h):
                c_h, v_h = c_all[own, lanes(h)], v[rows, lanes(h)]
                return (c_h, v_h) if query else (v_h, c_h)

            for h in range(begin, heads):
                l_h, r_h = sides(h)
                scores_buf[n, h] = jnp.where(allowed, dot_nt(l_h, r_h), 0.0).astype(jnp.bfloat16)
            for h in range(heads):
                if i > 0:
                    so_far = total[h]
                elif seeded:
                    so_far = seed[h]
                else:
                    so_far = jnp.zeros((HEAD_SIZE, HEAD_SIZE), jnp.float32)
                states[n, h] = so_far.astype(jnp.bfloat16)
                if not seeded or i + 1 < slots:
                    added = dot_tn(sides(h)[1], x_all[rows, lanes(h)])
                    if query and n > 0:
                        added = jnp.where(live, added, 0.0)
                    total[h] = so_far + added
            for h in range(begin, heads):
                l_h, _ = sides(h)
                x_h = x_all[rows, lanes(h)]
                if i == 0 and not seeded:
                    out = dot(scores_buf[n, h], x_h)
                else:
                    out = dot(
                        jnp.concatenate([scores_buf[n, h], l_h], axis=1),
                        jnp.concatenate([x_h, states[n, h]], axis=0),
                    )
                out = (scale * out).astype(jnp.bfloat16)
                put_rows(chunk, tail, n, lanes(h - begin), out)
        full = jnp.where(live_of(blocks, slots - 1), 1.0, 0.0)
        if not seeded:
            total[heads] = jnp.full((HEAD_SIZE, HEAD_SIZE), full, jnp.float32)
            loads[2 if query else 3].wait()
        elif split:
            other = seed[heads, 0:8, :]
            own_full = jnp.full(other.shape, full, jnp.float32)
            info[...] = jnp.where(own_full + other > 1.5, 2.0, own_full if query else other)

    by_role(query_side, body)


def side(factor, query_side, begin, split, arrays, c_all=None, seed=None):
    router, blocks = arrays[:2]
    shard_rows, width = arrays[2].shape[-2:]
    heads = width // HEAD_SIZE
    slots = blocks.shape[2]
    square = (HEAD_SIZE, HEAD_SIZE)
    out_width = (heads - begin) * HEAD_SIZE
    if split:
        out_shape = split_rows(slots, out_width)
    else:
        out_shape = [pltpu.VMEM((slots * BLOCK_ROWS, out_width), jnp.bfloat16)]
    out_shape.append(pltpu.VMEM((slots, heads) + square, jnp.bfloat16))
    scratch = [pltpu.VMEM((slots, heads) + square, jnp.bfloat16)]
    seeded = seed is not None
    if seeded:
        if split:
            out_shape.append(pltpu.VMEM((8, HEAD_SIZE), jnp.float32))
        out_specs = [VMEM] * len(out_shape)
        scratch.append(pltpu.VMEM((heads,) + square, jnp.float32))
        extra = (c_all, seed)
        in_specs = [VMEM, SMEM] + [VMEM] * 6
    else:
        out_shape.append(pltpu.VMEM((heads + 1,) + square, jnp.float32))
        out_shape.append(pltpu.VMEM((slots * BLOCK_ROWS, width), jnp.bfloat16))
        out_shape += [pltpu.VMEM(router.shape, router.dtype), pltpu.SMEM(blocks.shape, blocks.dtype)]
        out_shape += [pltpu.VMEM((shard_rows, width), jnp.bfloat16)] * 4
        out_specs = [VMEM] * 6 + [SMEM] + [VMEM] * 4
        scratch.append(pltpu.SemaphoreType.DMA((6,)))
        extra = ()
        in_specs = [HBM] * 6
    return pl.pallas_call(
        functools.partial(side_kernel, factor, query_side, begin, seeded, split),
        name="side",
        out_shape=out_shape,
        in_specs=in_specs,
        out_specs=out_specs,
        scratch_shapes=scratch,
        compiler_params=compiler_params(),
        cost_estimate=cost(4 * slots * heads, 0 if seeded else 8 * shard_rows * width),
    )(*arrays, *extra)


def value_kernel(factor, take_one, split, blocks, q, k, c_all, one, two, *refs):
    if split:
        tail_a, tail_b, tail_c, chunk, tails, scores_buf = refs
        tail = tails.at[2]
    else:
        chunk, scores_buf = refs
        tail = None
    slots = blocks.shape[2]
    heads = q.shape[1] // HEAD_SIZE
    allowed = row_minus_column() <= 0

    def body(pick):
        states = one if pick else two
        for n in range(slots):
            rows = rows_of(blocks[0, 0, n])
            own = rows_of(n)
            scale = jnp.where(live_of(blocks, n), factor, 0.0)
            for h in range(heads):
                scores_buf[n, h] = jnp.where(
                    allowed, dot_nt(k[rows, lanes(h)], q[rows, lanes(h)]), 0.0
                ).astype(jnp.bfloat16)
            for h in range(heads):
                out = dot(scores_buf[n, h], c_all[own, lanes(h)])
                out = out + dot_nt(k[rows, lanes(h)], states[n, h])
                put_rows(chunk, tail, n, lanes(h), (scale * out).astype(jnp.bfloat16))
        if split:
            begin = tail_a.shape[1] // HEAD_SIZE
            early, late = (1, 0) if pick else (0, 1)
            tails[early, :, lanes(0, begin)] = tail_a[...]
            tails[early, :, lanes(begin, heads - begin)] = tail_b[...]
            tails[late] = tail_c[...]

    by_role(take_one, body)


def value_side(factor, take_one, loaded, c_all, one, two, tails=()):
    _, blocks, q, k, _, _ = loaded
    slots, heads = one.shape[:2]
    width = heads * HEAD_SIZE
    split = len(tails) > 0
    if split:
        out_shape = [
            split_rows(slots, width)[0], pltpu.VMEM((3, BLOCK_ROWS, width), jnp.bfloat16)
        ]
    else:
        out_shape = [pltpu.VMEM((slots * BLOCK_ROWS, width), jnp.bfloat16)]
    return pl.pallas_call(
        functools.partial(value_kernel, factor, take_one, split),
        name="value_side",
        out_shape=out_shape,
        in_specs=[SMEM] + [VMEM] * (5 + len(tails)),
        out_specs=[VMEM] * len(out_shape),
        scratch_shapes=[pltpu.VMEM(one.shape, jnp.bfloat16)],
        compiler_params=compiler_params(),
        cost_estimate=cost(3 * slots * heads, 0),
    )(blocks, q, k, c_all, one, two, *tails)


def router_kernel(factor, take_one, blocks, q, k, v, g, one, two, partial, scores_buf):
    slots = blocks.shape[2]
    heads = q.shape[1] // HEAD_SIZE
    allowed = row_minus_column() >= 0

    def body(pick):
        states = one if pick else two
        for n in range(slots):
            rows = rows_of(blocks[0, 0, n])
            for h in range(heads):
                scores_buf[n, h] = jnp.where(
                    allowed, dot_nt(q[rows, lanes(h)], k[rows, lanes(h)]), 0.0
                ).astype(jnp.bfloat16)
            by_row = jnp.zeros((BLOCK_ROWS, HEAD_SIZE), jnp.float32)
            for h in range(heads):
                core = dot(scores_buf[n, h], v[rows, lanes(h)])
                core = factor * (core + dot_nt(q[rows, lanes(h)], states[n, h]))
                by_row = by_row + g[rows, lanes(h)].astype(jnp.float32) * core
            by_row = jnp.where(live_of(blocks, n), by_row, 0.0)
            partial[0:1, rows_of(n)] = jnp.sum(by_row.T, axis=0, keepdims=True)

    by_role(take_one, body)


def router_side(factor, take_one, loaded, one, two):
    _, blocks, *arrays = loaded
    slots = one.shape[0]
    return pl.pallas_call(
        functools.partial(router_kernel, factor, take_one),
        name="router_side",
        out_shape=jax.ShapeDtypeStruct((1, slots * BLOCK_ROWS), jnp.float32),
        in_specs=[SMEM] + [VMEM] * 6,
        out_specs=VMEM,
        scratch_shapes=[pltpu.VMEM(one.shape, jnp.bfloat16)],
        compiler_params=compiler_params(),
        cost_estimate=cost(3 * slots * one.shape[1], 0),
    )(blocks, *arrays, one, two)


def place_kernel(section_of, begin, *refs):
    chunk, out, sem = refs[-3:]
    rows, width = chunk.shape
    target = out.at[0, section_of(), pl.ds(0, rows), lanes(begin, width // HEAD_SIZE)]
    copy = pltpu.make_async_copy(chunk, target, sem)
    copy.start()
    copy.wait()


def place_tail_kernel(whole, tails, out, sem):
    del whole
    rows = out.shape[2] - tails.shape[1]
    copy = pltpu.make_async_copy(tails, out.at[0, :, pl.ds(rows, tails.shape[1])], sem)
    copy.start()
    copy.wait()


def finish_kernel(section, whole, chunk, *refs):
    del whole
    parts, (out, total, sem) = refs[:-3], refs[-3:]
    copy = pltpu.make_async_copy(chunk, out.at[0, section, pl.ds(0, chunk.shape[0])], sem)
    copy.start()
    total[...] = folded([part[...] for part in parts])
    copy.wait()


def finish(section, whole, chunk, parts):
    return pl.pallas_call(
        functools.partial(finish_kernel, section),
        name="finish",
        out_shape=[
            pltpu.HBM(whole.shape, whole.dtype),
            jax.ShapeDtypeStruct(parts[0].shape, parts[0].dtype),
        ],
        in_specs=[HBM, ANY] + [VMEM] * len(parts),
        out_specs=[HBM, VMEM],
        scratch_shapes=[pltpu.SemaphoreType.DMA],
        input_output_aliases={0: 0},
        compiler_params=pltpu.CompilerParams(vmem_limit_bytes=2**20),
        cost_estimate=cost(0, 4 * chunk.size),
    )(whole, chunk, *parts)


def put(body, whole, chunk, shape):
    operands = (chunk,) if whole is None else (whole, chunk)
    return pl.pallas_call(
        body,
        name="place",
        out_shape=pltpu.HBM(shape, chunk.dtype),
        in_specs=[HBM] * (len(operands) - 1) + [ANY],
        out_specs=HBM,
        scratch_shapes=[pltpu.SemaphoreType.DMA],
        input_output_aliases={} if whole is None else {0: 0},
        compiler_params=pltpu.CompilerParams(vmem_limit_bytes=2**20),
        cost_estimate=cost(0, 4 * chunk.size),
    )(*operands)


def place(whole, chunk, shape, section_of, begin):
    return put(functools.partial(place_kernel, section_of, begin), whole, chunk, shape)


def pick_kernel(*refs):
    infos, out = refs[:-1], refs[-1]
    count = len(infos)
    here = lax.axis_index("pipe")
    both = jnp.bool_(False)
    choice = jnp.int32(0)
    for k, info in enumerate(infos):
        code = jnp.max(info[...])
        section = lax.rem(here + k, count)
        weight = jnp.left_shift(jnp.int32(1), count - 1 - section)
        both = jnp.logical_or(both, code > 1.5)
        choice = choice + jnp.where(code > 0.5, weight, 0)
    out[0, 0] = jnp.where(both, 0, 1 + choice)


def pick(infos):
    return pl.pallas_call(
        pick_kernel,
        name="pick",
        out_shape=pltpu.SMEM((1, 1), jnp.int32),
        in_specs=[VMEM] * len(infos),
        out_specs=SMEM,
        compiler_params=pltpu.CompilerParams(vmem_limit_bytes=2**20),
    )(*infos)


def third_pairs(pipe_count):
    def pair(s, p):
        return (s * pipe_count + p, s * pipe_count + (p - 1) % pipe_count)

    every = [pair(s, p) for s in (0, 1) for p in range(pipe_count)]
    return [every] + [
        [pair(s, p) for p, s in enumerate(cores)]
        for cores in itertools.product((0, 1), repeat=pipe_count)
    ]


def folded(parts):
    while len(parts) > 1:
        half = len(parts) // 2
        parts = [parts[k] + parts[k + half] for k in range(half)]
    return parts[0]


def shard_states(queries, keys, values, grad_out, router, blocks, counts):
    heads = queries.shape[2] // HEAD_SIZE
    slots = blocks.shape[2]
    shard_blocks = queries.shape[1] // BLOCK_ROWS
    live = jnp.arange(slots, dtype=jnp.int32) < counts[0, 0]
    taken = (blocks[0, 0, :, None] == jnp.arange(shard_blocks, dtype=jnp.int32)) & live[:, None]
    mask = jnp.repeat(jnp.any(taken, axis=0), BLOCK_ROWS)[:, None]

    def rows(array):
        picked = jnp.where(mask, array[0], jnp.zeros((), array.dtype))
        return picked.reshape(-1, heads, HEAD_SIZE)

    weighted = (router[0][:, None, None] * rows(grad_out).astype(jnp.float32)).astype(jnp.bfloat16)
    key_value = jnp.einsum(
        "the,thd->hed", rows(values), rows(keys), preferred_element_type=jnp.float32
    )
    query_grad = jnp.einsum(
        "the,thd->hed", weighted, rows(queries), preferred_element_type=jnp.float32
    )
    return key_value, query_grad


def gathered_gradient(grad_out, router, blocks, counts):
    slots = blocks.shape[2]
    live = jnp.arange(slots, dtype=jnp.int32) < counts[0, 0]
    grouped = grad_out[0].reshape(-1, BLOCK_ROWS, grad_out.shape[2])[blocks[0, 0]]
    weight = jnp.where(live[:, None], router[0].reshape(-1, BLOCK_ROWS)[blocks[0, 0]], 0.0)
    weighted = weight[:, :, None] * grouped.astype(jnp.float32)
    return weighted.astype(jnp.bfloat16).reshape(slots * BLOCK_ROWS, -1)


def fits(seq_count, pipe_count, tp_count, slots):
    return seq_count == 2 and pipe_count <= 4 and tp_count in (1, 2, 4, 8) and slots > 1


def own_side():
    return jnp.where(is_first(), 0, 1)


def other_side():
    return jnp.where(is_first(), 1, 0)


def on_device(queries, keys, values, grad_out, router, blocks, counts):
    slots = blocks.shape[2]
    rows = slots * BLOCK_ROWS
    width = queries.shape[2]
    heads = width // HEAD_SIZE
    seq_count, pipe_count, tp_count = (lax.axis_size(axis) for axis in ("seq", "pipe", "tp"))
    factor = 1.0 / math.sqrt(HEAD_SIZE * rows * seq_count)
    arrays = (queries, keys, values, grad_out)
    shape = (1, 3, rows, width)
    if fits(seq_count, pipe_count, tp_count, slots):
        head_start = max(1, 2 * heads // 3)
        small = (in_hbm(router), in_hbm(blocks))
        arrays = tuple(in_hbm(x) for x in arrays)

        def sent(x, axis="pipe", by=-1):
            return from_behind(x, axis, by)

        def kernel(call, *operands):
            return call(factor, *operands)

        chunk_a, tail_a = kernel(opened, is_first, head_start, small, arrays)
        chunk_a = sent(chunk_a)
        chunk_b, tail_b, own, total, c_all, *loaded = kernel(
            side, is_first, head_start, True, small + arrays
        )
        total = sent(total, "seq", 1)
        chunk_b = sent(chunk_b)
        chunk_c, tail_c, other, info = kernel(side, is_last, 0, True, loaded, c_all, total)
        chunk_c = sent(chunk_c)
        infos = [info] + [sent(info, "pipe", -k) for k in range(1, pipe_count)]
        chunk_d, tails = kernel(
            value_side, is_last, loaded, c_all, own, other, (tail_a, tail_b, tail_c)
        )
        chunk_d = sent(chunk_d)
        partial = kernel(router_side, is_first, loaded, own, other)
        parts = [partial] + [sent(partial, "tp", -k) for k in range(1, tp_count)]
        handed = place(None, chunk_a, shape, own_side, 0)
        handed = place(handed, chunk_b, shape, own_side, head_start)
        handed = place(handed, chunk_c, shape, other_side, 0)
        choice = pick(infos)[0, 0]

        def third(pairs, whole, x):
            return put(place_tail_kernel, whole, lax.ppermute(x, ("seq", "pipe"), pairs), shape)

        branches = [functools.partial(third, pairs) for pairs in third_pairs(pipe_count)]
        handed = lax.switch(choice, branches, handed, tails)
        handed, router_grad = finish(2, handed, chunk_d, parts)
    else:
        index = lax.axis_index("seq")
        places = jnp.arange(seq_count)[:, None, None, None]
        key_value, query_grad = shard_states(queries, keys, values, grad_out, router, blocks, counts)
        gathered = lax.all_gather(key_value, "seq")
        earlier = jnp.sum(jnp.where(places < index, gathered, 0.0), axis=0)
        gathered = lax.all_gather(query_grad, "seq")
        later = jnp.sum(jnp.where(places > index, gathered, 0.0), axis=0)
        loaded = (router, blocks) + tuple(x[0] for x in arrays)
        c_all = gathered_gradient(grad_out, router, blocks, counts)
        d_query, before = side(factor, always, 0, False, loaded, c_all, earlier)
        d_key, after = side(factor, never, 0, False, loaded, c_all, later)
        (d_value,) = value_side(factor, always, loaded, c_all, after, after)
        partial = router_side(factor, always, loaded, before, before)
        handed = None
        for section, chunk in enumerate((d_query, d_key, d_value)):
            chunk = from_behind(chunk, "pipe", -1)
            handed = place(handed, chunk, shape, functools.partial(int, section), 0)
        router_grad = lax.psum(partial, "tp")
    return (handed, router_grad)


def solution(mesh):
    return jax.shard_map(
        on_device,
        mesh=mesh,
        in_specs=(
            P("pipe", "seq", "tp"),
            P("pipe", "seq", "tp"),
            P("pipe", "seq", "tp"),
            P("pipe", "seq", "tp"),
            P("pipe", "seq"),
            P("pipe", "seq", None),
            P("pipe", "seq"),
        ),
        out_specs=(P("pipe", None, "seq", "tp"), P("pipe", "seq")),
        check_vma=False,
    )
```

```python
import functools
import itertools
import math

import jax
import jax.numpy as jnp
from jax import lax
from jax.experimental import pallas as pl
from jax.experimental.pallas import tpu as pltpu
from jax.sharding import PartitionSpec as P


HEAD_SIZE = 128
BLOCK_ROWS = 128
GRANT = 16 * 2**20


ANY = pl.BlockSpec(memory_space=pl.ANY)
HBM = pl.BlockSpec(memory_space=pltpu.HBM)
VMEM = pl.BlockSpec(memory_space=pltpu.VMEM)
SMEM = pl.BlockSpec(memory_space=pltpu.SMEM)


def from_behind(x, axis, by):
    count = lax.axis_size(axis)
    return lax.ppermute(x, axis, [(i, (i + by) % count) for i in range(count)])


def in_hbm(x):
    return pltpu.with_memory_space_constraint(x, pltpu.HBM)


def dot(a, b):
    return jnp.dot(a, b, preferred_element_type=jnp.float32)


def dot_nt(a, b):
    return lax.dot_general(a, b, (((1,), (1,)), ((), ())), preferred_element_type=jnp.float32)


def dot_tn(a, b):
    return lax.dot_general(a, b, (((0,), (0,)), ((), ())), preferred_element_type=jnp.float32)


def lanes(h, count=1):
    return pl.ds(h * HEAD_SIZE, count * HEAD_SIZE)


def rows_of(n):
    if isinstance(n, int):
        return pl.ds(n * BLOCK_ROWS, BLOCK_ROWS)
    return pl.ds(pl.multiple_of(n * BLOCK_ROWS, BLOCK_ROWS), BLOCK_ROWS)


def down_rows(router, block):
    weight = router[0:1, rows_of(block)]
    return jnp.broadcast_to(weight, (BLOCK_ROWS, BLOCK_ROWS)).T


def row_minus_column():
    shape = (BLOCK_ROWS, BLOCK_ROWS)
    return lax.broadcasted_iota(jnp.int32, shape, 0) - lax.broadcasted_iota(jnp.int32, shape, 1)


def compiler_params():
    return pltpu.CompilerParams(vmem_limit_bytes=GRANT)


def cost(matmuls, moved):
    return pl.CostEstimate(
        flops=2 * matmuls * HEAD_SIZE**3, bytes_accessed=moved, transcendentals=0
    )


def is_first():
    return lax.axis_index("seq") == 0


def is_last():
    return lax.axis_index("seq") != 0


def always():
    return True


def never():
    return False


def live_of(blocks, n):
    return jnp.bool_(True) if n == 0 else blocks[0, 0, n] > 0


def by_role(query_side, body):
    flag = query_side()
    if isinstance(flag, bool):
        body(flag)
    else:
        pl.when(flag)(lambda: body(True))
        pl.when(jnp.logical_not(flag))(lambda: body(False))


def in_order(query, slots):
    return list(range(slots)) if query else list(reversed(range(slots)))


def weigh(weight, grad):
    return (weight * grad.astype(jnp.float32)).astype(jnp.bfloat16)


def put_rows(chunk, tail, n, columns, rows):
    if tail is not None and n * BLOCK_ROWS == chunk.shape[0]:
        tail[:, columns] = rows
    else:
        chunk[rows_of(n), columns] = rows


def head_loads(pairs, begin, count, sem):
    return [
        pltpu.make_async_copy(source.at[0, :, lanes(begin, count)], target, sem.at[j])
        for j, (source, target) in enumerate(pairs)
    ]


def open_kernel(
    factor, query_side, end, router, blocks, q, k, v, g, chunk, tail,
    router_buf, blocks_buf, x_buf, v_buf, g_buf, c_buf, scores_buf, states_buf, acc,
    small_sem, load_sem,
):
    slots = blocks.shape[2]
    small = [
        pltpu.make_async_copy(blocks, blocks_buf, small_sem.at[0]),
        pltpu.make_async_copy(router, router_buf, small_sem.at[1]),
    ]
    for copy in small:
        copy.start()
    shared = head_loads(((g, g_buf), (v, v_buf)), 0, end, load_sem)
    for load in shared:
        load.start()

    def start(query):
        x = k if query else q
        pltpu.make_async_copy(x.at[0, :, lanes(0, end)], x_buf, load_sem.at[2]).start()

    by_role(query_side, start)
    difference = row_minus_column()
    for copy in small + shared[:1]:
        copy.wait()
    for n in range(slots):
        block = blocks_buf[0, 0, n]
        weight = jnp.where(live_of(blocks_buf, n), down_rows(router_buf, block), 0.0)
        for h in range(end):
            c_buf[rows_of(n), lanes(h)] = weigh(weight, g_buf[rows_of(block), lanes(h)])
    shared[1].wait()
    pltpu.make_async_copy(k.at[0, :, lanes(0, end)], x_buf, load_sem.at[2]).wait()

    def body(query):
        allowed = difference >= 0 if query else difference <= 0
        order = in_order(query, slots)

        def sides(n, h):
            c_h = c_buf[rows_of(n), lanes(h)]
            v_h = v_buf[rows_of(blocks_buf[0, 0, n]), lanes(h)]
            return (c_h, v_h) if query else (v_h, c_h)

        def x_of(n, h):
            return x_buf[rows_of(blocks_buf[0, 0, n]), lanes(h)]

        for n in order:
            for h in range(end):
                l_h, r_h = sides(n, h)
                scores_buf[n, h] = jnp.where(allowed, dot_nt(l_h, r_h), 0.0).astype(jnp.bfloat16)
        for i, n in enumerate(order[:-1]):
            for h in range(end):
                added = dot_tn(sides(n, h)[1], x_of(n, h))
                if i > 0:
                    added = acc[h] + added
                acc[h] = added
                states_buf[order[i + 1], h] = added.astype(jnp.bfloat16)
        for i, n in enumerate(order):
            scale = jnp.where(live_of(blocks_buf, n), factor, 0.0)
            for h in range(end):
                if i == 0:
                    out = dot(scores_buf[n, h], x_of(n, h))
                else:
                    out = dot(
                        jnp.concatenate([scores_buf[n, h], sides(n, h)[0]], axis=1),
                        jnp.concatenate([x_of(n, h), states_buf[n, h]], axis=0),
                    )
                put_rows(chunk, tail, n, lanes(h), (scale * out).astype(jnp.bfloat16))

    by_role(query_side, body)


def split_rows(slots, width):
    return [
        pltpu.VMEM(((slots - 1) * BLOCK_ROWS, width), jnp.bfloat16),
        pltpu.VMEM((BLOCK_ROWS, width), jnp.bfloat16),
    ]


def opened(factor, query_side, end, small, arrays):
    router, blocks = small
    _, shard_rows, _ = arrays[0].shape
    slots = blocks.shape[2]
    part = pltpu.VMEM((shard_rows, end * HEAD_SIZE), jnp.bfloat16)
    return pl.pallas_call(
        functools.partial(open_kernel, factor, query_side, end),
        name="opened",
        out_shape=split_rows(slots, end * HEAD_SIZE),
        in_specs=[HBM] * 6,
        out_specs=[VMEM] * 2,
        scratch_shapes=[
            pltpu.VMEM(router.shape, router.dtype),
            pltpu.SMEM(blocks.shape, blocks.dtype),
            part, part, part,
            pltpu.VMEM((slots * BLOCK_ROWS, end * HEAD_SIZE), jnp.bfloat16),
            pltpu.VMEM((slots, end, HEAD_SIZE, HEAD_SIZE), jnp.bfloat16),
            pltpu.VMEM((slots, end, HEAD_SIZE, HEAD_SIZE), jnp.bfloat16),
            pltpu.VMEM((end, HEAD_SIZE, HEAD_SIZE), jnp.float32),
            pltpu.SemaphoreType.DMA((2,)),
            pltpu.SemaphoreType.DMA((3,)),
        ],
        compiler_params=compiler_params(),
        cost_estimate=cost(4 * slots * end, 6 * shard_rows * end * HEAD_SIZE),
    )(router, blocks, *arrays)


def side_kernel(factor, query_side, begin, seeded, split, *refs):
    (router, blocks, q, k, v, g), refs = refs[:6], refs[6:]
    tail = None
    if seeded and split:
        c_all, seed, chunk, tail, states, info, scores_buf, total = refs
    elif seeded:
        c_all, seed, chunk, states, scores_buf, total = refs
    else:
        sources = (router, blocks, q, k, v, g)
        chunk, tail, states, total, c_all, *targets = refs[:11]
        scores_buf, load_sem = refs[11:]
        router, blocks, q, k, v, g = targets
    slots = blocks.shape[2]
    heads = states.shape[1]
    difference = row_minus_column()

    if not seeded:
        loads = [
            pltpu.make_async_copy(source if j < 2 else source.at[0], target, load_sem.at[j])
            for j, (source, target) in enumerate(zip(sources, targets))
        ]
        for j in (1, 0, 5, 4):
            loads[j].start()

        def start(query):
            for j in (3, 2) if query else (2, 3):
                loads[j].start()

        by_role(query_side, start)
        for j in (1, 0, 5):
            loads[j].wait()

    def body(query):
        allowed = difference >= 0 if query else difference <= 0
        x_all = k if query else q
        order = in_order(query, slots)
        if not seeded:
            for n in order:
                block = blocks[0, 0, n]
                weight = jnp.where(live_of(blocks, n), down_rows(router, block), 0.0)
                for h in range(heads):
                    c_all[rows_of(n), lanes(h)] = weigh(weight, g[rows_of(block), lanes(h)])
            for j in (4, 3 if query else 2):
                loads[j].wait()
        for i, n in enumerate(order):
            live = live_of(blocks, n)
            rows = rows_of(blocks[0, 0, n])
            own = rows_of(n)
            scale = jnp.where(live, factor, 0.0)

            def sides(h):
                c_h, v_h = c_all[own, lanes(h)], v[rows, lanes(h)]
                return (c_h, v_h) if query else (v_h, c_h)

            for h in range(begin, heads):
                l_h, r_h = sides(h)
                scores_buf[n, h] = jnp.where(allowed, dot_nt(l_h, r_h), 0.0).astype(jnp.bfloat16)
            for h in range(heads):
                if i > 0:
                    so_far = total[h]
                elif seeded:
                    so_far = seed[h]
                else:
                    so_far = jnp.zeros((HEAD_SIZE, HEAD_SIZE), jnp.float32)
                states[n, h] = so_far.astype(jnp.bfloat16)
                if not seeded or i + 1 < slots:
                    added = dot_tn(sides(h)[1], x_all[rows, lanes(h)])
                    if query and n > 0:
                        added = jnp.where(live, added, 0.0)
                    total[h] = so_far + added
            for h in range(begin, heads):
                l_h, _ = sides(h)
                x_h = x_all[rows, lanes(h)]
                if i == 0 and not seeded:
                    out = dot(scores_buf[n, h], x_h)
                else:
                    out = dot(
                        jnp.concatenate([scores_buf[n, h], l_h], axis=1),
                        jnp.concatenate([x_h, states[n, h]], axis=0),
                    )
                out = (scale * out).astype(jnp.bfloat16)
                put_rows(chunk, tail, n, lanes(h - begin), out)
        full = jnp.where(live_of(blocks, slots - 1), 1.0, 0.0)
        if not seeded:
            total[heads] = jnp.full((HEAD_SIZE, HEAD_SIZE), full, jnp.float32)
            loads[2 if query else 3].wait()
        elif split:
            other = seed[heads, 0:8, :]
            own_full = jnp.full(other.shape, full, jnp.float32)
            info[...] = jnp.where(own_full + other > 1.5, 2.0, own_full if query else other)

    by_role(query_side, body)


def side(factor, query_side, begin, split, arrays, c_all=None, seed=None):
    router, blocks = arrays[:2]
    shard_rows, width = arrays[2].shape[-2:]
    heads = width // HEAD_SIZE
    slots = blocks.shape[2]
    square = (HEAD_SIZE, HEAD_SIZE)
    out_width = (heads - begin) * HEAD_SIZE
    if split:
        out_shape = split_rows(slots, out_width)
    else:
        out_shape = [pltpu.VMEM((slots * BLOCK_ROWS, out_width), jnp.bfloat16)]
    out_shape.append(pltpu.VMEM((slots, heads) + square, jnp.bfloat16))
    scratch = [pltpu.VMEM((slots, heads) + square, jnp.bfloat16)]
    seeded = seed is not None
    if seeded:
        if split:
            out_shape.append(pltpu.VMEM((8, HEAD_SIZE), jnp.float32))
        out_specs = [VMEM] * len(out_shape)
        scratch.append(pltpu.VMEM((heads,) + square, jnp.float32))
        extra = (c_all, seed)
        in_specs = [VMEM, SMEM] + [VMEM] * 6
    else:
        out_shape.append(pltpu.VMEM((heads + 1,) + square, jnp.float32))
        out_shape.append(pltpu.VMEM((slots * BLOCK_ROWS, width), jnp.bfloat16))
        out_shape += [pltpu.VMEM(router.shape, router.dtype), pltpu.SMEM(blocks.shape, blocks.dtype)]
        out_shape += [pltpu.VMEM((shard_rows, width), jnp.bfloat16)] * 4
        out_specs = [VMEM] * 6 + [SMEM] + [VMEM] * 4
        scratch.append(pltpu.SemaphoreType.DMA((6,)))
        extra = ()
        in_specs = [HBM] * 6
    return pl.pallas_call(
        functools.partial(side_kernel, factor, query_side, begin, seeded, split),
        name="side",
        out_shape=out_shape,
        in_specs=in_specs,
        out_specs=out_specs,
        scratch_shapes=scratch,
        compiler_params=compiler_params(),
        cost_estimate=cost(4 * slots * heads, 0 if seeded else 8 * shard_rows * width),
    )(*arrays, *extra)


def value_kernel(factor, take_one, split, blocks, q, k, c_all, one, two, *refs):
    if split:
        tail_a, tail_b, tail_c, chunk, tails, scores_buf = refs
        tail = tails.at[2]
    else:
        chunk, scores_buf = refs
        tail = None
    slots = blocks.shape[2]
    heads = q.shape[1] // HEAD_SIZE
    allowed = row_minus_column() <= 0

    def body(pick):
        states = one if pick else two
        for n in range(slots):
            rows = rows_of(blocks[0, 0, n])
            own = rows_of(n)
            scale = jnp.where(live_of(blocks, n), factor, 0.0)
            for h in range(heads):
                scores_buf[n, h] = jnp.where(
                    allowed, dot_nt(k[rows, lanes(h)], q[rows, lanes(h)]), 0.0
                ).astype(jnp.bfloat16)
            for h in range(heads):
                out = dot(scores_buf[n, h], c_all[own, lanes(h)])
                out = out + dot_nt(k[rows, lanes(h)], states[n, h])
                put_rows(chunk, tail, n, lanes(h), (scale * out).astype(jnp.bfloat16))
        if split:
            begin = tail_a.shape[1] // HEAD_SIZE
            early, late = (1, 0) if pick else (0, 1)
            tails[early, :, lanes(0, begin)] = tail_a[...]
            tails[early, :, lanes(begin, heads - begin)] = tail_b[...]
            tails[late] = tail_c[...]

    by_role(take_one, body)


def value_side(factor, take_one, loaded, c_all, one, two, tails=()):
    _, blocks, q, k, _, _ = loaded
    slots, heads = one.shape[:2]
    width = heads * HEAD_SIZE
    split = len(tails) > 0
    if split:
        out_shape = [
            split_rows(slots, width)[0], pltpu.VMEM((3, BLOCK_ROWS, width), jnp.bfloat16)
        ]
    else:
        out_shape = [pltpu.VMEM((slots * BLOCK_ROWS, width), jnp.bfloat16)]
    return pl.pallas_call(
        functools.partial(value_kernel, factor, take_one, split),
        name="value_side",
        out_shape=out_shape,
        in_specs=[SMEM] + [VMEM] * (5 + len(tails)),
        out_specs=[VMEM] * len(out_shape),
        scratch_shapes=[pltpu.VMEM(one.shape, jnp.bfloat16)],
        compiler_params=compiler_params(),
        cost_estimate=cost(3 * slots * heads, 0),
    )(blocks, q, k, c_all, one, two, *tails)


def router_kernel(factor, take_one, blocks, q, k, v, g, one, two, partial, scores_buf):
    slots = blocks.shape[2]
    heads = q.shape[1] // HEAD_SIZE
    allowed = row_minus_column() >= 0

    def body(pick):
        states = one if pick else two
        for n in range(slots):
            rows = rows_of(blocks[0, 0, n])
            for h in range(heads):
                scores_buf[n, h] = jnp.where(
                    allowed, dot_nt(q[rows, lanes(h)], k[rows, lanes(h)]), 0.0
                ).astype(jnp.bfloat16)
            by_row = jnp.zeros((BLOCK_ROWS, HEAD_SIZE), jnp.float32)
            for h in range(heads):
                core = dot(scores_buf[n, h], v[rows, lanes(h)])
                core = factor * (core + dot_nt(q[rows, lanes(h)], states[n, h]))
                by_row = by_row + g[rows, lanes(h)].astype(jnp.float32) * core
            by_row = jnp.where(live_of(blocks, n), by_row, 0.0)
            partial[0:1, rows_of(n)] = jnp.sum(by_row.T, axis=0, keepdims=True)

    by_role(take_one, body)


def router_side(factor, take_one, loaded, one, two):
    _, blocks, *arrays = loaded
    slots = one.shape[0]
    return pl.pallas_call(
        functools.partial(router_kernel, factor, take_one),
        name="router_side",
        out_shape=jax.ShapeDtypeStruct((1, slots * BLOCK_ROWS), jnp.float32),
        in_specs=[SMEM] + [VMEM] * 6,
        out_specs=VMEM,
        scratch_shapes=[pltpu.VMEM(one.shape, jnp.bfloat16)],
        compiler_params=compiler_params(),
        cost_estimate=cost(3 * slots * one.shape[1], 0),
    )(blocks, *arrays, one, two)


def place_kernel(section_of, begin, *refs):
    chunk, out, sem = refs[-3:]
    rows, width = chunk.shape
    target = out.at[0, section_of(), pl.ds(0, rows), lanes(begin, width // HEAD_SIZE)]
    copy = pltpu.make_async_copy(chunk, target, sem)
    copy.start()
    copy.wait()


def keep_kernel(old, new, out):
    del old
    out[...] = new[...]


def third(pairs, tails):
    received = lax.ppermute(tails, ("seq", "pipe"), pairs)
    return pl.pallas_call(
        keep_kernel,
        name="keep",
        out_shape=pltpu.VMEM(tails.shape, tails.dtype),
        in_specs=[VMEM] * 2,
        out_specs=VMEM,
        input_output_aliases={0: 0},
        compiler_params=pltpu.CompilerParams(vmem_limit_bytes=2**20),
    )(tails, received)


def finish_kernel(section, whole, chunk, tails, *refs):
    del whole
    parts, (out, total, total_buf, sem) = refs[:-4], refs[-4:]
    rows = chunk.shape[0]
    copies = [
        pltpu.make_async_copy(tails, out.at[0, :, pl.ds(rows, tails.shape[1])], sem.at[0]),
        pltpu.make_async_copy(chunk, out.at[0, section, pl.ds(0, rows)], sem.at[1]),
        pltpu.make_async_copy(total_buf, total, sem.at[2]),
    ]
    copies[0].start()
    copies[1].start()
    total_buf[...] = folded([part[...] for part in parts])
    copies[2].start()
    for copy in copies:
        copy.wait()


def finish(section, whole, chunk, tails, parts):
    return pl.pallas_call(
        functools.partial(finish_kernel, section),
        name="finish",
        out_shape=[
            pltpu.HBM(whole.shape, whole.dtype),
            pltpu.HBM(parts[0].shape, parts[0].dtype),
        ],
        in_specs=[HBM, ANY, ANY] + [VMEM] * len(parts),
        out_specs=[HBM, HBM],
        scratch_shapes=[
            pltpu.VMEM(parts[0].shape, parts[0].dtype),
            pltpu.SemaphoreType.DMA((3,)),
        ],
        input_output_aliases={0: 0},
        compiler_params=pltpu.CompilerParams(vmem_limit_bytes=2**20),
        cost_estimate=cost(0, 4 * (chunk.size + tails.size)),
    )(whole, chunk, tails, *parts)


def place(whole, chunk, shape, section_of, begin):
    operands = (chunk,) if whole is None else (whole, chunk)
    return pl.pallas_call(
        functools.partial(place_kernel, section_of, begin),
        name="place",
        out_shape=pltpu.HBM(shape, chunk.dtype),
        in_specs=[HBM] * (len(operands) - 1) + [ANY],
        out_specs=HBM,
        scratch_shapes=[pltpu.SemaphoreType.DMA],
        input_output_aliases={} if whole is None else {0: 0},
        compiler_params=pltpu.CompilerParams(vmem_limit_bytes=2**20),
        cost_estimate=cost(0, 4 * chunk.size),
    )(*operands)


def pick_kernel(*refs):
    infos, out = refs[:-1], refs[-1]
    count = len(infos)
    here = lax.axis_index("pipe")
    both = jnp.bool_(False)
    choice = jnp.int32(0)
    for k, info in enumerate(infos):
        code = jnp.max(info[...])
        section = lax.rem(here + k, count)
        weight = jnp.left_shift(jnp.int32(1), count - 1 - section)
        both = jnp.logical_or(both, code > 1.5)
        choice = choice + jnp.where(code > 0.5, weight, 0)
    out[0, 0] = jnp.where(both, 0, 1 + choice)


def pick(infos):
    return pl.pallas_call(
        pick_kernel,
        name="pick",
        out_shape=pltpu.SMEM((1, 1), jnp.int32),
        in_specs=[VMEM] * len(infos),
        out_specs=SMEM,
        compiler_params=pltpu.CompilerParams(vmem_limit_bytes=2**20),
    )(*infos)


def third_pairs(pipe_count):
    def pair(s, p):
        return (s * pipe_count + p, s * pipe_count + (p - 1) % pipe_count)

    every = [pair(s, p) for s in (0, 1) for p in range(pipe_count)]
    return [every] + [
        [pair(s, p) for p, s in enumerate(cores)]
        for cores in itertools.product((0, 1), repeat=pipe_count)
    ]


def folded(parts):
    while len(parts) > 1:
        half = len(parts) // 2
        parts = [parts[k] + parts[k + half] for k in range(half)]
    return parts[0]


def shard_states(queries, keys, values, grad_out, router, blocks, counts):
    heads = queries.shape[2] // HEAD_SIZE
    slots = blocks.shape[2]
    shard_blocks = queries.shape[1] // BLOCK_ROWS
    live = jnp.arange(slots, dtype=jnp.int32) < counts[0, 0]
    taken = (blocks[0, 0, :, None] == jnp.arange(shard_blocks, dtype=jnp.int32)) & live[:, None]
    mask = jnp.repeat(jnp.any(taken, axis=0), BLOCK_ROWS)[:, None]

    def rows(array):
        picked = jnp.where(mask, array[0], jnp.zeros((), array.dtype))
        return picked.reshape(-1, heads, HEAD_SIZE)

    weighted = (router[0][:, None, None] * rows(grad_out).astype(jnp.float32)).astype(jnp.bfloat16)
    key_value = jnp.einsum(
        "the,thd->hed", rows(values), rows(keys), preferred_element_type=jnp.float32
    )
    query_grad = jnp.einsum(
        "the,thd->hed", weighted, rows(queries), preferred_element_type=jnp.float32
    )
    return key_value, query_grad


def gathered_gradient(grad_out, router, blocks, counts):
    slots = blocks.shape[2]
    live = jnp.arange(slots, dtype=jnp.int32) < counts[0, 0]
    grouped = grad_out[0].reshape(-1, BLOCK_ROWS, grad_out.shape[2])[blocks[0, 0]]
    weight = jnp.where(live[:, None], router[0].reshape(-1, BLOCK_ROWS)[blocks[0, 0]], 0.0)
    weighted = weight[:, :, None] * grouped.astype(jnp.float32)
    return weighted.astype(jnp.bfloat16).reshape(slots * BLOCK_ROWS, -1)


def fits(seq_count, pipe_count, tp_count, slots):
    return seq_count == 2 and pipe_count <= 4 and tp_count in (1, 2, 4, 8) and slots > 1


def own_side():
    return jnp.where(is_first(), 0, 1)


def other_side():
    return jnp.where(is_first(), 1, 0)


def on_device(queries, keys, values, grad_out, router, blocks, counts):
    slots = blocks.shape[2]
    rows = slots * BLOCK_ROWS
    width = queries.shape[2]
    heads = width // HEAD_SIZE
    seq_count, pipe_count, tp_count = (lax.axis_size(axis) for axis in ("seq", "pipe", "tp"))
    factor = 1.0 / math.sqrt(HEAD_SIZE * rows * seq_count)
    arrays = (queries, keys, values, grad_out)
    shape = (1, 3, rows, width)
    if fits(seq_count, pipe_count, tp_count, slots):
        head_start = max(1, 2 * heads // 3)
        small = (in_hbm(router), in_hbm(blocks))
        arrays = tuple(in_hbm(x) for x in arrays)

        def sent(x, axis="pipe", by=-1):
            return from_behind(x, axis, by)

        def kernel(call, *operands):
            return call(factor, *operands)

        chunk_a, tail_a = kernel(opened, is_first, head_start, small, arrays)
        chunk_a = sent(chunk_a)
        chunk_b, tail_b, own, total, c_all, *loaded = kernel(
            side, is_first, head_start, True, small + arrays
        )
        total = sent(total, "seq", 1)
        chunk_b = sent(chunk_b)
        chunk_c, tail_c, other, info = kernel(side, is_last, 0, True, loaded, c_all, total)
        chunk_c = sent(chunk_c)
        infos = [info] + [sent(info, "pipe", -k) for k in range(1, pipe_count)]
        chunk_d, tails = kernel(
            value_side, is_last, loaded, c_all, own, other, (tail_a, tail_b, tail_c)
        )
        chunk_d = sent(chunk_d)
        partial = kernel(router_side, is_first, loaded, own, other)
        parts = [partial] + [sent(partial, "tp", -k) for k in range(1, tp_count)]
        handed = place(None, chunk_a, shape, own_side, 0)
        handed = place(handed, chunk_b, shape, own_side, head_start)
        handed = place(handed, chunk_c, shape, other_side, 0)
        choice = pick(infos)[0, 0]

        branches = [functools.partial(third, pairs) for pairs in third_pairs(pipe_count)]
        handed, tails = lax.optimization_barrier((handed, tails))
        tails = lax.switch(choice, branches, tails)
        handed, router_grad = finish(2, handed, chunk_d, tails, parts)
    else:
        index = lax.axis_index("seq")
        places = jnp.arange(seq_count)[:, None, None, None]
        key_value, query_grad = shard_states(queries, keys, values, grad_out, router, blocks, counts)
        gathered = lax.all_gather(key_value, "seq")
        earlier = jnp.sum(jnp.where(places < index, gathered, 0.0), axis=0)
        gathered = lax.all_gather(query_grad, "seq")
        later = jnp.sum(jnp.where(places > index, gathered, 0.0), axis=0)
        loaded = (router, blocks) + tuple(x[0] for x in arrays)
        c_all = gathered_gradient(grad_out, router, blocks, counts)
        d_query, before = side(factor, always, 0, False, loaded, c_all, earlier)
        d_key, after = side(factor, never, 0, False, loaded, c_all, later)
        (d_value,) = value_side(factor, always, loaded, c_all, after, after)
        partial = router_side(factor, always, loaded, before, before)
        handed = None
        for section, chunk in enumerate((d_query, d_key, d_value)):
            chunk = from_behind(chunk, "pipe", -1)
            handed = place(handed, chunk, shape, functools.partial(int, section), 0)
        router_grad = lax.psum(partial, "tp")
    return (handed, router_grad)


def solution(mesh):
    return jax.shard_map(
        on_device,
        mesh=mesh,
        in_specs=(
            P("pipe", "seq", "tp"),
            P("pipe", "seq", "tp"),
            P("pipe", "seq", "tp"),
            P("pipe", "seq", "tp"),
            P("pipe", "seq"),
            P("pipe", "seq", None),
            P("pipe", "seq"),
        ),
        out_specs=(P("pipe", None, "seq", "tp"), P("pipe", "seq")),
        check_vma=False,
    )
```

```python
import functools
import itertools
import math

import jax
import jax.numpy as jnp
from jax import lax
from jax.experimental import pallas as pl
from jax.experimental.pallas import tpu as pltpu
from jax.sharding import PartitionSpec as P


HEAD_SIZE = 128
BLOCK_ROWS = 128
GRANT = 16 * 2**20


ANY = pl.BlockSpec(memory_space=pl.ANY)
HBM = pl.BlockSpec(memory_space=pltpu.HBM)
VMEM = pl.BlockSpec(memory_space=pltpu.VMEM)
SMEM = pl.BlockSpec(memory_space=pltpu.SMEM)


def from_behind(x, axis, by):
    count = lax.axis_size(axis)
    return lax.ppermute(x, axis, [(i, (i + by) % count) for i in range(count)])


def in_hbm(x):
    return pltpu.with_memory_space_constraint(x, pltpu.HBM)


def dot(a, b):
    return jnp.dot(a, b, preferred_element_type=jnp.float32)


def dot_nt(a, b):
    return lax.dot_general(a, b, (((1,), (1,)), ((), ())), preferred_element_type=jnp.float32)


def dot_tn(a, b):
    return lax.dot_general(a, b, (((0,), (0,)), ((), ())), preferred_element_type=jnp.float32)


def lanes(h, count=1):
    return pl.ds(h * HEAD_SIZE, count * HEAD_SIZE)


def rows_of(n):
    if isinstance(n, int):
        return pl.ds(n * BLOCK_ROWS, BLOCK_ROWS)
    return pl.ds(pl.multiple_of(n * BLOCK_ROWS, BLOCK_ROWS), BLOCK_ROWS)


def down_rows(router, block):
    weight = router[0:1, rows_of(block)]
    return jnp.broadcast_to(weight, (BLOCK_ROWS, BLOCK_ROWS)).T


def row_minus_column():
    shape = (BLOCK_ROWS, BLOCK_ROWS)
    return lax.broadcasted_iota(jnp.int32, shape, 0) - lax.broadcasted_iota(jnp.int32, shape, 1)


def compiler_params():
    return pltpu.CompilerParams(vmem_limit_bytes=GRANT)


def cost(matmuls, moved):
    return pl.CostEstimate(
        flops=2 * matmuls * HEAD_SIZE**3, bytes_accessed=moved, transcendentals=0
    )


def is_first():
    return lax.axis_index("seq") == 0


def is_last():
    return lax.axis_index("seq") != 0


def always():
    return True


def never():
    return False


def live_of(blocks, n):
    return jnp.bool_(True) if n == 0 else blocks[0, 0, n] > 0


def by_role(query_side, body):
    flag = query_side()
    if isinstance(flag, bool):
        body(flag)
    else:
        pl.when(flag)(lambda: body(True))
        pl.when(jnp.logical_not(flag))(lambda: body(False))


def in_order(query, slots):
    return list(range(slots)) if query else list(reversed(range(slots)))


def weigh(weight, grad):
    return (weight * grad.astype(jnp.float32)).astype(jnp.bfloat16)


def put_rows(chunk, tail, n, columns, rows):
    if tail is not None and n * BLOCK_ROWS == chunk.shape[0]:
        tail[:, columns] = rows
    else:
        chunk[rows_of(n), columns] = rows


def head_loads(pairs, begin, count, sem):
    return [
        pltpu.make_async_copy(source.at[0, :, lanes(begin, count)], target, sem.at[j])
        for j, (source, target) in enumerate(pairs)
    ]


def open_kernel(
    factor, query_side, end, router, blocks, q, k, v, g, chunk, tail, router_buf, blocks_buf,
    x_buf, v_buf, g_buf, c_buf, scores_buf, states_buf, acc,
    small_sem, load_sem,
):
    slots = blocks.shape[2]
    small = [
        pltpu.make_async_copy(blocks, blocks_buf, small_sem.at[0]),
        pltpu.make_async_copy(router, router_buf, small_sem.at[1]),
    ]
    for copy in small:
        copy.start()
    shared = head_loads(((g, g_buf), (v, v_buf)), 0, end, load_sem)
    for load in shared:
        load.start()

    def start(query):
        x = k if query else q
        pltpu.make_async_copy(x.at[0, :, lanes(0, end)], x_buf, load_sem.at[2]).start()

    by_role(query_side, start)
    difference = row_minus_column()
    for copy in small + shared[:1]:
        copy.wait()
    for n in range(slots):
        block = blocks_buf[0, 0, n]
        weight = jnp.where(live_of(blocks_buf, n), down_rows(router_buf, block), 0.0)
        for h in range(end):
            c_buf[rows_of(n), lanes(h)] = weigh(weight, g_buf[rows_of(block), lanes(h)])
    shared[1].wait()
    pltpu.make_async_copy(k.at[0, :, lanes(0, end)], x_buf, load_sem.at[2]).wait()

    def body(query):
        allowed = difference >= 0 if query else difference <= 0
        order = in_order(query, slots)

        def sides(n, h):
            c_h = c_buf[rows_of(n), lanes(h)]
            v_h = v_buf[rows_of(blocks_buf[0, 0, n]), lanes(h)]
            return (c_h, v_h) if query else (v_h, c_h)

        def x_of(n, h):
            return x_buf[rows_of(blocks_buf[0, 0, n]), lanes(h)]

        for n in order:
            for h in range(end):
                l_h, r_h = sides(n, h)
                scores_buf[n, h] = jnp.where(allowed, dot_nt(l_h, r_h), 0.0).astype(jnp.bfloat16)
        for i, n in enumerate(order[:-1]):
            for h in range(end):
                added = dot_tn(sides(n, h)[1], x_of(n, h))
                if i > 0:
                    added = acc[h] + added
                acc[h] = added
                states_buf[order[i + 1], h] = added.astype(jnp.bfloat16)
        for i, n in enumerate(order):
            scale = jnp.where(live_of(blocks_buf, n), factor, 0.0)
            for h in range(end):
                if i == 0:
                    out = dot(scores_buf[n, h], x_of(n, h))
                else:
                    out = dot(
                        jnp.concatenate([scores_buf[n, h], sides(n, h)[0]], axis=1),
                        jnp.concatenate([x_of(n, h), states_buf[n, h]], axis=0),
                    )
                put_rows(chunk, tail, n, lanes(h), (scale * out).astype(jnp.bfloat16))

    by_role(query_side, body)


def split_rows(slots, width):
    return [
        pltpu.VMEM(((slots - 1) * BLOCK_ROWS, width), jnp.bfloat16),
        pltpu.VMEM((BLOCK_ROWS, width), jnp.bfloat16),
    ]


def opened(factor, query_side, end, small, arrays):
    router, blocks = small
    _, shard_rows, _ = arrays[0].shape
    slots = blocks.shape[2]
    part = pltpu.VMEM((shard_rows, end * HEAD_SIZE), jnp.bfloat16)
    return pl.pallas_call(
        functools.partial(open_kernel, factor, query_side, end),
        name="opened",
        out_shape=split_rows(slots, end * HEAD_SIZE)
        + [pltpu.VMEM(router.shape, router.dtype), pltpu.SMEM(blocks.shape, blocks.dtype)],
        in_specs=[HBM] * 6,
        out_specs=[VMEM] * 3 + [SMEM],
        scratch_shapes=[
            part, part, part,
            pltpu.VMEM((slots * BLOCK_ROWS, end * HEAD_SIZE), jnp.bfloat16),
            pltpu.VMEM((slots, end, HEAD_SIZE, HEAD_SIZE), jnp.bfloat16),
            pltpu.VMEM((slots, end, HEAD_SIZE, HEAD_SIZE), jnp.bfloat16),
            pltpu.VMEM((end, HEAD_SIZE, HEAD_SIZE), jnp.float32),
            pltpu.SemaphoreType.DMA((2,)),
            pltpu.SemaphoreType.DMA((3,)),
        ],
        compiler_params=compiler_params(),
        cost_estimate=cost(4 * slots * end, 6 * shard_rows * end * HEAD_SIZE),
    )(router, blocks, *arrays)


def side_kernel(factor, query_side, begin, seeded, split, *refs):
    (router, blocks, q, k, v, g), refs = refs[:6], refs[6:]
    tail = None
    if seeded and split:
        c_all, seed, chunk, tail, states, info, scores_buf, total = refs
    elif seeded:
        c_all, seed, chunk, states, scores_buf, total = refs
    else:
        chunk, tail, states, total, c_all, scores_buf = refs
    slots = blocks.shape[2]
    heads = states.shape[1]
    difference = row_minus_column()

    def body(query):
        allowed = difference >= 0 if query else difference <= 0
        x_all = k if query else q
        order = in_order(query, slots)
        if not seeded:
            for n in order:
                block = blocks[0, 0, n]
                weight = jnp.where(live_of(blocks, n), down_rows(router, block), 0.0)
                for h in range(heads):
                    c_all[rows_of(n), lanes(h)] = weigh(weight, g[rows_of(block), lanes(h)])
        for i, n in enumerate(order):
            live = live_of(blocks, n)
            rows = rows_of(blocks[0, 0, n])
            own = rows_of(n)
            scale = jnp.where(live, factor, 0.0)

            def sides(h):
                c_h, v_h = c_all[own, lanes(h)], v[rows, lanes(h)]
                return (c_h, v_h) if query else (v_h, c_h)

            for h in range(begin, heads):
                l_h, r_h = sides(h)
                scores_buf[n, h] = jnp.where(allowed, dot_nt(l_h, r_h), 0.0).astype(jnp.bfloat16)
            for h in range(heads):
                if i > 0:
                    so_far = total[h]
                elif seeded:
                    so_far = seed[h]
                else:
                    so_far = jnp.zeros((HEAD_SIZE, HEAD_SIZE), jnp.float32)
                states[n, h] = so_far.astype(jnp.bfloat16)
                if not seeded or i + 1 < slots:
                    added = dot_tn(sides(h)[1], x_all[rows, lanes(h)])
                    if query and n > 0:
                        added = jnp.where(live, added, 0.0)
                    total[h] = so_far + added
            for h in range(begin, heads):
                l_h, _ = sides(h)
                x_h = x_all[rows, lanes(h)]
                if i == 0 and not seeded:
                    out = dot(scores_buf[n, h], x_h)
                else:
                    out = dot(
                        jnp.concatenate([scores_buf[n, h], l_h], axis=1),
                        jnp.concatenate([x_h, states[n, h]], axis=0),
                    )
                out = (scale * out).astype(jnp.bfloat16)
                put_rows(chunk, tail, n, lanes(h - begin), out)
        full = jnp.where(live_of(blocks, slots - 1), 1.0, 0.0)
        if not seeded:
            total[heads] = jnp.full((HEAD_SIZE, HEAD_SIZE), full, jnp.float32)
        elif split:
            other = seed[heads, 0:8, :]
            own_full = jnp.full(other.shape, full, jnp.float32)
            info[...] = jnp.where(own_full + other > 1.5, 2.0, own_full if query else other)

    by_role(query_side, body)


def side(factor, query_side, begin, split, arrays, c_all=None, seed=None):
    _, blocks = arrays[:2]
    width = arrays[2].shape[1]
    heads = width // HEAD_SIZE
    slots = blocks.shape[2]
    square = (HEAD_SIZE, HEAD_SIZE)
    out_width = (heads - begin) * HEAD_SIZE
    if split:
        out_shape = split_rows(slots, out_width)
    else:
        out_shape = [pltpu.VMEM((slots * BLOCK_ROWS, out_width), jnp.bfloat16)]
    out_shape.append(pltpu.VMEM((slots, heads) + square, jnp.bfloat16))
    scratch = [pltpu.VMEM((slots, heads) + square, jnp.bfloat16)]
    seeded = seed is not None
    if seeded:
        if split:
            out_shape.append(pltpu.VMEM((8, HEAD_SIZE), jnp.float32))
        scratch.append(pltpu.VMEM((heads,) + square, jnp.float32))
        extra = (c_all, seed)
    else:
        out_shape.append(pltpu.VMEM((heads + 1,) + square, jnp.float32))
        out_shape.append(pltpu.VMEM((slots * BLOCK_ROWS, width), jnp.bfloat16))
        extra = ()
    return pl.pallas_call(
        functools.partial(side_kernel, factor, query_side, begin, seeded, split),
        name="side",
        out_shape=out_shape,
        in_specs=[VMEM, SMEM] + [VMEM] * (4 + len(extra)),
        out_specs=[VMEM] * len(out_shape),
        scratch_shapes=scratch,
        compiler_params=compiler_params(),
        cost_estimate=cost(4 * slots * heads, 0),
    )(*arrays, *extra)


def value_kernel(factor, take_one, split, blocks, q, k, c_all, one, two, *refs):
    if split:
        tail_a, tail_b, tail_c, chunk, tails, scores_buf = refs
        tail = tails.at[2]
    else:
        chunk, scores_buf = refs
        tail = None
    slots = blocks.shape[2]
    heads = q.shape[1] // HEAD_SIZE
    allowed = row_minus_column() <= 0

    def body(pick):
        states = one if pick else two
        for n in range(slots):
            rows = rows_of(blocks[0, 0, n])
            own = rows_of(n)
            scale = jnp.where(live_of(blocks, n), factor, 0.0)
            for h in range(heads):
                scores_buf[n, h] = jnp.where(
                    allowed, dot_nt(k[rows, lanes(h)], q[rows, lanes(h)]), 0.0
                ).astype(jnp.bfloat16)
            for h in range(heads):
                out = dot(scores_buf[n, h], c_all[own, lanes(h)])
                out = out + dot_nt(k[rows, lanes(h)], states[n, h])
                put_rows(chunk, tail, n, lanes(h), (scale * out).astype(jnp.bfloat16))
        if split:
            begin = tail_a.shape[1] // HEAD_SIZE
            early, late = (1, 0) if pick else (0, 1)
            tails[early, :, lanes(0, begin)] = tail_a[...]
            tails[early, :, lanes(begin, heads - begin)] = tail_b[...]
            tails[late] = tail_c[...]

    by_role(take_one, body)


def value_side(factor, take_one, loaded, c_all, one, two, tails=()):
    _, blocks, q, k, _, _ = loaded
    slots, heads = one.shape[:2]
    width = heads * HEAD_SIZE
    split = len(tails) > 0
    if split:
        out_shape = [
            split_rows(slots, width)[0], pltpu.VMEM((3, BLOCK_ROWS, width), jnp.bfloat16)
        ]
    else:
        out_shape = [pltpu.VMEM((slots * BLOCK_ROWS, width), jnp.bfloat16)]
    return pl.pallas_call(
        functools.partial(value_kernel, factor, take_one, split),
        name="value_side",
        out_shape=out_shape,
        in_specs=[SMEM] + [VMEM] * (5 + len(tails)),
        out_specs=[VMEM] * len(out_shape),
        scratch_shapes=[pltpu.VMEM(one.shape, jnp.bfloat16)],
        compiler_params=compiler_params(),
        cost_estimate=cost(3 * slots * heads, 0),
    )(blocks, q, k, c_all, one, two, *tails)


def router_kernel(factor, take_one, blocks, q, k, v, g, one, two, partial, scores_buf):
    slots = blocks.shape[2]
    heads = q.shape[1] // HEAD_SIZE
    allowed = row_minus_column() >= 0

    def body(pick):
        states = one if pick else two
        for n in range(slots):
            rows = rows_of(blocks[0, 0, n])
            for h in range(heads):
                scores_buf[n, h] = jnp.where(
                    allowed, dot_nt(q[rows, lanes(h)], k[rows, lanes(h)]), 0.0
                ).astype(jnp.bfloat16)
            by_row = jnp.zeros((BLOCK_ROWS, HEAD_SIZE), jnp.float32)
            for h in range(heads):
                core = dot(scores_buf[n, h], v[rows, lanes(h)])
                core = factor * (core + dot_nt(q[rows, lanes(h)], states[n, h]))
                by_row = by_row + g[rows, lanes(h)].astype(jnp.float32) * core
            by_row = jnp.where(live_of(blocks, n), by_row, 0.0)
            partial[0:1, rows_of(n)] = jnp.sum(by_row.T, axis=0, keepdims=True)

    by_role(take_one, body)


def router_side(factor, take_one, loaded, one, two):
    _, blocks, *arrays = loaded
    slots = one.shape[0]
    return pl.pallas_call(
        functools.partial(router_kernel, factor, take_one),
        name="router_side",
        out_shape=jax.ShapeDtypeStruct((1, slots * BLOCK_ROWS), jnp.float32),
        in_specs=[SMEM] + [VMEM] * 6,
        out_specs=VMEM,
        scratch_shapes=[pltpu.VMEM(one.shape, jnp.bfloat16)],
        compiler_params=compiler_params(),
        cost_estimate=cost(3 * slots * one.shape[1], 0),
    )(blocks, *arrays, one, two)


def place_kernel(section_of, begin, *refs):
    chunk, out, sem = refs[-3:]
    rows, width = chunk.shape
    target = out.at[0, section_of(), pl.ds(0, rows), lanes(begin, width // HEAD_SIZE)]
    copy = pltpu.make_async_copy(chunk, target, sem)
    copy.start()
    copy.wait()


def keep_kernel(old, new, *refs):
    del old
    parts, (out, total) = refs[:-2], refs[-2:]
    out[...] = new[...]
    total[...] = folded([part[...] for part in parts])


def third(pairs, tails, partial):
    received = lax.ppermute(tails, ("seq", "pipe"), pairs)
    parts = [partial]
    parts += [from_behind(partial, "tp", -k) for k in range(1, lax.axis_size("tp"))]
    return pl.pallas_call(
        keep_kernel,
        name="keep",
        out_shape=[
            pltpu.VMEM(tails.shape, tails.dtype), pltpu.VMEM(partial.shape, partial.dtype)
        ],
        in_specs=[VMEM] * (2 + len(parts)),
        out_specs=[VMEM] * 2,
        input_output_aliases={0: 0, 2: 1},
        compiler_params=pltpu.CompilerParams(vmem_limit_bytes=2**20),
    )(tails, received, *parts)


def finish_kernel(section, whole, chunk, tails, part, out, total, sem):
    del whole
    rows = chunk.shape[0]
    copies = [
        pltpu.make_async_copy(tails, out.at[0, :, pl.ds(rows, tails.shape[1])], sem.at[0]),
        pltpu.make_async_copy(chunk, out.at[0, section, pl.ds(0, rows)], sem.at[1]),
        pltpu.make_async_copy(part, total, sem.at[2]),
    ]
    for copy in copies:
        copy.start()
    for copy in copies:
        copy.wait()


def finish(section, whole, chunk, tails, total):
    return pl.pallas_call(
        functools.partial(finish_kernel, section),
        name="finish",
        out_shape=[pltpu.HBM(whole.shape, whole.dtype), pltpu.HBM(total.shape, total.dtype)],
        in_specs=[HBM, ANY, ANY, ANY],
        out_specs=[HBM, HBM],
        scratch_shapes=[pltpu.SemaphoreType.DMA((3,))],
        input_output_aliases={0: 0},
        compiler_params=pltpu.CompilerParams(vmem_limit_bytes=2**20),
        cost_estimate=cost(0, 4 * (chunk.size + tails.size)),
    )(whole, chunk, tails, total)


def place(whole, chunk, shape, section_of, begin):
    operands = (chunk,) if whole is None else (whole, chunk)
    return pl.pallas_call(
        functools.partial(place_kernel, section_of, begin),
        name="place",
        out_shape=pltpu.HBM(shape, chunk.dtype),
        in_specs=[HBM] * (len(operands) - 1) + [ANY],
        out_specs=HBM,
        scratch_shapes=[pltpu.SemaphoreType.DMA],
        input_output_aliases={} if whole is None else {0: 0},
        compiler_params=pltpu.CompilerParams(vmem_limit_bytes=2**20),
        cost_estimate=cost(0, 4 * chunk.size),
    )(*operands)


def pick_kernel(*refs):
    infos, out = refs[:-1], refs[-1]
    count = len(infos)
    here = lax.axis_index("pipe")
    both = jnp.bool_(False)
    choice = jnp.int32(0)
    for k, info in enumerate(infos):
        code = jnp.max(info[...])
        section = lax.rem(here + k, count)
        weight = jnp.left_shift(jnp.int32(1), count - 1 - section)
        both = jnp.logical_or(both, code > 1.5)
        choice = choice + jnp.where(code > 0.5, weight, 0)
    out[0, 0] = jnp.where(both, 0, 1 + choice)


def pick(infos):
    return pl.pallas_call(
        pick_kernel,
        name="pick",
        out_shape=pltpu.SMEM((1, 1), jnp.int32),
        in_specs=[VMEM] * len(infos),
        out_specs=SMEM,
        compiler_params=pltpu.CompilerParams(vmem_limit_bytes=2**20),
    )(*infos)


def other_core(pipe_count, by):
    return [
        (s * pipe_count + p, (1 - s) * pipe_count + (p - by) % pipe_count)
        for s in (0, 1) for p in range(pipe_count)
    ]


def third_pairs(pipe_count):
    def pair(s, p):
        return (s * pipe_count + p, s * pipe_count + (p - 1) % pipe_count)

    every = [pair(s, p) for s in (0, 1) for p in range(pipe_count)]
    return [every] + [
        [pair(s, p) for p, s in enumerate(cores)]
        for cores in itertools.product((0, 1), repeat=pipe_count)
    ]


def folded(parts):
    while len(parts) > 1:
        half = len(parts) // 2
        parts = [parts[k] + parts[k + half] for k in range(half)]
    return parts[0]


def shard_states(queries, keys, values, grad_out, router, blocks, counts):
    heads = queries.shape[2] // HEAD_SIZE
    slots = blocks.shape[2]
    shard_blocks = queries.shape[1] // BLOCK_ROWS
    live = jnp.arange(slots, dtype=jnp.int32) < counts[0, 0]
    taken = (blocks[0, 0, :, None] == jnp.arange(shard_blocks, dtype=jnp.int32)) & live[:, None]
    mask = jnp.repeat(jnp.any(taken, axis=0), BLOCK_ROWS)[:, None]

    def rows(array):
        picked = jnp.where(mask, array[0], jnp.zeros((), array.dtype))
        return picked.reshape(-1, heads, HEAD_SIZE)

    weighted = (router[0][:, None, None] * rows(grad_out).astype(jnp.float32)).astype(jnp.bfloat16)
    key_value = jnp.einsum(
        "the,thd->hed", rows(values), rows(keys), preferred_element_type=jnp.float32
    )
    query_grad = jnp.einsum(
        "the,thd->hed", weighted, rows(queries), preferred_element_type=jnp.float32
    )
    return key_value, query_grad


def gathered_gradient(grad_out, router, blocks, counts):
    slots = blocks.shape[2]
    live = jnp.arange(slots, dtype=jnp.int32) < counts[0, 0]
    grouped = grad_out[0].reshape(-1, BLOCK_ROWS, grad_out.shape[2])[blocks[0, 0]]
    weight = jnp.where(live[:, None], router[0].reshape(-1, BLOCK_ROWS)[blocks[0, 0]], 0.0)
    weighted = weight[:, :, None] * grouped.astype(jnp.float32)
    return weighted.astype(jnp.bfloat16).reshape(slots * BLOCK_ROWS, -1)


def fits(seq_count, pipe_count, tp_count, slots):
    return seq_count == 2 and pipe_count <= 4 and tp_count in (1, 2, 4, 8) and slots > 1


def own_side():
    return jnp.where(is_first(), 0, 1)


def other_side():
    return jnp.where(is_first(), 1, 0)


def on_device(queries, keys, values, grad_out, router, blocks, counts):
    slots = blocks.shape[2]
    rows = slots * BLOCK_ROWS
    width = queries.shape[2]
    heads = width // HEAD_SIZE
    seq_count, pipe_count, tp_count = (lax.axis_size(axis) for axis in ("seq", "pipe", "tp"))
    factor = 1.0 / math.sqrt(HEAD_SIZE * rows * seq_count)
    arrays = (queries, keys, values, grad_out)
    shape = (1, 3, rows, width)
    if fits(seq_count, pipe_count, tp_count, slots):
        head_start = max(1, heads // 2)
        small = (in_hbm(router), in_hbm(blocks))
        held = tuple(in_hbm(x) for x in arrays)

        def sent(x, axis="pipe", by=-1):
            return from_behind(x, axis, by)

        def across(x, pairs):
            return lax.ppermute(x, ("seq", "pipe"), pairs)

        def kernel(call, *operands):
            return call(factor, *operands)

        chunk_a, tail_a, *loaded = kernel(opened, is_first, head_start, small, held)
        loaded += [x[0] for x in arrays]
        chunk_a = sent(chunk_a)
        chunk_b, tail_b, own, total, c_all = kernel(side, is_first, head_start, True, loaded)
        total = sent(total, "seq", 1)
        chunk_b = sent(chunk_b)
        chunk_c, tail_c, other, info = kernel(side, is_last, 0, True, loaded, c_all, total)
        chunk_c = sent(chunk_c)
        infos = [info] + [across(info, other_core(pipe_count, k)) for k in range(1, pipe_count)]
        chunk_d, tails = kernel(
            value_side, is_last, loaded, c_all, own, other, (tail_a, tail_b, tail_c)
        )
        chunk_d = sent(chunk_d)
        partial = kernel(router_side, is_first, loaded, own, other)
        choice = pick(infos)[0, 0]

        def branch(pairs, tails, partial, a, b, c):
            handed = place(None, a, shape, own_side, 0)
            handed = place(handed, b, shape, own_side, head_start)
            handed = place(handed, c, shape, other_side, 0)
            return handed, *third(pairs, tails, partial)

        branches = [functools.partial(branch, pairs) for pairs in third_pairs(pipe_count)]
        handed, tails, router_grad = lax.switch(
            choice, branches, tails, partial, chunk_a, chunk_b, chunk_c
        )
        handed, router_grad = finish(2, handed, chunk_d, tails, router_grad)
    else:
        index = lax.axis_index("seq")
        places = jnp.arange(seq_count)[:, None, None, None]
        key_value, query_grad = shard_states(queries, keys, values, grad_out, router, blocks, counts)
        gathered = lax.all_gather(key_value, "seq")
        earlier = jnp.sum(jnp.where(places < index, gathered, 0.0), axis=0)
        gathered = lax.all_gather(query_grad, "seq")
        later = jnp.sum(jnp.where(places > index, gathered, 0.0), axis=0)
        loaded = (router, blocks) + tuple(x[0] for x in arrays)
        c_all = gathered_gradient(grad_out, router, blocks, counts)
        d_query, before = side(factor, always, 0, False, loaded, c_all, earlier)
        d_key, after = side(factor, never, 0, False, loaded, c_all, later)
        (d_value,) = value_side(factor, always, loaded, c_all, after, after)
        partial = router_side(factor, always, loaded, before, before)
        handed = None
        for section, chunk in enumerate((d_query, d_key, d_value)):
            chunk = from_behind(chunk, "pipe", -1)
            handed = place(handed, chunk, shape, functools.partial(int, section), 0)
        router_grad = lax.psum(partial, "tp")
    return (handed, router_grad)


def solution(mesh):
    return jax.shard_map(
        on_device,
        mesh=mesh,
        in_specs=(
            P("pipe", "seq", "tp"),
            P("pipe", "seq", "tp"),
            P("pipe", "seq", "tp"),
            P("pipe", "seq", "tp"),
            P("pipe", "seq"),
            P("pipe", "seq", None),
            P("pipe", "seq"),
        ),
        out_specs=(P("pipe", None, "seq", "tp"), P("pipe", "seq")),
        check_vma=False,
    )
```

```python
import functools
import itertools
import math

import jax
import jax.numpy as jnp
from jax import lax
from jax.experimental import pallas as pl
from jax.experimental.pallas import tpu as pltpu
from jax.sharding import PartitionSpec as P


HEAD_SIZE = 128
BLOCK_ROWS = 128
GRANT = 16 * 2**20
PIECES = 8


ANY = pl.BlockSpec(memory_space=pl.ANY)
HBM = pl.BlockSpec(memory_space=pltpu.HBM)
VMEM = pl.BlockSpec(memory_space=pltpu.VMEM)
SMEM = pl.BlockSpec(memory_space=pltpu.SMEM)


def from_behind(x, axis, by):
    count = lax.axis_size(axis)
    return lax.ppermute(x, axis, [(i, (i + by) % count) for i in range(count)])


def in_hbm(x):
    return pltpu.with_memory_space_constraint(x, pltpu.HBM)


def dot(a, b):
    return jnp.dot(a, b, preferred_element_type=jnp.float32)


def dot_nt(a, b):
    return lax.dot_general(a, b, (((1,), (1,)), ((), ())), preferred_element_type=jnp.float32)


def dot_tn(a, b):
    return lax.dot_general(a, b, (((0,), (0,)), ((), ())), preferred_element_type=jnp.float32)


def lanes(h, count=1):
    return pl.ds(h * HEAD_SIZE, count * HEAD_SIZE)


def rows_of(n):
    if isinstance(n, int):
        return pl.ds(n * BLOCK_ROWS, BLOCK_ROWS)
    return pl.ds(pl.multiple_of(n * BLOCK_ROWS, BLOCK_ROWS), BLOCK_ROWS)


def down_rows(router, block):
    weight = router[0:1, rows_of(block)]
    return jnp.broadcast_to(weight, (BLOCK_ROWS, BLOCK_ROWS)).T


def row_minus_column():
    shape = (BLOCK_ROWS, BLOCK_ROWS)
    return lax.broadcasted_iota(jnp.int32, shape, 0) - lax.broadcasted_iota(jnp.int32, shape, 1)


def compiler_params():
    return pltpu.CompilerParams(vmem_limit_bytes=GRANT)


def cost(matmuls, moved):
    return pl.CostEstimate(
        flops=2 * matmuls * HEAD_SIZE**3, bytes_accessed=moved, transcendentals=0
    )


def is_first():
    return lax.axis_index("seq") == 0


def is_last():
    return lax.axis_index("seq") != 0


def always():
    return True


def never():
    return False


def live_of(blocks, n):
    return jnp.bool_(True) if n == 0 else blocks[0, 0, n] > 0


def by_role(query_side, body):
    flag = query_side()
    if isinstance(flag, bool):
        body(flag)
    else:
        pl.when(flag)(lambda: body(True))
        pl.when(jnp.logical_not(flag))(lambda: body(False))


def in_order(query, slots):
    return list(range(slots)) if query else list(reversed(range(slots)))


def weigh(weight, grad):
    return (weight * grad.astype(jnp.float32)).astype(jnp.bfloat16)


def put_rows(chunk, tail, n, columns, rows):
    if tail is not None and n * BLOCK_ROWS == chunk.shape[0]:
        tail[:, columns] = rows
    else:
        chunk[rows_of(n), columns] = rows


def head_loads(pairs, begin, count, sem):
    return [
        pltpu.make_async_copy(source.at[0, :, lanes(begin, count)], target, sem.at[j])
        for j, (source, target) in enumerate(pairs)
    ]


def open_kernel(
    factor, query_side, end, router, blocks, q, k, v, g, chunk, router_buf, blocks_buf,
    x_buf, v_buf, g_buf, c_buf, scores_buf, states_buf, acc,
    small_sem, load_sem,
):
    slots = blocks.shape[2]
    small = [
        pltpu.make_async_copy(blocks, blocks_buf, small_sem.at[0]),
        pltpu.make_async_copy(router, router_buf, small_sem.at[1]),
    ]
    for copy in small:
        copy.start()
    shared = head_loads(((g, g_buf), (v, v_buf)), 0, end, load_sem)
    rows = q.shape[1] // PIECES

    def start_pieces(source, target, sem):
        for i in range(PIECES):
            at = pl.ds(i * rows, rows)
            pltpu.make_async_copy(
                source.at[0, at, lanes(0, end)], target.at[at], load_sem.at[sem]
            ).start()

    start_pieces(g, g_buf, 0)
    start_pieces(v, v_buf, 1)

    def start(query):
        start_pieces(k if query else q, x_buf, 2)

    by_role(query_side, start)
    difference = row_minus_column()
    for copy in small + shared[:1]:
        copy.wait()

    def body(query):
        allowed = difference >= 0 if query else difference <= 0
        order = in_order(query, slots)
        sent = range(slots - 1)
        for n in sent if query else order:
            block = blocks_buf[0, 0, n]
            weight = jnp.where(live_of(blocks_buf, n), down_rows(router_buf, block), 0.0)
            for h in range(end):
                c_buf[rows_of(n), lanes(h)] = weigh(weight, g_buf[rows_of(block), lanes(h)])
        shared[1].wait()
        pltpu.make_async_copy(k.at[0, :, lanes(0, end)], x_buf, load_sem.at[2]).wait()

        def sides(n, h):
            c_h = c_buf[rows_of(n), lanes(h)]
            v_h = v_buf[rows_of(blocks_buf[0, 0, n]), lanes(h)]
            return (c_h, v_h) if query else (v_h, c_h)

        def x_of(n, h):
            return x_buf[rows_of(blocks_buf[0, 0, n]), lanes(h)]

        for n in sent:
            for h in range(end):
                l_h, r_h = sides(n, h)
                scores_buf[n, h] = jnp.where(allowed, dot_nt(l_h, r_h), 0.0).astype(jnp.bfloat16)
        for i, n in enumerate(order[:-1]):
            if order[i + 1] not in sent:
                break
            for h in range(end):
                added = dot_tn(sides(n, h)[1], x_of(n, h))
                if i > 0:
                    added = acc[h] + added
                acc[h] = added
                states_buf[order[i + 1], h] = added.astype(jnp.bfloat16)
        for i, n in enumerate(order):
            if n not in sent:
                continue
            scale = jnp.where(live_of(blocks_buf, n), factor, 0.0)
            for h in range(end):
                if i == 0:
                    out = dot(scores_buf[n, h], x_of(n, h))
                else:
                    out = dot(
                        jnp.concatenate([scores_buf[n, h], sides(n, h)[0]], axis=1),
                        jnp.concatenate([x_of(n, h), states_buf[n, h]], axis=0),
                    )
                chunk[rows_of(n), lanes(h)] = (scale * out).astype(jnp.bfloat16)

    by_role(query_side, body)


def split_rows(slots, width):
    return [
        pltpu.VMEM(((slots - 1) * BLOCK_ROWS, width), jnp.bfloat16),
        pltpu.VMEM((BLOCK_ROWS, width), jnp.bfloat16),
    ]


def opened(factor, query_side, end, small, arrays):
    router, blocks = small
    _, shard_rows, _ = arrays[0].shape
    slots = blocks.shape[2]
    part = pltpu.VMEM((shard_rows, end * HEAD_SIZE), jnp.bfloat16)
    return pl.pallas_call(
        functools.partial(open_kernel, factor, query_side, end),
        name="opened",
        out_shape=split_rows(slots, end * HEAD_SIZE)[:1]
        + [pltpu.VMEM(router.shape, router.dtype), pltpu.SMEM(blocks.shape, blocks.dtype)],
        in_specs=[HBM] * 6,
        out_specs=[VMEM] * 2 + [SMEM],
        scratch_shapes=[
            part, part, part,
            pltpu.VMEM((slots * BLOCK_ROWS, end * HEAD_SIZE), jnp.bfloat16),
            pltpu.VMEM((slots, end, HEAD_SIZE, HEAD_SIZE), jnp.bfloat16),
            pltpu.VMEM((slots, end, HEAD_SIZE, HEAD_SIZE), jnp.bfloat16),
            pltpu.VMEM((end, HEAD_SIZE, HEAD_SIZE), jnp.float32),
            pltpu.SemaphoreType.DMA((2,)),
            pltpu.SemaphoreType.DMA((3,)),
        ],
        compiler_params=compiler_params(),
        cost_estimate=cost(4 * slots * end, 6 * shard_rows * end * HEAD_SIZE),
    )(router, blocks, *arrays)


def side_kernel(factor, query_side, begin, seeded, split, *refs):
    (router, blocks, q, k, v, g), refs = refs[:6], refs[6:]
    tail = None
    if seeded and split:
        c_all, seed, chunk, tail, states, info, scores_buf, total = refs
    elif seeded:
        c_all, seed, chunk, states, scores_buf, total = refs
    else:
        chunk, tail, states, total, c_all, scores_buf = refs
    slots = blocks.shape[2]
    heads = states.shape[1]
    difference = row_minus_column()

    def body(query):
        allowed = difference >= 0 if query else difference <= 0
        x_all = k if query else q
        order = in_order(query, slots)
        if not seeded:
            for n in order:
                block = blocks[0, 0, n]
                weight = jnp.where(live_of(blocks, n), down_rows(router, block), 0.0)
                for h in range(heads):
                    c_all[rows_of(n), lanes(h)] = weigh(weight, g[rows_of(block), lanes(h)])
        for i, n in enumerate(order):
            live = live_of(blocks, n)
            rows = rows_of(blocks[0, 0, n])
            own = rows_of(n)
            scale = jnp.where(live, factor, 0.0)

            def sides(h):
                c_h, v_h = c_all[own, lanes(h)], v[rows, lanes(h)]
                return (c_h, v_h) if query else (v_h, c_h)

            low = 0 if split and n == slots - 1 else begin
            for h in range(low, heads):
                l_h, r_h = sides(h)
                scores_buf[n, h] = jnp.where(allowed, dot_nt(l_h, r_h), 0.0).astype(jnp.bfloat16)
            for h in range(heads):
                if i > 0:
                    so_far = total[h]
                elif seeded:
                    so_far = seed[h]
                else:
                    so_far = jnp.zeros((HEAD_SIZE, HEAD_SIZE), jnp.float32)
                states[n, h] = so_far.astype(jnp.bfloat16)
                if not seeded or i + 1 < slots:
                    added = dot_tn(sides(h)[1], x_all[rows, lanes(h)])
                    if query and n > 0:
                        added = jnp.where(live, added, 0.0)
                    total[h] = so_far + added
            for h in range(low, heads):
                l_h, _ = sides(h)
                x_h = x_all[rows, lanes(h)]
                if i == 0 and not seeded:
                    out = dot(scores_buf[n, h], x_h)
                else:
                    out = dot(
                        jnp.concatenate([scores_buf[n, h], l_h], axis=1),
                        jnp.concatenate([x_h, states[n, h]], axis=0),
                    )
                out = (scale * out).astype(jnp.bfloat16)
                put_rows(chunk, tail, n, lanes(h - low), out)
        full = jnp.where(live_of(blocks, slots - 1), 1.0, 0.0)
        if not seeded:
            total[heads] = jnp.full((HEAD_SIZE, HEAD_SIZE), full, jnp.float32)
        elif split:
            other = seed[heads, 0:8, :]
            own_full = jnp.full(other.shape, full, jnp.float32)
            info[...] = jnp.where(own_full + other > 1.5, 2.0, own_full if query else other)

    by_role(query_side, body)


def side(factor, query_side, begin, split, arrays, c_all=None, seed=None):
    _, blocks = arrays[:2]
    width = arrays[2].shape[1]
    heads = width // HEAD_SIZE
    slots = blocks.shape[2]
    square = (HEAD_SIZE, HEAD_SIZE)
    out_width = (heads - begin) * HEAD_SIZE
    if split:
        out_shape = [split_rows(slots, out_width)[0], split_rows(slots, width)[1]]
    else:
        out_shape = [pltpu.VMEM((slots * BLOCK_ROWS, out_width), jnp.bfloat16)]
    out_shape.append(pltpu.VMEM((slots, heads) + square, jnp.bfloat16))
    scratch = [pltpu.VMEM((slots, heads) + square, jnp.bfloat16)]
    seeded = seed is not None
    if seeded:
        if split:
            out_shape.append(pltpu.VMEM((8, HEAD_SIZE), jnp.float32))
        scratch.append(pltpu.VMEM((heads,) + square, jnp.float32))
        extra = (c_all, seed)
    else:
        out_shape.append(pltpu.VMEM((heads + 1,) + square, jnp.float32))
        out_shape.append(pltpu.VMEM((slots * BLOCK_ROWS, width), jnp.bfloat16))
        extra = ()
    return pl.pallas_call(
        functools.partial(side_kernel, factor, query_side, begin, seeded, split),
        name="side",
        out_shape=out_shape,
        in_specs=[VMEM, SMEM] + [VMEM] * (4 + len(extra)),
        out_specs=[VMEM] * len(out_shape),
        scratch_shapes=scratch,
        compiler_params=compiler_params(),
        cost_estimate=cost(4 * slots * heads, 0),
    )(*arrays, *extra)


def value_kernel(factor, take_one, split, blocks, q, k, c_all, one, two, *refs):
    if split:
        tail_b, tail_c, chunk, tails, scores_buf = refs
        tail = tails.at[2]
    else:
        chunk, scores_buf = refs
        tail = None
    slots = blocks.shape[2]
    heads = q.shape[1] // HEAD_SIZE
    allowed = row_minus_column() <= 0

    def body(pick):
        states = one if pick else two
        for n in range(slots):
            rows = rows_of(blocks[0, 0, n])
            own = rows_of(n)
            scale = jnp.where(live_of(blocks, n), factor, 0.0)
            for h in range(heads):
                scores_buf[n, h] = jnp.where(
                    allowed, dot_nt(k[rows, lanes(h)], q[rows, lanes(h)]), 0.0
                ).astype(jnp.bfloat16)
            for h in range(heads):
                out = dot(scores_buf[n, h], c_all[own, lanes(h)])
                out = out + dot_nt(k[rows, lanes(h)], states[n, h])
                put_rows(chunk, tail, n, lanes(h), (scale * out).astype(jnp.bfloat16))
        if split:
            tails[1 if pick else 0] = tail_b[...]
            tails[0 if pick else 1] = tail_c[...]

    by_role(take_one, body)


def value_side(factor, take_one, loaded, c_all, one, two, tails=()):
    _, blocks, q, k, _, _ = loaded
    slots, heads = one.shape[:2]
    width = heads * HEAD_SIZE
    split = len(tails) > 0
    if split:
        out_shape = [
            split_rows(slots, width)[0], pltpu.VMEM((3, BLOCK_ROWS, width), jnp.bfloat16)
        ]
    else:
        out_shape = [pltpu.VMEM((slots * BLOCK_ROWS, width), jnp.bfloat16)]
    return pl.pallas_call(
        functools.partial(value_kernel, factor, take_one, split),
        name="value_side",
        out_shape=out_shape,
        in_specs=[SMEM] + [VMEM] * (5 + len(tails)),
        out_specs=[VMEM] * len(out_shape),
        scratch_shapes=[pltpu.VMEM(one.shape, jnp.bfloat16)],
        compiler_params=compiler_params(),
        cost_estimate=cost(3 * slots * heads, 0),
    )(blocks, q, k, c_all, one, two, *tails)


def router_kernel(factor, take_one, blocks, q, k, v, g, one, two, partial, scores_buf):
    slots = blocks.shape[2]
    heads = q.shape[1] // HEAD_SIZE
    allowed = row_minus_column() >= 0

    def body(pick):
        states = one if pick else two
        for n in range(slots):
            rows = rows_of(blocks[0, 0, n])
            for h in range(heads):
                scores_buf[n, h] = jnp.where(
                    allowed, dot_nt(q[rows, lanes(h)], k[rows, lanes(h)]), 0.0
                ).astype(jnp.bfloat16)
            by_row = jnp.zeros((BLOCK_ROWS, HEAD_SIZE), jnp.float32)
            for h in range(heads):
                core = dot(scores_buf[n, h], v[rows, lanes(h)])
                core = factor * (core + dot_nt(q[rows, lanes(h)], states[n, h]))
                by_row = by_row + g[rows, lanes(h)].astype(jnp.float32) * core
            by_row = jnp.where(live_of(blocks, n), by_row, 0.0)
            partial[0:1, rows_of(n)] = jnp.sum(by_row.T, axis=0, keepdims=True)

    by_role(take_one, body)


def router_side(factor, take_one, loaded, one, two):
    _, blocks, *arrays = loaded
    slots = one.shape[0]
    return pl.pallas_call(
        functools.partial(router_kernel, factor, take_one),
        name="router_side",
        out_shape=jax.ShapeDtypeStruct((1, slots * BLOCK_ROWS), jnp.float32),
        in_specs=[SMEM] + [VMEM] * 6,
        out_specs=VMEM,
        scratch_shapes=[pltpu.VMEM(one.shape, jnp.bfloat16)],
        compiler_params=compiler_params(),
        cost_estimate=cost(3 * slots * one.shape[1], 0),
    )(blocks, *arrays, one, two)


def place_kernel(section_of, begin, *refs):
    chunk, out, sem = refs[-3:]
    rows, width = chunk.shape
    target = out.at[0, section_of(), pl.ds(0, rows), lanes(begin, width // HEAD_SIZE)]
    copy = pltpu.make_async_copy(chunk, target, sem)
    copy.start()
    copy.wait()


def keep_kernel(old, new, *refs):
    del old
    parts, (out, total) = refs[:-2], refs[-2:]
    out[...] = new[...]
    total[...] = folded([part[...] for part in parts])


def third(pairs, tails, partial):
    received = lax.ppermute(tails, ("seq", "pipe"), pairs)
    parts = [partial]
    parts += [from_behind(partial, "tp", -k) for k in range(1, lax.axis_size("tp"))]
    return pl.pallas_call(
        keep_kernel,
        name="keep",
        out_shape=[
            pltpu.VMEM(tails.shape, tails.dtype), pltpu.VMEM(partial.shape, partial.dtype)
        ],
        in_specs=[VMEM] * (2 + len(parts)),
        out_specs=[VMEM] * 2,
        input_output_aliases={0: 0, 2: 1},
        compiler_params=pltpu.CompilerParams(vmem_limit_bytes=2**20),
    )(tails, received, *parts)


def finish_kernel(section, whole, chunk, tails, part, out, total, sem):
    del whole
    rows = chunk.shape[0]
    copies = [
        pltpu.make_async_copy(tails, out.at[0, :, pl.ds(rows, tails.shape[1])], sem.at[0]),
        pltpu.make_async_copy(chunk, out.at[0, section, pl.ds(0, rows)], sem.at[1]),
        pltpu.make_async_copy(part, total, sem.at[2]),
    ]
    for copy in copies:
        copy.start()
    for copy in copies:
        copy.wait()


def finish(section, whole, chunk, tails, total):
    return pl.pallas_call(
        functools.partial(finish_kernel, section),
        name="finish",
        out_shape=[pltpu.HBM(whole.shape, whole.dtype), pltpu.HBM(total.shape, total.dtype)],
        in_specs=[HBM, ANY, ANY, ANY],
        out_specs=[HBM, HBM],
        scratch_shapes=[pltpu.SemaphoreType.DMA((3,))],
        input_output_aliases={0: 0},
        compiler_params=pltpu.CompilerParams(vmem_limit_bytes=2**20),
        cost_estimate=cost(0, 4 * (chunk.size + tails.size)),
    )(whole, chunk, tails, total)


def place(whole, chunk, shape, section_of, begin):
    operands = (chunk,) if whole is None else (whole, chunk)
    return pl.pallas_call(
        functools.partial(place_kernel, section_of, begin),
        name="place",
        out_shape=pltpu.HBM(shape, chunk.dtype),
        in_specs=[HBM] * (len(operands) - 1) + [ANY],
        out_specs=HBM,
        scratch_shapes=[pltpu.SemaphoreType.DMA],
        input_output_aliases={} if whole is None else {0: 0},
        compiler_params=pltpu.CompilerParams(vmem_limit_bytes=2**20),
        cost_estimate=cost(0, 4 * chunk.size),
    )(*operands)


def pick_kernel(*refs):
    infos, out = refs[:-1], refs[-1]
    count = len(infos)
    here = lax.axis_index("pipe")
    both = jnp.bool_(False)
    choice = jnp.int32(0)
    for k, info in enumerate(infos):
        code = jnp.max(info[...])
        section = lax.rem(here + k, count)
        weight = jnp.left_shift(jnp.int32(1), count - 1 - section)
        both = jnp.logical_or(both, code > 1.5)
        choice = choice + jnp.where(code > 0.5, weight, 0)
    out[0, 0] = jnp.where(both, 0, 1 + choice)


def pick(infos):
    return pl.pallas_call(
        pick_kernel,
        name="pick",
        out_shape=pltpu.SMEM((1, 1), jnp.int32),
        in_specs=[VMEM] * len(infos),
        out_specs=SMEM,
        compiler_params=pltpu.CompilerParams(vmem_limit_bytes=2**20),
    )(*infos)


def other_core(pipe_count, by):
    return [
        (s * pipe_count + p, (1 - s) * pipe_count + (p - by) % pipe_count)
        for s in (0, 1) for p in range(pipe_count)
    ]


def third_pairs(pipe_count):
    def pair(s, p):
        return (s * pipe_count + p, s * pipe_count + (p - 1) % pipe_count)

    every = [pair(s, p) for s in (0, 1) for p in range(pipe_count)]
    return [every] + [
        [pair(s, p) for p, s in enumerate(cores)]
        for cores in itertools.product((0, 1), repeat=pipe_count)
    ]


def folded(parts):
    while len(parts) > 1:
        half = len(parts) // 2
        parts = [parts[k] + parts[k + half] for k in range(half)]
    return parts[0]


def shard_states(queries, keys, values, grad_out, router, blocks, counts):
    heads = queries.shape[2] // HEAD_SIZE
    slots = blocks.shape[2]
    shard_blocks = queries.shape[1] // BLOCK_ROWS
    live = jnp.arange(slots, dtype=jnp.int32) < counts[0, 0]
    taken = (blocks[0, 0, :, None] == jnp.arange(shard_blocks, dtype=jnp.int32)) & live[:, None]
    mask = jnp.repeat(jnp.any(taken, axis=0), BLOCK_ROWS)[:, None]

    def rows(array):
        picked = jnp.where(mask, array[0], jnp.zeros((), array.dtype))
        return picked.reshape(-1, heads, HEAD_SIZE)

    weighted = (router[0][:, None, None] * rows(grad_out).astype(jnp.float32)).astype(jnp.bfloat16)
    key_value = jnp.einsum(
        "the,thd->hed", rows(values), rows(keys), preferred_element_type=jnp.float32
    )
    query_grad = jnp.einsum(
        "the,thd->hed", weighted, rows(queries), preferred_element_type=jnp.float32
    )
    return key_value, query_grad


def gathered_gradient(grad_out, router, blocks, counts):
    slots = blocks.shape[2]
    live = jnp.arange(slots, dtype=jnp.int32) < counts[0, 0]
    grouped = grad_out[0].reshape(-1, BLOCK_ROWS, grad_out.shape[2])[blocks[0, 0]]
    weight = jnp.where(live[:, None], router[0].reshape(-1, BLOCK_ROWS)[blocks[0, 0]], 0.0)
    weighted = weight[:, :, None] * grouped.astype(jnp.float32)
    return weighted.astype(jnp.bfloat16).reshape(slots * BLOCK_ROWS, -1)


def fits(seq_count, pipe_count, tp_count, slots):
    return seq_count == 2 and pipe_count <= 4 and tp_count in (1, 2, 4, 8) and slots > 1


def own_side():
    return jnp.where(is_first(), 0, 1)


def other_side():
    return jnp.where(is_first(), 1, 0)


def on_device(queries, keys, values, grad_out, router, blocks, counts):
    slots = blocks.shape[2]
    rows = slots * BLOCK_ROWS
    width = queries.shape[2]
    heads = width // HEAD_SIZE
    seq_count, pipe_count, tp_count = (lax.axis_size(axis) for axis in ("seq", "pipe", "tp"))
    factor = 1.0 / math.sqrt(HEAD_SIZE * rows * seq_count)
    arrays = (queries, keys, values, grad_out)
    shape = (1, 3, rows, width)
    if fits(seq_count, pipe_count, tp_count, slots):
        head_start = max(1, heads // 2)
        small = (in_hbm(router), in_hbm(blocks))
        held = tuple(in_hbm(x) for x in arrays)

        def sent(x, axis="pipe", by=-1):
            return from_behind(x, axis, by)

        def across(x, pairs):
            return lax.ppermute(x, ("seq", "pipe"), pairs)

        def kernel(call, *operands):
            return call(factor, *operands)

        chunk_a, *loaded = kernel(opened, is_first, head_start, small, held)
        loaded += [x[0] for x in arrays]
        chunk_a = sent(chunk_a)
        chunk_b, tail_b, own, total, c_all = kernel(side, is_first, head_start, True, loaded)
        total = sent(total, "seq", 1)
        chunk_b = sent(chunk_b)
        chunk_c, tail_c, other, info = kernel(side, is_last, 0, True, loaded, c_all, total)
        chunk_c = sent(chunk_c)
        infos = [info] + [across(info, other_core(pipe_count, k)) for k in range(1, pipe_count)]
        chunk_d, tails = kernel(value_side, is_last, loaded, c_all, own, other, (tail_b, tail_c))
        chunk_d = sent(chunk_d)
        partial = kernel(router_side, is_first, loaded, own, other)
        choice = pick(infos)[0, 0]

        def branch(pairs, tails, partial, a, b, c):
            handed = place(None, a, shape, own_side, 0)
            handed = place(handed, b, shape, own_side, head_start)
            handed = place(handed, c, shape, other_side, 0)
            return handed, *third(pairs, tails, partial)

        branches = [functools.partial(branch, pairs) for pairs in third_pairs(pipe_count)]
        handed, tails, router_grad = lax.switch(
            choice, branches, tails, partial, chunk_a, chunk_b, chunk_c
        )
        handed, router_grad = finish(2, handed, chunk_d, tails, router_grad)
    else:
        index = lax.axis_index("seq")
        places = jnp.arange(seq_count)[:, None, None, None]
        key_value, query_grad = shard_states(queries, keys, values, grad_out, router, blocks, counts)
        gathered = lax.all_gather(key_value, "seq")
        earlier = jnp.sum(jnp.where(places < index, gathered, 0.0), axis=0)
        gathered = lax.all_gather(query_grad, "seq")
        later = jnp.sum(jnp.where(places > index, gathered, 0.0), axis=0)
        loaded = (router, blocks) + tuple(x[0] for x in arrays)
        c_all = gathered_gradient(grad_out, router, blocks, counts)
        d_query, before = side(factor, always, 0, False, loaded, c_all, earlier)
        d_key, after = side(factor, never, 0, False, loaded, c_all, later)
        (d_value,) = value_side(factor, always, loaded, c_all, after, after)
        partial = router_side(factor, always, loaded, before, before)
        handed = None
        for section, chunk in enumerate((d_query, d_key, d_value)):
            chunk = from_behind(chunk, "pipe", -1)
            handed = place(handed, chunk, shape, functools.partial(int, section), 0)
        router_grad = lax.psum(partial, "tp")
    return (handed, router_grad)


def solution(mesh):
    return jax.shard_map(
        on_device,
        mesh=mesh,
        in_specs=(
            P("pipe", "seq", "tp"),
            P("pipe", "seq", "tp"),
            P("pipe", "seq", "tp"),
            P("pipe", "seq", "tp"),
            P("pipe", "seq"),
            P("pipe", "seq", None),
            P("pipe", "seq"),
        ),
        out_specs=(P("pipe", None, "seq", "tp"), P("pipe", "seq")),
        check_vma=False,
    )
```

```python
import functools
import itertools
import math

import jax
import jax.numpy as jnp
from jax import lax
from jax.experimental import pallas as pl
from jax.experimental.pallas import tpu as pltpu
from jax.sharding import PartitionSpec as P


HEAD_SIZE = 128
BLOCK_ROWS = 128
GRANT = 16 * 2**20
PIECES = 8


ANY = pl.BlockSpec(memory_space=pl.ANY)
HBM = pl.BlockSpec(memory_space=pltpu.HBM)
VMEM = pl.BlockSpec(memory_space=pltpu.VMEM)
SMEM = pl.BlockSpec(memory_space=pltpu.SMEM)


def from_behind(x, axis, by):
    count = lax.axis_size(axis)
    return lax.ppermute(x, axis, [(i, (i + by) % count) for i in range(count)])


def in_hbm(x):
    return pltpu.with_memory_space_constraint(x, pltpu.HBM)


def dot(a, b):
    return jnp.dot(a, b, preferred_element_type=jnp.float32)


def dot_nt(a, b):
    return lax.dot_general(a, b, (((1,), (1,)), ((), ())), preferred_element_type=jnp.float32)


def dot_tn(a, b):
    return lax.dot_general(a, b, (((0,), (0,)), ((), ())), preferred_element_type=jnp.float32)


def lanes(h, count=1):
    return pl.ds(h * HEAD_SIZE, count * HEAD_SIZE)


def rows_of(n):
    if isinstance(n, int):
        return pl.ds(n * BLOCK_ROWS, BLOCK_ROWS)
    return pl.ds(pl.multiple_of(n * BLOCK_ROWS, BLOCK_ROWS), BLOCK_ROWS)


def down_rows(router, block):
    weight = router[0:1, rows_of(block)]
    return jnp.broadcast_to(weight, (BLOCK_ROWS, BLOCK_ROWS)).T


def row_minus_column():
    shape = (BLOCK_ROWS, BLOCK_ROWS)
    return lax.broadcasted_iota(jnp.int32, shape, 0) - lax.broadcasted_iota(jnp.int32, shape, 1)


def compiler_params():
    return pltpu.CompilerParams(vmem_limit_bytes=GRANT)


def cost(matmuls, moved):
    return pl.CostEstimate(
        flops=2 * matmuls * HEAD_SIZE**3, bytes_accessed=moved, transcendentals=0
    )


def is_first():
    return lax.axis_index("seq") == 0


def is_last():
    return lax.axis_index("seq") != 0


def always():
    return True


def never():
    return False


def live_of(blocks, n):
    return jnp.bool_(True) if n == 0 else blocks[0, 0, n] > 0


def by_role(query_side, body):
    flag = query_side()
    if isinstance(flag, bool):
        body(flag)
    else:
        pl.when(flag)(lambda: body(True))
        pl.when(jnp.logical_not(flag))(lambda: body(False))


def in_order(query, slots):
    return list(range(slots)) if query else list(reversed(range(slots)))


def weigh(weight, grad):
    return (weight * grad.astype(jnp.float32)).astype(jnp.bfloat16)


def put_rows(chunk, tail, n, columns, rows):
    if chunk is None or (tail is not None and n * BLOCK_ROWS == chunk.shape[0]):
        tail[:, columns] = rows
    else:
        chunk[rows_of(n), columns] = rows


def head_loads(pairs, begin, count, sem):
    return [
        pltpu.make_async_copy(source.at[0, :, lanes(begin, count)], target, sem.at[j])
        for j, (source, target) in enumerate(pairs)
    ]


def open_kernel(
    factor, query_side, end, router, blocks, q, k, v, g, chunk, router_buf, blocks_buf,
    x_buf, v_buf, g_buf, c_buf, scores_buf, states_buf, acc,
    small_sem, load_sem,
):
    slots = blocks.shape[2]
    small = [
        pltpu.make_async_copy(blocks, blocks_buf, small_sem.at[0]),
        pltpu.make_async_copy(router, router_buf, small_sem.at[1]),
    ]
    for copy in small:
        copy.start()
    shared = head_loads(((g, g_buf), (v, v_buf)), 0, end, load_sem)
    rows = q.shape[1] // PIECES

    def start_pieces(source, target, sem):
        for i in range(PIECES):
            at = pl.ds(i * rows, rows)
            pltpu.make_async_copy(
                source.at[0, at, lanes(0, end)], target.at[at], load_sem.at[sem]
            ).start(priority=1)

    start_pieces(g, g_buf, 0)
    start_pieces(v, v_buf, 1)

    def start(query):
        start_pieces(k if query else q, x_buf, 2)

    by_role(query_side, start)
    difference = row_minus_column()
    for copy in small + shared[:1]:
        copy.wait()

    def body(query):
        allowed = difference >= 0 if query else difference <= 0
        order = in_order(query, slots)
        sent = range(slots - 1)
        for n in sent if query else order:
            block = blocks_buf[0, 0, n]
            weight = jnp.where(live_of(blocks_buf, n), down_rows(router_buf, block), 0.0)
            for h in range(end):
                c_buf[rows_of(n), lanes(h)] = weigh(weight, g_buf[rows_of(block), lanes(h)])
        shared[1].wait()
        pltpu.make_async_copy(k.at[0, :, lanes(0, end)], x_buf, load_sem.at[2]).wait()

        def sides(n, h):
            c_h = c_buf[rows_of(n), lanes(h)]
            v_h = v_buf[rows_of(blocks_buf[0, 0, n]), lanes(h)]
            return (c_h, v_h) if query else (v_h, c_h)

        def x_of(n, h):
            return x_buf[rows_of(blocks_buf[0, 0, n]), lanes(h)]

        for n in sent:
            for h in range(end):
                l_h, r_h = sides(n, h)
                scores_buf[n, h] = jnp.where(allowed, dot_nt(l_h, r_h), 0.0).astype(jnp.bfloat16)
        for i, n in enumerate(order[:-1]):
            if order[i + 1] not in sent:
                break
            for h in range(end):
                added = dot_tn(sides(n, h)[1], x_of(n, h))
                if i > 0:
                    added = acc[h] + added
                acc[h] = added
                states_buf[order[i + 1], h] = added.astype(jnp.bfloat16)
        for i, n in enumerate(order):
            if n not in sent:
                continue
            scale = jnp.where(live_of(blocks_buf, n), factor, 0.0)
            for h in range(end):
                if i == 0:
                    out = dot(scores_buf[n, h], x_of(n, h))
                else:
                    out = dot(
                        jnp.concatenate([scores_buf[n, h], sides(n, h)[0]], axis=1),
                        jnp.concatenate([x_of(n, h), states_buf[n, h]], axis=0),
                    )
                chunk[rows_of(n), lanes(h)] = (scale * out).astype(jnp.bfloat16)

    by_role(query_side, body)


def split_rows(slots, width):
    return [
        pltpu.VMEM(((slots - 1) * BLOCK_ROWS, width), jnp.bfloat16),
        pltpu.VMEM((BLOCK_ROWS, width), jnp.bfloat16),
    ]


def opened(factor, query_side, end, small, arrays):
    router, blocks = small
    _, shard_rows, _ = arrays[0].shape
    slots = blocks.shape[2]
    part = pltpu.VMEM((shard_rows, end * HEAD_SIZE), jnp.bfloat16)
    return pl.pallas_call(
        functools.partial(open_kernel, factor, query_side, end),
        name="opened",
        out_shape=split_rows(slots, end * HEAD_SIZE)[:1]
        + [pltpu.VMEM(router.shape, router.dtype), pltpu.SMEM(blocks.shape, blocks.dtype)],
        in_specs=[HBM] * 6,
        out_specs=[VMEM] * 2 + [SMEM],
        scratch_shapes=[
            part, part, part,
            pltpu.VMEM((slots * BLOCK_ROWS, end * HEAD_SIZE), jnp.bfloat16),
            pltpu.VMEM((slots, end, HEAD_SIZE, HEAD_SIZE), jnp.bfloat16),
            pltpu.VMEM((slots, end, HEAD_SIZE, HEAD_SIZE), jnp.bfloat16),
            pltpu.VMEM((end, HEAD_SIZE, HEAD_SIZE), jnp.float32),
            pltpu.SemaphoreType.DMA((2,)),
            pltpu.SemaphoreType.DMA((3,)),
        ],
        compiler_params=compiler_params(),
        cost_estimate=cost(4 * slots * end, 6 * shard_rows * end * HEAD_SIZE),
    )(router, blocks, *arrays)


def rest_kernel(
    factor, query_side, begin, router, blocks, q, k, v, g, chunk,
    c_buf, scores_buf, states_buf, acc,
):
    slots = blocks.shape[2]
    end = acc.shape[0]
    difference = row_minus_column()

    def body(query):
        allowed = difference >= 0 if query else difference <= 0
        x_all = k if query else q
        order = in_order(query, slots)
        sent = range(slots - 1)
        for n in sent if query else order:
            block = blocks[0, 0, n]
            weight = jnp.where(live_of(blocks, n), down_rows(router, block), 0.0)
            for h in range(end):
                c_buf[rows_of(n), lanes(h)] = weigh(weight, g[rows_of(block), lanes(begin + h)])

        def sides(n, h):
            c_h = c_buf[rows_of(n), lanes(h)]
            v_h = v[rows_of(blocks[0, 0, n]), lanes(begin + h)]
            return (c_h, v_h) if query else (v_h, c_h)

        def x_of(n, h):
            return x_all[rows_of(blocks[0, 0, n]), lanes(begin + h)]

        for n in sent:
            for h in range(end):
                l_h, r_h = sides(n, h)
                scores_buf[n, h] = jnp.where(allowed, dot_nt(l_h, r_h), 0.0).astype(jnp.bfloat16)
        for i, n in enumerate(order[:-1]):
            if order[i + 1] not in sent:
                break
            for h in range(end):
                added = dot_tn(sides(n, h)[1], x_of(n, h))
                if i > 0:
                    added = acc[h] + added
                acc[h] = added
                states_buf[order[i + 1], h] = added.astype(jnp.bfloat16)
        for i, n in enumerate(order):
            if n not in sent:
                continue
            scale = jnp.where(live_of(blocks, n), factor, 0.0)
            for h in range(end):
                if i == 0:
                    out = dot(scores_buf[n, h], x_of(n, h))
                else:
                    out = dot(
                        jnp.concatenate([scores_buf[n, h], sides(n, h)[0]], axis=1),
                        jnp.concatenate([x_of(n, h), states_buf[n, h]], axis=0),
                    )
                chunk[rows_of(n), lanes(h)] = (scale * out).astype(jnp.bfloat16)

    by_role(query_side, body)


def rest(factor, query_side, begin, loaded):
    blocks = loaded[1]
    slots = blocks.shape[2]
    span = loaded[2].shape[1] // HEAD_SIZE - begin
    return pl.pallas_call(
        functools.partial(rest_kernel, factor, query_side, begin),
        name="rest",
        out_shape=split_rows(slots, span * HEAD_SIZE)[0],
        in_specs=[VMEM, SMEM] + [VMEM] * 4,
        out_specs=VMEM,
        scratch_shapes=[
            pltpu.VMEM((slots * BLOCK_ROWS, span * HEAD_SIZE), jnp.bfloat16),
            pltpu.VMEM((slots, span, HEAD_SIZE, HEAD_SIZE), jnp.bfloat16),
            pltpu.VMEM((slots, span, HEAD_SIZE, HEAD_SIZE), jnp.bfloat16),
            pltpu.VMEM((span, HEAD_SIZE, HEAD_SIZE), jnp.float32),
        ],
        compiler_params=compiler_params(),
        cost_estimate=cost(4 * slots * span, 0),
    )(*loaded)


def side_kernel(factor, query_side, begin, seeded, split, *refs):
    (router, blocks, q, k, v, g), refs = refs[:6], refs[6:]
    tail = None
    if begin * HEAD_SIZE == q.shape[1]:
        refs = (None,) + refs
    if seeded and split:
        c_all, seed, chunk, tail, states, info, scores_buf, total = refs
    elif seeded:
        c_all, seed, chunk, states, scores_buf, total = refs
    else:
        chunk, tail, states, total, c_all, scores_buf = refs
    slots = blocks.shape[2]
    heads = states.shape[1]
    difference = row_minus_column()

    def body(query):
        allowed = difference >= 0 if query else difference <= 0
        x_all = k if query else q
        order = in_order(query, slots)
        if not seeded:
            for n in order:
                block = blocks[0, 0, n]
                weight = jnp.where(live_of(blocks, n), down_rows(router, block), 0.0)
                for h in range(heads):
                    c_all[rows_of(n), lanes(h)] = weigh(weight, g[rows_of(block), lanes(h)])
        for i, n in enumerate(order):
            live = live_of(blocks, n)
            rows = rows_of(blocks[0, 0, n])
            own = rows_of(n)
            scale = jnp.where(live, factor, 0.0)

            def sides(h):
                c_h, v_h = c_all[own, lanes(h)], v[rows, lanes(h)]
                return (c_h, v_h) if query else (v_h, c_h)

            low = 0 if split and n == slots - 1 else begin
            for h in range(low, heads):
                l_h, r_h = sides(h)
                scores_buf[n, h] = jnp.where(allowed, dot_nt(l_h, r_h), 0.0).astype(jnp.bfloat16)
            for h in range(heads):
                if i > 0:
                    so_far = total[h]
                elif seeded:
                    so_far = seed[h]
                else:
                    so_far = jnp.zeros((HEAD_SIZE, HEAD_SIZE), jnp.float32)
                states[n, h] = so_far.astype(jnp.bfloat16)
                if not seeded or i + 1 < slots:
                    added = dot_tn(sides(h)[1], x_all[rows, lanes(h)])
                    if query and n > 0:
                        added = jnp.where(live, added, 0.0)
                    total[h] = so_far + added
            for h in range(low, heads):
                l_h, _ = sides(h)
                x_h = x_all[rows, lanes(h)]
                if i == 0 and not seeded:
                    out = dot(scores_buf[n, h], x_h)
                else:
                    out = dot(
                        jnp.concatenate([scores_buf[n, h], l_h], axis=1),
                        jnp.concatenate([x_h, states[n, h]], axis=0),
                    )
                out = (scale * out).astype(jnp.bfloat16)
                put_rows(chunk, tail, n, lanes(h - low), out)
        full = jnp.where(live_of(blocks, slots - 1), 1.0, 0.0)
        if not seeded:
            total[heads] = jnp.full((HEAD_SIZE, HEAD_SIZE), full, jnp.float32)
        elif split:
            other = seed[heads, 0:8, :]
            own_full = jnp.full(other.shape, full, jnp.float32)
            info[...] = jnp.where(own_full + other > 1.5, 2.0, own_full if query else other)

    by_role(query_side, body)


def side(factor, query_side, begin, split, arrays, c_all=None, seed=None):
    _, blocks = arrays[:2]
    width = arrays[2].shape[1]
    heads = width // HEAD_SIZE
    slots = blocks.shape[2]
    square = (HEAD_SIZE, HEAD_SIZE)
    out_width = (heads - begin) * HEAD_SIZE
    if split:
        out_shape = [split_rows(slots, out_width)[0]] if begin < heads else []
        out_shape.append(split_rows(slots, width)[1])
    else:
        out_shape = [pltpu.VMEM((slots * BLOCK_ROWS, out_width), jnp.bfloat16)]
    out_shape.append(pltpu.VMEM((slots, heads) + square, jnp.bfloat16))
    scratch = [pltpu.VMEM((slots, heads) + square, jnp.bfloat16)]
    seeded = seed is not None
    if seeded:
        if split:
            out_shape.append(pltpu.VMEM((8, HEAD_SIZE), jnp.float32))
        scratch.append(pltpu.VMEM((heads,) + square, jnp.float32))
        extra = (c_all, seed)
    else:
        out_shape.append(pltpu.VMEM((heads + 1,) + square, jnp.float32))
        out_shape.append(pltpu.VMEM((slots * BLOCK_ROWS, width), jnp.bfloat16))
        extra = ()
    return pl.pallas_call(
        functools.partial(side_kernel, factor, query_side, begin, seeded, split),
        name="side",
        out_shape=out_shape,
        in_specs=[VMEM, SMEM] + [VMEM] * (4 + len(extra)),
        out_specs=[VMEM] * len(out_shape),
        scratch_shapes=scratch,
        compiler_params=compiler_params(),
        cost_estimate=cost(4 * slots * heads, 0),
    )(*arrays, *extra)


def value_kernel(factor, take_one, split, blocks, q, k, c_all, one, two, *refs):
    if split:
        tail_b, tail_c, chunk, tails, scores_buf = refs
        tail = tails.at[2]
    else:
        chunk, scores_buf = refs
        tail = None
    slots = blocks.shape[2]
    heads = q.shape[1] // HEAD_SIZE
    allowed = row_minus_column() <= 0

    def body(pick):
        states = one if pick else two
        for n in range(slots):
            rows = rows_of(blocks[0, 0, n])
            own = rows_of(n)
            scale = jnp.where(live_of(blocks, n), factor, 0.0)
            for h in range(heads):
                scores_buf[n, h] = jnp.where(
                    allowed, dot_nt(k[rows, lanes(h)], q[rows, lanes(h)]), 0.0
                ).astype(jnp.bfloat16)
            for h in range(heads):
                out = dot(scores_buf[n, h], c_all[own, lanes(h)])
                out = out + dot_nt(k[rows, lanes(h)], states[n, h])
                put_rows(chunk, tail, n, lanes(h), (scale * out).astype(jnp.bfloat16))
        if split:
            tails[1 if pick else 0] = tail_b[...]
            tails[0 if pick else 1] = tail_c[...]

    by_role(take_one, body)


def value_side(factor, take_one, loaded, c_all, one, two, tails=()):
    _, blocks, q, k, _, _ = loaded
    slots, heads = one.shape[:2]
    width = heads * HEAD_SIZE
    split = len(tails) > 0
    if split:
        out_shape = [
            split_rows(slots, width)[0], pltpu.VMEM((3, BLOCK_ROWS, width), jnp.bfloat16)
        ]
    else:
        out_shape = [pltpu.VMEM((slots * BLOCK_ROWS, width), jnp.bfloat16)]
    return pl.pallas_call(
        functools.partial(value_kernel, factor, take_one, split),
        name="value_side",
        out_shape=out_shape,
        in_specs=[SMEM] + [VMEM] * (5 + len(tails)),
        out_specs=[VMEM] * len(out_shape),
        scratch_shapes=[pltpu.VMEM(one.shape, jnp.bfloat16)],
        compiler_params=compiler_params(),
        cost_estimate=cost(3 * slots * heads, 0),
    )(blocks, q, k, c_all, one, two, *tails)


def router_kernel(factor, take_one, blocks, q, k, v, g, one, two, partial, scores_buf):
    slots = blocks.shape[2]
    heads = q.shape[1] // HEAD_SIZE
    allowed = row_minus_column() >= 0

    def body(pick):
        states = one if pick else two
        for n in range(slots):
            rows = rows_of(blocks[0, 0, n])
            for h in range(heads):
                scores_buf[n, h] = jnp.where(
                    allowed, dot_nt(q[rows, lanes(h)], k[rows, lanes(h)]), 0.0
                ).astype(jnp.bfloat16)
            by_row = jnp.zeros((BLOCK_ROWS, HEAD_SIZE), jnp.float32)
            for h in range(heads):
                core = dot(scores_buf[n, h], v[rows, lanes(h)])
                core = factor * (core + dot_nt(q[rows, lanes(h)], states[n, h]))
                by_row = by_row + g[rows, lanes(h)].astype(jnp.float32) * core
            by_row = jnp.where(live_of(blocks, n), by_row, 0.0)
            partial[0:1, rows_of(n)] = jnp.sum(by_row.T, axis=0, keepdims=True)

    by_role(take_one, body)


def router_side(factor, take_one, loaded, one, two):
    _, blocks, *arrays = loaded
    slots = one.shape[0]
    return pl.pallas_call(
        functools.partial(router_kernel, factor, take_one),
        name="router_side",
        out_shape=jax.ShapeDtypeStruct((1, slots * BLOCK_ROWS), jnp.float32),
        in_specs=[SMEM] + [VMEM] * 6,
        out_specs=VMEM,
        scratch_shapes=[pltpu.VMEM(one.shape, jnp.bfloat16)],
        compiler_params=compiler_params(),
        cost_estimate=cost(3 * slots * one.shape[1], 0),
    )(blocks, *arrays, one, two)


def place_kernel(section_of, begin, *refs):
    chunk, out, sem = refs[-3:]
    rows, width = chunk.shape
    target = out.at[0, section_of(), pl.ds(0, rows), lanes(begin, width // HEAD_SIZE)]
    copy = pltpu.make_async_copy(chunk, target, sem)
    copy.start()
    copy.wait()


def keep_kernel(old, new, *refs):
    del old
    parts, (out, total) = refs[:-2], refs[-2:]
    out[...] = new[...]
    total[...] = folded([part[...] for part in parts])


def third(pairs, tails, partial):
    received = lax.ppermute(tails, ("seq", "pipe"), pairs)
    parts = [partial]
    parts += [from_behind(partial, "tp", -k) for k in range(1, lax.axis_size("tp"))]
    return pl.pallas_call(
        keep_kernel,
        name="keep",
        out_shape=[
            pltpu.VMEM(tails.shape, tails.dtype), pltpu.VMEM(partial.shape, partial.dtype)
        ],
        in_specs=[VMEM] * (2 + len(parts)),
        out_specs=[VMEM] * 2,
        input_output_aliases={0: 0, 2: 1},
        compiler_params=pltpu.CompilerParams(vmem_limit_bytes=2**20),
    )(tails, received, *parts)


def finish_kernel(section, whole, chunk, tails, part, out, total, sem):
    del whole
    rows = chunk.shape[0]
    copies = [
        pltpu.make_async_copy(tails, out.at[0, :, pl.ds(rows, tails.shape[1])], sem.at[0]),
        pltpu.make_async_copy(chunk, out.at[0, section, pl.ds(0, rows)], sem.at[1]),
        pltpu.make_async_copy(part, total, sem.at[2]),
    ]
    for copy in copies:
        copy.start()
    for copy in copies:
        copy.wait()


def finish(section, whole, chunk, tails, total):
    return pl.pallas_call(
        functools.partial(finish_kernel, section),
        name="finish",
        out_shape=[pltpu.HBM(whole.shape, whole.dtype), pltpu.HBM(total.shape, total.dtype)],
        in_specs=[HBM, ANY, ANY, ANY],
        out_specs=[HBM, HBM],
        scratch_shapes=[pltpu.SemaphoreType.DMA((3,))],
        input_output_aliases={0: 0},
        compiler_params=pltpu.CompilerParams(vmem_limit_bytes=2**20),
        cost_estimate=cost(0, 4 * (chunk.size + tails.size)),
    )(whole, chunk, tails, total)


def place(whole, chunk, shape, section_of, begin):
    operands = (chunk,) if whole is None else (whole, chunk)
    return pl.pallas_call(
        functools.partial(place_kernel, section_of, begin),
        name="place",
        out_shape=pltpu.HBM(shape, chunk.dtype),
        in_specs=[HBM] * (len(operands) - 1) + [ANY],
        out_specs=HBM,
        scratch_shapes=[pltpu.SemaphoreType.DMA],
        input_output_aliases={} if whole is None else {0: 0},
        compiler_params=pltpu.CompilerParams(vmem_limit_bytes=2**20),
        cost_estimate=cost(0, 4 * chunk.size),
    )(*operands)


def pick_kernel(*refs):
    infos, out = refs[:-1], refs[-1]
    count = len(infos)
    here = lax.axis_index("pipe")
    both = jnp.bool_(False)
    choice = jnp.int32(0)
    for k, info in enumerate(infos):
        code = jnp.max(info[...])
        section = lax.rem(here + k, count)
        weight = jnp.left_shift(jnp.int32(1), count - 1 - section)
        both = jnp.logical_or(both, code > 1.5)
        choice = choice + jnp.where(code > 0.5, weight, 0)
    out[0, 0] = jnp.where(both, 0, 1 + choice)


def pick(infos):
    return pl.pallas_call(
        pick_kernel,
        name="pick",
        out_shape=pltpu.SMEM((1, 1), jnp.int32),
        in_specs=[VMEM] * len(infos),
        out_specs=SMEM,
        compiler_params=pltpu.CompilerParams(vmem_limit_bytes=2**20),
    )(*infos)


def other_core(pipe_count, by):
    return [
        (s * pipe_count + p, (1 - s) * pipe_count + (p - by) % pipe_count)
        for s in (0, 1) for p in range(pipe_count)
    ]


def third_pairs(pipe_count):
    def pair(s, p):
        return (s * pipe_count + p, s * pipe_count + (p - 1) % pipe_count)

    every = [pair(s, p) for s in (0, 1) for p in range(pipe_count)]
    return [every] + [
        [pair(s, p) for p, s in enumerate(cores)]
        for cores in itertools.product((0, 1), repeat=pipe_count)
    ]


def folded(parts):
    while len(parts) > 1:
        half = len(parts) // 2
        parts = [parts[k] + parts[k + half] for k in range(half)]
    return parts[0]


def shard_states(queries, keys, values, grad_out, router, blocks, counts):
    heads = queries.shape[2] // HEAD_SIZE
    slots = blocks.shape[2]
    shard_blocks = queries.shape[1] // BLOCK_ROWS
    live = jnp.arange(slots, dtype=jnp.int32) < counts[0, 0]
    taken = (blocks[0, 0, :, None] == jnp.arange(shard_blocks, dtype=jnp.int32)) & live[:, None]
    mask = jnp.repeat(jnp.any(taken, axis=0), BLOCK_ROWS)[:, None]

    def rows(array):
        picked = jnp.where(mask, array[0], jnp.zeros((), array.dtype))
        return picked.reshape(-1, heads, HEAD_SIZE)

    weighted = (router[0][:, None, None] * rows(grad_out).astype(jnp.float32)).astype(jnp.bfloat16)
    key_value = jnp.einsum(
        "the,thd->hed", rows(values), rows(keys), preferred_element_type=jnp.float32
    )
    query_grad = jnp.einsum(
        "the,thd->hed", weighted, rows(queries), preferred_element_type=jnp.float32
    )
    return key_value, query_grad


def gathered_gradient(grad_out, router, blocks, counts):
    slots = blocks.shape[2]
    live = jnp.arange(slots, dtype=jnp.int32) < counts[0, 0]
    grouped = grad_out[0].reshape(-1, BLOCK_ROWS, grad_out.shape[2])[blocks[0, 0]]
    weight = jnp.where(live[:, None], router[0].reshape(-1, BLOCK_ROWS)[blocks[0, 0]], 0.0)
    weighted = weight[:, :, None] * grouped.astype(jnp.float32)
    return weighted.astype(jnp.bfloat16).reshape(slots * BLOCK_ROWS, -1)


def fits(seq_count, pipe_count, tp_count, slots):
    return seq_count == 2 and pipe_count <= 4 and tp_count in (1, 2, 4, 8) and slots > 1


def own_side():
    return jnp.where(is_first(), 0, 1)


def other_side():
    return jnp.where(is_first(), 1, 0)


def on_device(queries, keys, values, grad_out, router, blocks, counts):
    slots = blocks.shape[2]
    rows = slots * BLOCK_ROWS
    width = queries.shape[2]
    heads = width // HEAD_SIZE
    seq_count, pipe_count, tp_count = (lax.axis_size(axis) for axis in ("seq", "pipe", "tp"))
    factor = 1.0 / math.sqrt(HEAD_SIZE * rows * seq_count)
    arrays = (queries, keys, values, grad_out)
    shape = (1, 3, rows, width)
    if fits(seq_count, pipe_count, tp_count, slots):
        head_start = max(1, heads // 3)
        small = (in_hbm(router), in_hbm(blocks))
        held = tuple(in_hbm(x) for x in arrays)

        def sent(x, axis="pipe", by=-1):
            return from_behind(x, axis, by)

        def across(x, pairs):
            return lax.ppermute(x, ("seq", "pipe"), pairs)

        def kernel(call, *operands):
            return call(factor, *operands)

        chunk_a, *loaded = kernel(opened, is_first, head_start, small, held)
        loaded += [x[0] for x in arrays]
        chunk_a = sent(chunk_a)
        chunk_b = kernel(rest, is_first, head_start, loaded)
        chunk_b = sent(chunk_b)
        tail_b, own, total, c_all = kernel(side, is_first, heads, True, loaded)
        total = sent(total, "seq", 1)
        chunk_c, tail_c, other, info = kernel(side, is_last, 0, True, loaded, c_all, total)
        chunk_c = sent(chunk_c)
        infos = [info] + [across(info, other_core(pipe_count, k)) for k in range(1, pipe_count)]
        chunk_d, tails = kernel(value_side, is_last, loaded, c_all, own, other, (tail_b, tail_c))
        chunk_d = sent(chunk_d)
        partial = kernel(router_side, is_first, loaded, own, other)
        choice = pick(infos)[0, 0]

        def branch(pairs, tails, partial, a, b, c):
            handed = place(None, a, shape, own_side, 0)
            handed = place(handed, b, shape, own_side, head_start)
            handed = place(handed, c, shape, other_side, 0)
            return handed, *third(pairs, tails, partial)

        branches = [functools.partial(branch, pairs) for pairs in third_pairs(pipe_count)]
        handed, tails, router_grad = lax.switch(
            choice, branches, tails, partial, chunk_a, chunk_b, chunk_c
        )
        handed, router_grad = finish(2, handed, chunk_d, tails, router_grad)
    else:
        index = lax.axis_index("seq")
        places = jnp.arange(seq_count)[:, None, None, None]
        key_value, query_grad = shard_states(queries, keys, values, grad_out, router, blocks, counts)
        gathered = lax.all_gather(key_value, "seq")
        earlier = jnp.sum(jnp.where(places < index, gathered, 0.0), axis=0)
        gathered = lax.all_gather(query_grad, "seq")
        later = jnp.sum(jnp.where(places > index, gathered, 0.0), axis=0)
        loaded = (router, blocks) + tuple(x[0] for x in arrays)
        c_all = gathered_gradient(grad_out, router, blocks, counts)
        d_query, before = side(factor, always, 0, False, loaded, c_all, earlier)
        d_key, after = side(factor, never, 0, False, loaded, c_all, later)
        (d_value,) = value_side(factor, always, loaded, c_all, after, after)
        partial = router_side(factor, always, loaded, before, before)
        handed = None
        for section, chunk in enumerate((d_query, d_key, d_value)):
            chunk = from_behind(chunk, "pipe", -1)
            handed = place(handed, chunk, shape, functools.partial(int, section), 0)
        router_grad = lax.psum(partial, "tp")
    return (handed, router_grad)


def solution(mesh):
    return jax.shard_map(
        on_device,
        mesh=mesh,
        in_specs=(
            P("pipe", "seq", "tp"),
            P("pipe", "seq", "tp"),
            P("pipe", "seq", "tp"),
            P("pipe", "seq", "tp"),
            P("pipe", "seq"),
            P("pipe", "seq", None),
            P("pipe", "seq"),
        ),
        out_specs=(P("pipe", None, "seq", "tp"), P("pipe", "seq")),
        check_vma=False,
    )
```
